32 devices in a mesh: region: 4 (over y, core), sub: 8 (over z, x).
Axes of the slice: x: 2, y: 2, z: 4, core: 2. Of those that a mesh axis runs over, the one named last changes fastest.
Arguments:
- coords: float32 [3, 2048, 128], P(None, ('region', 'sub')), may hold values from -3 to 3
- smooth: float32 [2048, 128], P(('region', 'sub')), may hold values from 0.6 to 1.5
- masses: float32 [2048, 128], P(('region', 'sub')), may hold values from 0.01 to 0.1
- owners: int32 [2048], P(('region', 'sub')), may hold values from 0 to 3, as said below
- counts: int32 [2048], P(('region', 'sub')), may hold values from 32 to 128
- neighbours: int32 [2048, 4], P(('region', 'sub')), may hold values from 0 to 71, as said below
Outputs:
- density: float32 [2048, 128], P(('region', 'sub'))
- accel: float32 [3, 2048, 128], P(None, ('region', 'sub'))
The draws below stay inside these ranges and needn't reach their ends.
Inputs may be any that keep to these rules, and one draw needn't show every extreme that they name: `owners`: within the 64 tiles of each device's block, every value 0 to 4 - 1 appears exactly 16 times. `neighbours`: the first entry of the list of slot t is 4 + t (the tile itself); the entries of one list are distinct and lie within 4 of 4 + t.
All inputs are finite; a program needn't handle non-finite values.
Results may differ from the reference program's by a relative error of at most 0.0001.
Values sent between devices are 32-bit elements; how exact they have to be, the bound alone decides.
No kernel may reach another device: no remote copies, remote signals or barrier semaphores. Data moves between devices by JAX's collectives and lax.ppermute only.
A program may use at most 64 MiB of HBM per device.

```python
import math
import jax
import jax.numpy as jnp
from jax import lax

TILE_ROWS = 128
TILE_DEV = 64
HALO_TILES = 4
NEIGHBOURS = 4
PER_DEST = 16
TILES = 2048
N_REGION = 4
N_SUB = 8


def draw_owners(key, part):
    blocks = TILES // TILE_DEV
    key_list = jax.random.split(jax.random.fold_in(key, 11), blocks)

    def shuffled(sub_key):
        return jax.random.permutation(sub_key, TILE_DEV)
    permuted = jax.vmap(shuffled)(key_list)
    return (permuted // PER_DEST).reshape(-1).astype(jnp.int32)


def draw_neighbours(key, part):
    key_list = jax.random.split(jax.random.fold_in(key, 23), TILES)
    offsets = jnp.concatenate([jnp.arange(HALO_TILES, dtype=jnp.int32) - HALO_TILES, jnp.arange(HALO_TILES, dtype=jnp.int32) + 1])

    def choose_some(sub_key):
        return jax.random.permutation(sub_key, offsets)[:NEIGHBOURS - 1]
    chosen = jax.vmap(choose_some)(key_list)
    slot_index = jnp.arange(TILES, dtype=jnp.int32) % TILE_DEV + HALO_TILES
    return jnp.concatenate([slot_index[:, None], slot_index[:, None] + chosen], axis=1).astype(jnp.int32)


def with_ends(entries, key, smallest, top_value):
    place = [jax.random.randint(jax.random.fold_in(key, axis), (), 0, length) for axis, length in enumerate(entries.shape)]
    widest = entries.shape.index(max(entries.shape))
    neighbour = place[:widest] + [(place[widest] + 1) % entries.shape[widest]] + place[widest + 1:]
    return entries.at[tuple(place)].set(smallest).at[tuple(neighbour)].set(top_value)


def level_of(key, dims, cuts, least, top_value):
    loudness, own = 1.0, jax.random.fold_in(key, 6)
    for position, shards_of in cuts:
        heights = jnp.exp(jax.random.uniform(jax.random.fold_in(own, position), (shards_of,), jnp.float32, least / len(cuts), top_value / len(cuts)))
        loudness = loudness * jnp.repeat(heights, dims[position] // shards_of).reshape([-1 if axis == position else 1 for axis in range(len(dims))])
    return loudness


def centred(own_key, dims, spread, most, shards=(), held_as=jnp.bfloat16):
    entries = spread * jax.random.normal(own_key, dims, jnp.float32)
    if shards:
        entries = entries * level_of(own_key, dims, shards, -0.22, 0.18)
    return jnp.clip(entries, -most, most).astype(held_as)


def setup_inputs(seed: int = 0) -> dict:
    keys = jax.random.split(jax.random.key(seed), 7)
    return {
        "coords": centred(keys[0], (3, TILES, TILE_ROWS), 0.5, 3.0, ((1, 32),), jnp.float32),
        "smooth": jnp.clip(jnp.exp(math.log(1.5) - 0.9162907 * jax.random.uniform(keys[1], (TILES, TILE_ROWS), jnp.float32) ** level_of(keys[1], (TILES, TILE_ROWS), ((0, 32),), -0.2, 0.2)), 0.6, 1.5),
        "masses": jnp.clip(jnp.exp(math.log(0.1) - 2.3025851 * jax.random.uniform(keys[2], (TILES, TILE_ROWS), jnp.float32) ** level_of(keys[2], (TILES, TILE_ROWS), ((0, 32),), -0.2, 0.2)), 0.01, 0.1),
        "owners": draw_owners(jax.random.fold_in(keys[6], 71), 0),
        "counts": with_ends(jax.random.randint(keys[4], (TILES,), TILE_ROWS // 4, TILE_ROWS + 1), jax.random.fold_in(keys[4], 1), TILE_ROWS // 4, TILE_ROWS).astype(jnp.int32),
        "neighbours": draw_neighbours(jax.random.fold_in(keys[6], 71), 0),
    }


kernel_scale = math.pi ** -1.5


def pair_weights(pos_own, inverse_sq, kernel_norm, pos_partner):
    offset_vec = pos_own[:, :, :, None] - pos_partner[:, :, None, :]
    distance_sq = jnp.sum(offset_vec * offset_vec, axis=0)
    return offset_vec, jnp.exp(-distance_sq * inverse_sq[:, :, None]) * kernel_norm[:, :, None]


def own_part(extended, tile_dev):
    own_tiles = extended[:, HALO_TILES:HALO_TILES + tile_dev]
    smooth_len = own_tiles[3]
    inverse_sq = 1.0 / (smooth_len * smooth_len)
    kernel_norm = kernel_scale * inverse_sq / smooth_len
    return own_tiles, inverse_sq, kernel_norm


def density_pass(extended, neighbours):
    own_tiles, inverse_sq, kernel_norm = own_part(extended, neighbours.shape[0])
    partners = jnp.take(extended, neighbours, axis=1)
    density = jnp.zeros(inverse_sq.shape, jnp.float32)
    for nb_slot in range(neighbours.shape[1]):
        partner = partners[:, :, nb_slot]
        unused, weight_pair = pair_weights(own_tiles[:3], inverse_sq, kernel_norm, partner[:3])
        density = density + jnp.sum(weight_pair * partner[4][:, None, :], axis=-1)
    return density


def force_pass(extended, pressure_ext, neighbours, pressure_own):
    own_tiles, inverse_sq, kernel_norm = own_part(extended, neighbours.shape[0])
    partners = jnp.take(extended, neighbours, axis=1)
    pressure_nb = jnp.take(pressure_ext, neighbours, axis=0)
    accel_sum = jnp.zeros((3,) + inverse_sq.shape, jnp.float32)
    for nb_slot in range(neighbours.shape[1]):
        partner = partners[:, :, nb_slot]
        offset_vec, weight_pair = pair_weights(own_tiles[:3], inverse_sq, kernel_norm, partner[:3])
        coefficient = weight_pair * partner[4][:, None, :] * (pressure_own[:, :, None] + pressure_nb[:, nb_slot][:, None, :])
        accel_sum = accel_sum + jnp.sum(offset_vec * coefficient[None], axis=-1)
    return 2.0 * inverse_sq[None] * accel_sum


def with_rims(values, sub_axis, tile_axis):
    tile_dev = values.shape[tile_axis]
    below = lax.slice_in_dim(jnp.roll(values, 1, axis=sub_axis), tile_dev - HALO_TILES, tile_dev, axis=tile_axis)
    above = lax.slice_in_dim(jnp.roll(values, -1, axis=sub_axis), 0, HALO_TILES, axis=tile_axis)
    return jnp.concatenate([below, values, above], axis=tile_axis)


def density_block(bundle):
    return density_pass(bundle[0], bundle[1])


def force_block(bundle):
    return force_pass(bundle[0], bundle[1], bundle[2], bundle[3])


def reference(coords, smooth, masses, owners, counts, neighbours):
    regions = N_REGION
    subgroups = N_SUB
    tile_dev = TILE_DEV
    per_dest = tile_dev // regions
    blocks = regions * subgroups
    fields = jnp.concatenate([coords, smooth[None], masses[None]], axis=0)
    fields = fields.reshape(5, regions, subgroups, tile_dev, TILE_ROWS)
    ordering = jnp.argsort(owners.reshape(regions, subgroups, tile_dev), axis=-1, stable=True)
    index_full = jnp.broadcast_to(ordering[None, :, :, :, None], fields.shape)
    sorted_tiles = jnp.take_along_axis(fields, index_full, axis=3)
    arrived = sorted_tiles.reshape(5, regions, subgroups, regions, per_dest, TILE_ROWS)
    arrived = jnp.transpose(arrived, (0, 3, 2, 1, 4, 5)).reshape(5, regions, subgroups, tile_dev, TILE_ROWS)
    slot_ids = jnp.arange(TILE_ROWS, dtype=jnp.int32)
    live_mask = (slot_ids[None, None, None, :] < counts.reshape(regions, subgroups, tile_dev)[..., None]).astype(jnp.float32)
    outgoing = jnp.concatenate([arrived[:4], (arrived[4] * live_mask)[None]], axis=0)
    extended = with_rims(outgoing, 2, 3)
    ext_blocks = jnp.moveaxis(extended.reshape(5, blocks, tile_dev + 2 * HALO_TILES, TILE_ROWS), 1, 0)
    neighbour_blocks = neighbours.reshape(blocks, tile_dev, NEIGHBOURS)
    raw_density = lax.map(density_block, (ext_blocks, neighbour_blocks))
    live_blocks = live_mask.reshape(blocks, tile_dev, TILE_ROWS)
    safe_density = jnp.where(live_blocks > 0, raw_density, 1.0)
    pressure_own = jnp.where(live_blocks > 0, safe_density ** (-1.0 / 3.0), 0.0)
    pressure_ext = with_rims(pressure_own.reshape(regions, subgroups, tile_dev, TILE_ROWS), 1, 2)
    pressure_ext = pressure_ext.reshape(blocks, tile_dev + 2 * HALO_TILES, TILE_ROWS)
    accel_blocks = lax.map(force_block, (ext_blocks, pressure_ext, neighbour_blocks, pressure_own))
    density = (raw_density * live_blocks).reshape(blocks * tile_dev, TILE_ROWS)
    accel = jnp.moveaxis(accel_blocks * live_blocks[:, None], 1, 0).reshape(3, blocks * tile_dev, TILE_ROWS)
    return density, accel
```

```python
import functools
import math

import jax
import jax.numpy as jnp
from jax import lax
from jax.experimental import pallas as pl
from jax.experimental.pallas import tpu as pltpu
from jax.sharding import PartitionSpec as P

HALO_TILES = 4
RIM = 2 * HALO_TILES
FIELDS = 5
FEATURES = 32
SUMS = 16
EMPTY_LOG = -1024.0
LOG2E = 1.4426950408889634
kernel_scale = math.pi ** (-1.5)

f32, bf16 = jnp.float32, jnp.bfloat16
VMEM = pl.BlockSpec(memory_space=pltpu.VMEM)
SMEM = pl.BlockSpec(memory_space=pltpu.SMEM)


def group_kernel(per_dest, owners_ref, coords_ref, smooth_ref, masses_ref, out_ref, seen_ref):
    regions = out_ref.shape[0]
    for d in range(regions):
        seen_ref[d] = 0

    @pl.loop(0, owners_ref.shape[0], unroll=8)
    def _(n):
        d = owners_ref[n]
        k = seen_ref[d]
        seen_ref[d] = k + 1
        for c in range(3):
            out_ref[d, pl.ds(c * per_dest + k, 1)] = coords_ref[c, pl.ds(n, 1)]
        out_ref[d, pl.ds(3 * per_dest + k, 1)] = smooth_ref[pl.ds(n, 1)]
        out_ref[d, pl.ds(4 * per_dest + k, 1)] = masses_ref[pl.ds(n, 1)]


def group_tiles(coords, smooth, masses, owners, regions):
    tile_dev, rows = smooth.shape
    per_dest = tile_dev // regions
    return pl.pallas_call(
        functools.partial(group_kernel, per_dest),
        out_shape=jax.ShapeDtypeStruct((regions, FIELDS * per_dest, rows), f32),
        in_specs=[SMEM, VMEM, VMEM, VMEM],
        out_specs=VMEM,
        scratch_shapes=[pltpu.SMEM((regions,), jnp.int32)],
        name="group_tiles",
    )(owners, coords, smooth, masses)


def parts_of(x, count):
    parts = []
    for i in range(count):
        part = x.astype(bf16).astype(f32)
        parts.append(part)
        x = x - part
    return parts


def dot(a, b):
    return jnp.dot(a, b, preferred_element_type=f32)


def sph_kernel(
    tile_dev, unroll, lists_ref, rim_lists_ref, own_ref, live_ref, below_ref, above_ref, density_ref, accel_ref,
    feat_ref, featT_ref, own_feat_ref, coef_ref, coefb_ref, high_ref, low_ref, sum_ref, out_ref, q_ref,
):
    rows = own_ref.shape[-1]
    ext = tile_dev + 2 * RIM
    regions, per_dest = own_ref.shape[0], tile_dev // own_ref.shape[0]

    def field(f):
        own = jnp.concatenate([own_ref[r, f * per_dest:(f + 1) * per_dest] for r in range(regions)], axis=0)
        if f == 4:
            own = own * live_ref[...]
        return jnp.concatenate([below_ref[f * RIM:(f + 1) * RIM], own, above_ref[f * RIM:(f + 1) * RIM]], axis=0)

    pos = [field(f) for f in range(3)]
    h = field(3)
    mass = field(4)
    live = mass > 0
    inverse_sq = 1.0 / (h * h)
    norm = kernel_scale * inverse_sq / h
    c = inverse_sq * LOG2E
    square = pos[0] * pos[0] + pos[1] * pos[1] + pos[2] * pos[2]
    log_mass = jnp.where(live, jnp.log2(jnp.where(live, mass, 1.0)), EMPTY_LOG)
    one, zero = jnp.ones_like(c), jnp.zeros_like(c)
    partner_rows, own_rows = [], []
    for value, own in [(pos[0], 2 * c * pos[0]), (pos[1], 2 * c * pos[1]), (pos[2], 2 * c * pos[2]), (square, -c)]:
        p1, p2, p3 = parts_of(value, 3)
        o1, o2, o3 = parts_of(own, 3)
        partner_rows += [p1, p1, p2, p1, p3, p2]
        own_rows += [o1, o2, o1, o3, o1, o2]
    partner_rows += parts_of(log_mass, 3) + [one] * 3 + [zero] * 2
    own_rows += [one] * 3 + parts_of(-c * square, 3) + [zero] * 2
    for k in range(FEATURES):
        feat_ref[:, k] = partner_rows[k]

    def turn(e):
        block = feat_ref[e]
        featT_ref[e] = jnp.concatenate([block, block], axis=0).T.astype(bf16)

    pl.loop(0, ext, unroll=4)(turn)
    for k in range(FEATURES):
        feat_ref[:, k] = own_rows[k]
    blank = jnp.zeros((FEATURES, rows), f32)

    def pair_up(p):
        e = HALO_TILES + 2 * p
        a, b = feat_ref[e], feat_ref[e + 1]
        top = jnp.concatenate([a, blank], axis=1)
        low = jnp.concatenate([blank, b], axis=1)
        own_feat_ref[p] = jnp.concatenate([top, low], axis=0).astype(bf16)

    pairs = (tile_dev + RIM) // 2
    pl.loop(0, pairs, unroll=4)(pair_up)

    lane = lax.broadcasted_iota(jnp.int32, (rows, 2 * FEATURES), 1)
    first_half = lane < FEATURES

    def weights(p, partners):
        own = own_feat_ref[p]
        for e0, e1 in partners:
            left = jnp.where(first_half, featT_ref[e0], featT_ref[e1])
            yield jnp.exp2(dot(left, own))

    def density_pair(p, partners, store_at):
        total = None
        for n, t in enumerate(weights(p, partners)):
            if store_at is not None:
                high = t.astype(bf16)
                high_ref[store_at, n * rows:(n + 1) * rows] = high
                low_ref[store_at, n * rows:(n + 1) * rows] = (t - high.astype(f32)).astype(bf16)
            part = jnp.sum(t.reshape(rows // 8, 8, 2 * rows), axis=0)
            total = part if total is None else total + part
        total = jnp.sum(total, axis=0, keepdims=True)
        sum_ref[pl.ds(2 * p, 1)] = total[:, :rows]
        sum_ref[pl.ds(2 * p + 1, 1)] = total[:, rows:]

    listed = lists_ref.shape[1]

    def own_partners(u):
        return [(lists_ref[2 * u, n] + HALO_TILES, lists_ref[2 * u + 1, n] + HALO_TILES) for n in range(listed)]

    rim_pairs = HALO_TILES // 2
    for u in range(2 * rim_pairs):
        shift = HALO_TILES - tile_dev if u < rim_pairs else HALO_TILES + tile_dev
        partners = [
            (rim_lists_ref[2 * u * listed + n] + shift, rim_lists_ref[(2 * u + 1) * listed + n] + shift)
            for n in range(listed)
        ]
        density_pair(u if u < rim_pairs else u + tile_dev // 2, partners, None)

    @pl.loop(0, tile_dev // 2, unroll=unroll)
    def _(u):
        density_pair(u + rim_pairs, own_partners(u), u)

    inner = slice(HALO_TILES, ext - HALO_TILES)
    raw = sum_ref[...] * norm[inner]
    inner_live = live[inner]
    q = jnp.where(inner_live, jnp.exp2(jnp.log2(jnp.where(inner_live, raw, 1.0)) * (-1.0 / 3.0)), 0.0)
    pad = jnp.zeros((HALO_TILES, rows), f32)
    q = jnp.concatenate([pad, q, pad], axis=0)
    coef = [one]
    for value in pos + [q] + [q * x for x in pos]:
        coef += parts_of(value, 2)
    coef.append(zero)
    for k in range(SUMS):
        coef_ref[:, k] = coef[k]

    def narrow(e):
        coefb_ref[e] = coef_ref[e].astype(bf16)

    pl.loop(0, ext, unroll=8)(narrow)

    @pl.loop(0, tile_dev // 2, unroll=unroll)
    def _(u):
        total = None
        for n, (e0, e1) in enumerate(own_partners(u)):
            left = jnp.concatenate([coefb_ref[e0], coefb_ref[e1]], axis=0)
            part = dot(left, high_ref[u, n * rows:(n + 1) * rows]) + dot(left, low_ref[u, n * rows:(n + 1) * rows])
            total = part if total is None else total + part
        out_ref[2 * u] = total[:SUMS, :rows]
        out_ref[2 * u + 1] = total[SUMS:, rows:]

    mine = slice(RIM, RIM + tile_dev)
    own_live = live_ref[...]
    density_ref[...] = raw[HALO_TILES:HALO_TILES + tile_dev] * own_live
    q_own = q[mine]
    scale = own_live * (2.0 * inverse_sq[mine] * norm[mine])
    s0 = out_ref[:, 0]
    q0 = out_ref[:, 7] + out_ref[:, 8]
    for c in range(3):
        s1 = out_ref[:, 1 + 2 * c] + out_ref[:, 2 + 2 * c]
        q1 = out_ref[:, 9 + 2 * c] + out_ref[:, 10 + 2 * c]
        x = pos[c][mine]
        accel_ref[c] = scale * (q_own * (x * s0 - s1) + (x * q0 - q1))


def sph(lists, rim_lists, own, live, below, above):
    tile_dev, rows = live.shape
    ext = tile_dev + 2 * RIM
    listed = lists.shape[1]
    pairs = (tile_dev + RIM) // 2
    return pl.pallas_call(
        functools.partial(sph_kernel, tile_dev, 4),
        out_shape=(jax.ShapeDtypeStruct((tile_dev, rows), f32), jax.ShapeDtypeStruct((3, tile_dev, rows), f32)),
        in_specs=[SMEM, SMEM, VMEM, VMEM, VMEM, VMEM],
        out_specs=(VMEM, VMEM),
        scratch_shapes=[
            pltpu.VMEM((ext, FEATURES, rows), f32),
            pltpu.VMEM((ext, rows, 2 * FEATURES), bf16),
            pltpu.VMEM((pairs, 2 * FEATURES, 2 * rows), bf16),
            pltpu.VMEM((ext, SUMS, rows), f32),
            pltpu.VMEM((ext, SUMS, rows), bf16),
            pltpu.VMEM((tile_dev // 2, listed * rows, 2 * rows), bf16),
            pltpu.VMEM((tile_dev // 2, listed * rows, 2 * rows), bf16),
            pltpu.VMEM((tile_dev + RIM, rows), f32),
            pltpu.VMEM((tile_dev, SUMS, rows), f32),
            pltpu.VMEM((8, rows), f32),
        ],
        name="sph",
    )(lists, rim_lists, own, live, below, above)


def per_device(coords, smooth, masses, owners, counts, neighbours):
    tile_dev, rows = smooth.shape
    regions = lax.axis_size("region")
    subs = lax.axis_size("sub")
    per_dest = tile_dev // regions
    listed = neighbours.shape[1]
    grouped = group_tiles(coords, smooth, masses, owners, regions)
    own = lax.all_to_all(grouped, "region", 0, 0, tiled=True)
    live = (jnp.arange(rows, dtype=jnp.int32)[None, :] < counts[:, None]).astype(f32)
    by_field = own.reshape(regions, FIELDS, per_dest, rows)

    def rim(first):
        if per_dest >= RIM:
            block = by_field[regions - 1 if not first else 0]
            block = block[:, :RIM] if first else block[:, per_dest - RIM:]
        else:
            blocks = RIM // per_dest
            block = by_field[:blocks] if first else by_field[regions - blocks:]
            block = jnp.swapaxes(block, 0, 1).reshape(FIELDS, RIM, rows)
        tiles = slice(0, RIM) if first else slice(tile_dev - RIM, tile_dev)
        block = jnp.concatenate([block[:4], (block[4] * live[tiles])[None]], axis=0).reshape(FIELDS * RIM, rows)
        near = slice(0, HALO_TILES) if first else slice(tile_dev - HALO_TILES, tile_dev)
        ids = neighbours[near].astype(f32).reshape(1, HALO_TILES * listed)
        return jnp.concatenate([block, jnp.pad(ids, ((0, 7), (0, rows - HALO_TILES * listed)))], axis=0)

    up = [(i, (i + 1) % subs) for i in range(subs)]
    down = [(j, i) for i, j in up]
    below = lax.ppermute(rim(False), "sub", up)
    above = lax.ppermute(rim(True), "sub", down)
    count = HALO_TILES * listed
    rim_lists = jnp.concatenate([below[FIELDS * RIM, :count], above[FIELDS * RIM, :count]]).astype(jnp.int32)
    return sph(neighbours, rim_lists, own, live, below, above)


def solution(mesh):
    in_specs = (
        P(None, ("region", "sub"), None),
        P(("region", "sub"), None),
        P(("region", "sub"), None),
        P(("region", "sub")),
        P(("region", "sub")),
        P(("region", "sub"), None),
    )
    out_specs = (P(("region", "sub"), None), P(None, ("region", "sub"), None))
    return jax.shard_map(
        per_device, mesh=mesh, in_specs=in_specs, out_specs=out_specs, check_vma=False
    )
```

```python
import functools
import math

import jax
import jax.numpy as jnp
from jax import lax
from jax.experimental import pallas as pl
from jax.experimental.pallas import tpu as pltpu
from jax.sharding import PartitionSpec as P


HALO_TILES = 4
RIM = 2 * HALO_TILES
FIELDS = 5
DEPTH = 48
EMPTY_LOG = -1024.0
LOG2E = 1.4426950408889634
kernel_scale = math.pi ** (-1.5)

f32, bf16 = jnp.float32, jnp.bfloat16
VMEM = pl.BlockSpec(memory_space=pltpu.VMEM)
SMEM = pl.BlockSpec(memory_space=pltpu.SMEM)


def group_kernel(per_dest, owners_ref, coords_ref, smooth_ref, masses_ref, out_ref, seen_ref):
    regions = out_ref.shape[0]
    for d in range(regions):
        seen_ref[d] = 0

    @pl.loop(0, owners_ref.shape[0], unroll=8)
    def _(n):
        d = owners_ref[n]
        k = seen_ref[d]
        seen_ref[d] = k + 1
        for c in range(3):
            out_ref[d, pl.ds(c * per_dest + k, 1)] = coords_ref[c, pl.ds(n, 1)]
        out_ref[d, pl.ds(3 * per_dest + k, 1)] = smooth_ref[pl.ds(n, 1)]
        out_ref[d, pl.ds(4 * per_dest + k, 1)] = masses_ref[pl.ds(n, 1)]


def group_tiles(coords, smooth, masses, owners, regions):
    tile_dev, rows = smooth.shape
    per_dest = tile_dev // regions
    return pl.pallas_call(
        functools.partial(group_kernel, per_dest),
        out_shape=jax.ShapeDtypeStruct((regions, FIELDS * per_dest, rows), f32),
        in_specs=[SMEM, VMEM, VMEM, VMEM],
        out_specs=VMEM,
        scratch_shapes=[pltpu.SMEM((regions,), jnp.int32)],
        compiler_params=pltpu.CompilerParams(vmem_limit_bytes=8 << 20),
        name="group_tiles",
    )(owners, coords, smooth, masses)


def parts_of(x, count):
    parts = []
    for _ in range(count):
        part = x.astype(bf16).astype(f32)
        parts.append(part)
        x = x - part
    return parts


def dot(a, b):
    return jnp.dot(a, b, preferred_element_type=f32)


def sph_kernel(
    tile_dev, unroll, lists_ref, rim_lists_ref, own_ref, live_ref, below_ref, above_ref, density_ref, accel_ref,
    partner_ref, mine_ref, turned_ref, weights_ref, coef_ref, coefb_ref, pair_ref, part_ref, out_ref,
):
    rows = own_ref.shape[-1]
    ext = tile_dev + 2 * RIM
    regions, per_dest = own_ref.shape[0], tile_dev // own_ref.shape[0]

    def field(f):
        own = jnp.concatenate([own_ref[r, f * per_dest:(f + 1) * per_dest] for r in range(regions)], axis=0)
        if f == 4:
            own = own * live_ref[...]
        return jnp.concatenate([below_ref[f * RIM:(f + 1) * RIM], own, above_ref[f * RIM:(f + 1) * RIM]], axis=0)

    pos = [field(f) for f in range(3)]
    h = field(3)
    mass = field(4)
    live = mass > 0
    inverse_sq = 1.0 / (h * h)
    norm = kernel_scale * inverse_sq / h
    c = inverse_sq * LOG2E
    square = pos[0] * pos[0] + pos[1] * pos[1] + pos[2] * pos[2]
    log_mass = jnp.where(live, jnp.log2(jnp.where(live, mass, 1.0)), EMPTY_LOG)
    one, zero = jnp.ones_like(c), jnp.zeros_like(c)
    for k, value in enumerate(pos + [square, log_mass, one, zero, zero]):
        partner_ref[k * ext:(k + 1) * ext] = value
    for k, value in enumerate([2 * c * x for x in pos] + [-c, one, -c * square, zero, zero]):
        mine_ref[k * ext:(k + 1) * ext] = value
    turn_fill = jnp.zeros((rows - DEPTH, rows), bf16)

    def turn(e):
        p1, p2, p3 = parts_of(partner_ref[pl.ds(e, 8, stride=ext)], 3)
        block = jnp.concatenate([p1, p1, p2, p1, p3, p2], axis=0).astype(bf16)
        turned_ref[e] = jnp.concatenate([block, turn_fill], axis=0).T

    pl.loop(0, ext, unroll=8)(turn)
    blank = jnp.zeros((rows, rows), bf16)

    def own_weights(e):
        o1, o2, o3 = parts_of(mine_ref[pl.ds(e, 8, stride=ext)], 3)
        block = jnp.concatenate([o1, o2, o1, o3, o1, o2], axis=0).astype(bf16)
        return jnp.concatenate([block, turn_fill], axis=0)

    def pair_up(p):
        e = HALO_TILES + 2 * p
        top = jnp.concatenate([own_weights(e), blank], axis=1)
        low = jnp.concatenate([blank, own_weights(e + 1)], axis=1)
        weights_ref[p] = jnp.concatenate([top, low], axis=0)

    pairs = (tile_dev + RIM) // 2
    pl.loop(0, pairs, unroll=4)(pair_up)

    def density_pair(p, partners, store_at):
        own = weights_ref[p]
        total = None
        for n, (e0, e1) in enumerate(partners):
            left = jnp.concatenate([turned_ref[e0], turned_ref[e1]], axis=1)
            t = jnp.exp2(dot(left, own))
            if store_at is not None:
                pair_ref[store_at, n * rows:(n + 1) * rows] = t
            part = jnp.sum(t.reshape(rows // 8, 8, 2 * rows), axis=0)
            total = part if total is None else total + part
        part_ref[pl.ds(16 * p, 8)] = total[:, :rows]
        part_ref[pl.ds(16 * p + 8, 8)] = total[:, rows:]

    listed = lists_ref.shape[1]

    def own_partners(u):
        return [(lists_ref[2 * u, n] + HALO_TILES, lists_ref[2 * u + 1, n] + HALO_TILES) for n in range(listed)]

    rim_pairs = HALO_TILES // 2
    for u in range(2 * rim_pairs):
        shift = HALO_TILES - tile_dev if u < rim_pairs else HALO_TILES + tile_dev
        partners = [
            (rim_lists_ref[2 * u * listed + n] + shift, rim_lists_ref[(2 * u + 1) * listed + n] + shift)
            for n in range(listed)
        ]
        density_pair(u if u < rim_pairs else u + tile_dev // 2, partners, None)

    @pl.loop(0, tile_dev // 2, unroll=unroll)
    def _(u):
        density_pair(u + rim_pairs, own_partners(u), u)

    inner = slice(HALO_TILES, ext - HALO_TILES)
    raw = sum(part_ref[pl.ds(k, tile_dev + RIM, stride=8)] for k in range(8))
    raw = raw * norm[inner]
    inner_live = live[inner]
    q = jnp.where(inner_live, jnp.exp2(jnp.log2(jnp.where(inner_live, raw, 1.0)) * (-1.0 / 3.0)), 0.0)
    pad = jnp.zeros((HALO_TILES, rows), f32)
    q = jnp.concatenate([pad, q, pad], axis=0)
    for k, value in enumerate([one] + pos + [q] + [q * x for x in pos]):
        coef_ref[k * ext:(k + 1) * ext] = value

    def narrow(e):
        coefb_ref[e] = jnp.concatenate(parts_of(coef_ref[pl.ds(e, 8, stride=ext)], 2), axis=0).astype(bf16)

    pl.loop(0, ext, unroll=8)(narrow)

    @pl.loop(0, tile_dev // 2, unroll=unroll)
    def _(u):
        total = None
        for n, (e0, e1) in enumerate(own_partners(u)):
            left = jnp.concatenate([coefb_ref[e0], coefb_ref[e1]], axis=0)
            t = pair_ref[u, n * rows:(n + 1) * rows]
            high = t.astype(bf16)
            part = dot(left, high) + dot(left, (t - high.astype(f32)).astype(bf16))
            total = part if total is None else total + part
        out_ref[pl.ds(16 * u, 8)] = total[:8, :rows] + total[8:16, :rows]
        out_ref[pl.ds(16 * u + 8, 8)] = total[16:24, rows:] + total[24:, rows:]

    mine = slice(RIM, RIM + tile_dev)
    own_live = live_ref[...]
    density_ref[...] = raw[HALO_TILES:HALO_TILES + tile_dev] * own_live
    q_own = q[mine]
    scale = own_live * (2.0 * inverse_sq[mine] * norm[mine])
    sums = [out_ref[pl.ds(k, tile_dev, stride=8)] for k in range(8)]
    for c in range(3):
        x = pos[c][mine]
        accel_ref[c] = scale * (q_own * (x * sums[0] - sums[1 + c]) + (x * sums[4] - sums[5 + c]))


def sph(lists, rim_lists, own, live, below, above):
    tile_dev, rows = live.shape
    ext = tile_dev + 2 * RIM
    listed = lists.shape[1]
    pairs = (tile_dev + RIM) // 2
    return pl.pallas_call(
        functools.partial(sph_kernel, tile_dev, 8),
        out_shape=(jax.ShapeDtypeStruct((tile_dev, rows), f32), jax.ShapeDtypeStruct((3, tile_dev, rows), f32)),
        in_specs=[SMEM, SMEM, VMEM, VMEM, VMEM, VMEM],
        out_specs=(VMEM, VMEM),
        scratch_shapes=[
            pltpu.VMEM((8 * ext, rows), f32),
            pltpu.VMEM((8 * ext, rows), f32),
            pltpu.VMEM((ext, rows, rows), bf16),
            pltpu.VMEM((pairs, 2 * rows, 2 * rows), bf16),
            pltpu.VMEM((8 * ext, rows), f32),
            pltpu.VMEM((ext, 16, rows), bf16),
            pltpu.VMEM((tile_dev // 2, listed * rows, 2 * rows), f32),
            pltpu.VMEM((8 * (tile_dev + RIM), rows), f32),
            pltpu.VMEM((8 * tile_dev, rows), f32),
        ],
        compiler_params=pltpu.CompilerParams(vmem_limit_bytes=40 << 20),
        name="sph",
    )(lists, rim_lists, own, live, below, above)


def per_device(coords, smooth, masses, owners, counts, neighbours):
    tile_dev, rows = smooth.shape
    regions = lax.axis_size("region")
    subs = lax.axis_size("sub")
    per_dest = tile_dev // regions
    listed = neighbours.shape[1]
    grouped = group_tiles(coords, smooth, masses, owners, regions)
    own = lax.all_to_all(grouped, "region", 0, 0, tiled=True)
    live = (jnp.arange(rows, dtype=jnp.int32)[None, :] < counts[:, None]).astype(f32)
    by_field = own.reshape(regions, FIELDS, per_dest, rows)

    def rim(first):
        if per_dest >= RIM:
            block = by_field[regions - 1 if not first else 0]
            block = block[:, :RIM] if first else block[:, per_dest - RIM:]
        else:
            blocks = RIM // per_dest
            block = by_field[:blocks] if first else by_field[regions - blocks:]
            block = jnp.swapaxes(block, 0, 1).reshape(FIELDS, RIM, rows)
        tiles = slice(0, RIM) if first else slice(tile_dev - RIM, tile_dev)
        block = jnp.concatenate([block[:4], (block[4] * live[tiles])[None]], axis=0).reshape(FIELDS * RIM, rows)
        near = slice(0, HALO_TILES) if first else slice(tile_dev - HALO_TILES, tile_dev)
        ids = neighbours[near].astype(f32).reshape(1, HALO_TILES * listed)
        return jnp.concatenate([block, jnp.pad(ids, ((0, 7), (0, rows - HALO_TILES * listed)))], axis=0)

    up = [(i, (i + 1) % subs) for i in range(subs)]
    down = [(j, i) for i, j in up]
    below = lax.ppermute(rim(False), "sub", up)
    above = lax.ppermute(rim(True), "sub", down)
    count = HALO_TILES * listed
    rim_lists = jnp.concatenate([below[FIELDS * RIM, :count], above[FIELDS * RIM, :count]]).astype(jnp.int32)
    return sph(neighbours, rim_lists, own, live, below, above)


def solution(mesh):
    in_specs = (
        P(None, ("region", "sub"), None),
        P(("region", "sub"), None),
        P(("region", "sub"), None),
        P(("region", "sub")),
        P(("region", "sub")),
        P(("region", "sub"), None),
    )
    out_specs = (P(("region", "sub"), None), P(None, ("region", "sub"), None))
    return jax.shard_map(
        per_device, mesh=mesh, in_specs=in_specs, out_specs=out_specs, check_vma=False
    )
```

```python
import functools
import math

import jax
import jax.numpy as jnp
from jax import lax
from jax.experimental import pallas as pl
from jax.experimental.pallas import tpu as pltpu
from jax.sharding import PartitionSpec as P


HALO_TILES = 4
RIM = 2 * HALO_TILES
FIELDS = 5
UNROLL = 7
EMPTY_LOG = -1024.0
LOG2E = 1.4426950408889634
kernel_scale = math.pi ** (-1.5)

f32, bf16 = jnp.float32, jnp.bfloat16
VMEM = pl.BlockSpec(memory_space=pltpu.VMEM)
SMEM = pl.BlockSpec(memory_space=pltpu.SMEM)


def group_kernel(per_dest, owners_ref, coords_ref, smooth_ref, masses_ref, out_ref):
    regions = out_ref.shape[0]
    bits = per_dest.bit_length()
    per_word = 31 // bits
    seen = [jnp.int32(0)] * pl.cdiv(regions, per_word)
    for n in range(owners_ref.shape[0]):
        d = owners_ref[n]
        word = d // per_word if len(seen) > 1 else 0
        shift = (d - word * per_word) * bits
        k = seen[0]
        for w in range(1, len(seen)):
            k = jnp.where(word == w, seen[w], k)
        k = (k >> shift) & ((1 << bits) - 1)
        step = jnp.int32(1) << shift
        seen = [s + (jnp.where(word == w, step, 0) if len(seen) > 1 else step) for w, s in enumerate(seen)]
        for c in range(3):
            out_ref[d, pl.ds(c * per_dest + k, 1)] = coords_ref[c, n:n + 1]
        out_ref[d, pl.ds(3 * per_dest + k, 1)] = smooth_ref[n:n + 1]
        out_ref[d, pl.ds(4 * per_dest + k, 1)] = masses_ref[n:n + 1]


def group_tiles(coords, smooth, masses, owners, regions):
    tile_dev, rows = smooth.shape
    per_dest = tile_dev // regions
    return pl.pallas_call(
        functools.partial(group_kernel, per_dest),
        out_shape=jax.ShapeDtypeStruct((regions, FIELDS * per_dest, rows), f32),
        in_specs=[SMEM, VMEM, VMEM, VMEM],
        out_specs=VMEM,
        name="group_tiles",
    )(owners, coords, smooth, masses)


def parts_of(x, count):
    parts = []
    for _ in range(count):
        part = x.astype(bf16).astype(f32)
        parts.append(part)
        x = x - part
    return parts


def dot(a, b):
    return jnp.dot(a, b, preferred_element_type=f32)


def own_field(own_ref, live_ref, f):
    tile_dev = live_ref.shape[0]
    regions, per_dest = own_ref.shape[0], tile_dev // own_ref.shape[0]
    value = jnp.concatenate([own_ref[r, f * per_dest:(f + 1) * per_dest] for r in range(regions)], axis=0)
    return value * live_ref[...] if f == 4 else value


def field_terms(fields):
    pos, h, mass = fields[:3], fields[3], fields[4]
    inverse_sq = 1.0 / (h * h)
    return pos, mass > 0, mass, inverse_sq, kernel_scale * inverse_sq / h


def put_rows(ref, values):
    count = values[0].shape[0]
    for k, value in enumerate(values):
        ref[k * count:(k + 1) * count] = value


def put_features(pos, live, mass, inverse_sq, partner_ref, mine_ref):
    c = inverse_sq * LOG2E
    square = pos[0] * pos[0] + pos[1] * pos[1] + pos[2] * pos[2]
    log_mass = jnp.where(live, jnp.log2(jnp.where(live, mass, 1.0)), EMPTY_LOG)
    one, zero = jnp.ones_like(c), jnp.zeros_like(c)
    put_rows(partner_ref, pos + [square, log_mass, one, zero, zero])
    put_rows(mine_ref, [2 * c * x for x in pos] + [-c, one, -c * square, zero, zero])


def tile_of(ref, e):
    return ref[pl.ds(e, 8, stride=ref.shape[0] // 8)]


def turned(ref, e):
    p1, p2, p3 = parts_of(tile_of(ref, e), 3)
    block = jnp.concatenate([p1, p1, p2, p1, p3, p2], axis=0).astype(bf16)
    fill = jnp.zeros((block.shape[1] - block.shape[0], block.shape[1]), bf16)
    return jnp.concatenate([block, fill], axis=0).T


def pair_weights(ref, e):
    def one_tile(e):
        o1, o2, o3 = parts_of(tile_of(ref, e), 3)
        block = jnp.concatenate([o1, o2, o1, o3, o1, o2], axis=0).astype(bf16)
        return jnp.concatenate([block, jnp.zeros((block.shape[1] - block.shape[0], block.shape[1]), bf16)], axis=0)

    first, second = one_tile(e), one_tile(e + 1)
    blank = jnp.zeros_like(first)
    return jnp.concatenate(
        [jnp.concatenate([first, blank], axis=1), jnp.concatenate([blank, second], axis=1)], axis=0
    )


def density_pair(turned_ref, own, partners, part_ref, at, store):
    rows = own.shape[1] // 2
    total = None
    for n, (e0, e1) in enumerate(partners):
        t = jnp.exp2(dot(jnp.concatenate([turned_ref[e0], turned_ref[e1]], axis=1), own))
        if store is not None:
            store[n * rows:(n + 1) * rows] = t
        part = jnp.sum(t.reshape(rows // 8, 8, 2 * rows), axis=0)
        total = part if total is None else total + part
    part_ref[pl.ds(at, 8)] = total[:, :rows]
    part_ref[pl.ds(at + 8, 8)] = total[:, rows:]


def inner_kernel(
    lists_ref, own_ref, live_ref, pair_ref, part_ref, edge_ref, partner_ref, mine_ref, turned_ref, weights_ref,
):
    tile_dev = live_ref.shape[0]
    listed = lists_ref.shape[1]
    pos, live, mass, inverse_sq, _ = field_terms([own_field(own_ref, live_ref, f) for f in range(FIELDS)])
    put_features(pos, live, mass, inverse_sq, partner_ref, mine_ref)

    @pl.loop(0, tile_dev, unroll=8)
    def _(t):
        turned_ref[t] = turned(partner_ref, t)

    edge_ref[:RIM] = turned_ref[:RIM]
    edge_ref[RIM:] = turned_ref[tile_dev - RIM:]
    count = pair_ref.shape[0]

    @pl.loop(0, count, unroll=UNROLL)
    def _(p):
        weights_ref[p] = pair_weights(mine_ref, HALO_TILES + 2 * p)

    @pl.loop(0, count, unroll=UNROLL)
    def _(p):
        t = HALO_TILES + 2 * p
        partners = [(lists_ref[t, n] - HALO_TILES, lists_ref[t + 1, n] - HALO_TILES) for n in range(listed)]
        density_pair(turned_ref, weights_ref[p], partners, part_ref, 16 * p, pair_ref.at[p])


def outer_kernel(
    lists_ref, rim_lists_ref, own_ref, live_ref, below_ref, above_ref, pair_ref, part_ref, edge_ref,
    density_ref, accel_ref, partner_ref, mine_ref, turned_ref, rim_pair_ref, rim_part_ref, coef_ref, coefb_ref, out_ref,
):
    tile_dev, rows = live_ref.shape
    ext = tile_dev + 2 * RIM
    listed = lists_ref.shape[1]
    fields = [
        jnp.concatenate(
            [below_ref[f * RIM:(f + 1) * RIM], own_field(own_ref, live_ref, f), above_ref[f * RIM:(f + 1) * RIM]], axis=0
        )
        for f in range(FIELDS)
    ]
    pos, live, mass, inverse_sq, norm = field_terms(fields)

    def rims(x):
        return jnp.concatenate([x[:2 * RIM], x[tile_dev:]], axis=0)

    put_features([rims(x) for x in pos], rims(live), rims(mass), rims(inverse_sq), partner_ref, mine_ref)
    for e in range(RIM):
        turned_ref[e] = turned(partner_ref, e)
        turned_ref[RIM + e] = edge_ref[e]
        turned_ref[2 * RIM + e] = edge_ref[RIM + e]
        turned_ref[3 * RIM + e] = turned(partner_ref, 3 * RIM + e)

    edge_pairs = HALO_TILES
    half = HALO_TILES // 2
    for side in range(2):
        for i in range(edge_pairs):
            e = 2 * RIM * side + HALO_TILES + 2 * i
            own_side = (i >= half) if side == 0 else (i < half)
            if own_side:
                t = e - RIM if side == 0 else e - 3 * RIM + tile_dev
                shift = HALO_TILES if side == 0 else HALO_TILES - tile_dev + 2 * RIM
                partners = [(lists_ref[t, n] + shift, lists_ref[t + 1, n] + shift) for n in range(listed)]
                store = rim_pair_ref.at[half * side + i % half]
            else:
                first = (2 * i if side == 0 else HALO_TILES + 2 * (i - half)) * listed
                shift = HALO_TILES - tile_dev if side == 0 else HALO_TILES + 2 * RIM
                partners = [
                    (rim_lists_ref[first + n] + shift, rim_lists_ref[first + listed + n] + shift) for n in range(listed)
                ]
                store = None
            at = 16 * (edge_pairs * side + i)
            density_pair(turned_ref, pair_weights(mine_ref, e), partners, rim_part_ref, at, store)

    inner_tiles = tile_dev - RIM
    raw = jnp.concatenate(
        [
            sum(rim_part_ref[pl.ds(k, RIM, stride=8)] for k in range(8)),
            sum(part_ref[pl.ds(k, inner_tiles, stride=8)] for k in range(8)),
            sum(rim_part_ref[pl.ds(8 * RIM + k, RIM, stride=8)] for k in range(8)),
        ],
        axis=0,
    )
    inner = slice(HALO_TILES, ext - HALO_TILES)
    raw = raw * norm[inner]
    q = jnp.where(live[inner], jnp.exp2(jnp.log2(jnp.where(live[inner], raw, 1.0)) * (-1.0 / 3.0)), 0.0)
    pad = jnp.zeros((HALO_TILES, rows), f32)
    q = jnp.concatenate([pad, q, pad], axis=0)
    put_rows(coef_ref, [jnp.ones_like(q)] + pos + [q] + [q * x for x in pos])

    @pl.loop(0, ext, unroll=8)
    def _(e):
        coefb_ref[e] = jnp.concatenate(parts_of(tile_of(coef_ref, e), 2), axis=0).astype(bf16)

    def force_pair(t, pair):
        total = None
        for n in range(listed):
            e0, e1 = lists_ref[t, n] + HALO_TILES, lists_ref[t + 1, n] + HALO_TILES
            left = jnp.concatenate([coefb_ref[e0], coefb_ref[e1]], axis=0)
            w = pair[n * rows:(n + 1) * rows]
            high = w.astype(bf16)
            part = dot(left, high) + dot(left, (w - high.astype(f32)).astype(bf16))
            total = part if total is None else total + part
        at = 8 * t
        out_ref[pl.ds(at, 8)] = total[:8, :rows] + total[8:16, :rows]
        out_ref[pl.ds(at + 8, 8)] = total[16:24, rows:] + total[24:, rows:]

    for i in range(half):
        force_pair(2 * i, rim_pair_ref.at[i])
        force_pair(tile_dev - HALO_TILES + 2 * i, rim_pair_ref.at[half + i])

    @pl.loop(0, pair_ref.shape[0], unroll=UNROLL)
    def _(p):
        force_pair(HALO_TILES + 2 * p, pair_ref.at[p])

    mine = slice(RIM, RIM + tile_dev)
    own_live = live_ref[...]
    density_ref[...] = raw[HALO_TILES:HALO_TILES + tile_dev] * own_live
    q_own = q[mine]
    scale = own_live * (2.0 * inverse_sq[mine] * norm[mine])
    sums = [out_ref[pl.ds(k, tile_dev, stride=8)] for k in range(8)]
    for c in range(3):
        x = pos[c][mine]
        accel_ref[c] = scale * (q_own * (x * sums[0] - sums[1 + c]) + (x * sums[4] - sums[5 + c]))


def inner_density(lists, own, live):
    tile_dev, rows = live.shape
    listed = lists.shape[1]
    count = (tile_dev - RIM) // 2
    return pl.pallas_call(
        inner_kernel,
        out_shape=(
            jax.ShapeDtypeStruct((count, listed * rows, 2 * rows), f32),
            jax.ShapeDtypeStruct((16 * count, rows), f32),
            jax.ShapeDtypeStruct((2 * RIM, rows, rows), bf16),
        ),
        in_specs=[SMEM, VMEM, VMEM],
        out_specs=(VMEM, VMEM, VMEM),
        scratch_shapes=[
            pltpu.VMEM((8 * tile_dev, rows), f32),
            pltpu.VMEM((8 * tile_dev, rows), f32),
            pltpu.VMEM((tile_dev, rows, rows), bf16),
            pltpu.VMEM((count, 2 * rows, 2 * rows), bf16),
        ],
        compiler_params=pltpu.CompilerParams(vmem_limit_bytes=24 << 20),
        cost_estimate=pl.CostEstimate(flops=10 ** 9, bytes_accessed=10 ** 7, transcendentals=0),
        name="inner_density",
    )(lists, own, live)


def outer_step(lists, rim_lists, own, live, below, above, pair, part, edge):
    tile_dev, rows = live.shape
    ext = tile_dev + 2 * RIM
    listed = lists.shape[1]
    return pl.pallas_call(
        outer_kernel,
        out_shape=(jax.ShapeDtypeStruct((tile_dev, rows), f32), jax.ShapeDtypeStruct((3, tile_dev, rows), f32)),
        in_specs=[SMEM, SMEM] + [VMEM] * 7,
        out_specs=(VMEM, VMEM),
        scratch_shapes=[
            pltpu.VMEM((8 * 4 * RIM, rows), f32),
            pltpu.VMEM((8 * 4 * RIM, rows), f32),
            pltpu.VMEM((4 * RIM, rows, rows), bf16),
            pltpu.VMEM((HALO_TILES, listed * rows, 2 * rows), f32),
            pltpu.VMEM((8 * 2 * RIM, rows), f32),
            pltpu.VMEM((8 * ext, rows), f32),
            pltpu.VMEM((ext, 16, rows), bf16),
            pltpu.VMEM((8 * tile_dev, rows), f32),
        ],
        compiler_params=pltpu.CompilerParams(vmem_limit_bytes=24 << 20),
        name="outer_step",
    )(lists, rim_lists, own, live, below, above, pair, part, edge)


def per_device(coords, smooth, masses, owners, counts, neighbours):
    tile_dev, rows = smooth.shape
    regions = lax.axis_size("region")
    subs = lax.axis_size("sub")
    per_dest = tile_dev // regions
    listed = neighbours.shape[1]
    grouped = group_tiles(coords, smooth, masses, owners, regions)
    own = lax.all_to_all(grouped, "region", 0, 0, tiled=True)
    live = (jnp.arange(rows, dtype=jnp.int32)[None, :] < counts[:, None]).astype(f32)
    by_field = own.reshape(regions, FIELDS, per_dest, rows)

    def rim(first):
        if per_dest >= RIM:
            block = by_field[regions - 1 if not first else 0]
            block = block[:, :RIM] if first else block[:, per_dest - RIM:]
        else:
            blocks = RIM // per_dest
            block = by_field[:blocks] if first else by_field[regions - blocks:]
            block = jnp.swapaxes(block, 0, 1).reshape(FIELDS, RIM, rows)
        tiles = slice(0, RIM) if first else slice(tile_dev - RIM, tile_dev)
        block = jnp.concatenate([block[:4], (block[4] * live[tiles])[None]], axis=0).reshape(FIELDS * RIM, rows)
        near = slice(0, HALO_TILES) if first else slice(tile_dev - HALO_TILES, tile_dev)
        ids = neighbours[near].astype(f32).reshape(1, HALO_TILES * listed)
        return jnp.concatenate([block, jnp.pad(ids, ((0, 7), (0, rows - HALO_TILES * listed)))], axis=0)

    up = [(i, (i + 1) % subs) for i in range(subs)]
    down = [(j, i) for i, j in up]
    below = lax.ppermute(rim(False), "sub", up)
    above = lax.ppermute(rim(True), "sub", down)
    pair, part, edge = inner_density(neighbours, own, live)
    count = HALO_TILES * listed
    rim_lists = jnp.concatenate([below[FIELDS * RIM, :count], above[FIELDS * RIM, :count]]).astype(jnp.int32)
    return outer_step(neighbours, rim_lists, own, live, below, above, pair, part, edge)


def solution(mesh):
    in_specs = (
        P(None, ("region", "sub"), None),
        P(("region", "sub"), None),
        P(("region", "sub"), None),
        P(("region", "sub")),
        P(("region", "sub")),
        P(("region", "sub"), None),
    )
    out_specs = (P(("region", "sub"), None), P(None, ("region", "sub"), None))
    return jax.shard_map(
        per_device, mesh=mesh, in_specs=in_specs, out_specs=out_specs, check_vma=False
    )
```

```python
import functools
import math

import jax
import jax.numpy as jnp
from jax import lax
from jax.experimental import pallas as pl
from jax.experimental.pallas import tpu as pltpu
from jax.sharding import PartitionSpec as P


HALO_TILES = 4
RIM = 2 * HALO_TILES
FIELDS = 5
UNROLL = 7
EMPTY_LOG = -1024.0
LOG2E = 1.4426950408889634
kernel_scale = math.pi ** (-1.5)

f32, bf16 = jnp.float32, jnp.bfloat16
VMEM = pl.BlockSpec(memory_space=pltpu.VMEM)
SMEM = pl.BlockSpec(memory_space=pltpu.SMEM)


def group_kernel(pairwise, owners_ref, coords_hbm, smooth_hbm, masses_hbm, *refs):
    outs, (coords_ref, smooth_ref, masses_ref, sems) = refs[:-4], refs[-4:]
    copies = [
        pltpu.make_async_copy(source, target, sems.at[i])
        for i, (source, target) in enumerate(
            [(coords_hbm, coords_ref), (smooth_hbm, smooth_ref), (masses_hbm, masses_ref)]
        )
    ]
    for copy in copies:
        copy.start()
    block_ref, outs = outs[-1], outs[:-1]
    regions = block_ref.shape[0]
    per_dest = block_ref.shape[1] // FIELDS
    bits = per_dest.bit_length()
    per_word = 31 // bits
    seen = [jnp.int32(0)] * pl.cdiv(regions, per_word)
    me = lax.axis_index("region") if pairwise else 0
    places = []
    for n in range(owners_ref.shape[0]):
        d = owners_ref[n]
        word = d // per_word if len(seen) > 1 else 0
        shift = (d - word * per_word) * bits
        k = seen[0]
        for w in range(1, len(seen)):
            k = jnp.where(word == w, seen[w], k)
        k = (k >> shift) & ((1 << bits) - 1)
        step = jnp.int32(1) << shift
        seen = [s + (jnp.where(word == w, step, 0) if len(seen) > 1 else step) for w, s in enumerate(seen)]
        places.append((d ^ me if pairwise else d, k))
    for copy in copies:
        copy.wait()
    for n, (d, k) in enumerate(places):
        for c in range(3):
            block_ref[d, pl.ds(c * per_dest + k, 1)] = coords_ref[c, n:n + 1]
        block_ref[d, pl.ds(3 * per_dest + k, 1)] = smooth_ref[n:n + 1]
        block_ref[d, pl.ds(4 * per_dest + k, 1)] = masses_ref[n:n + 1]
    for k, out in enumerate(outs):
        out[...] = block_ref[k]


def group_tiles(coords, smooth, masses, owners, regions, pairwise):
    tile_dev, rows = smooth.shape
    per_dest = tile_dev // regions
    block = (FIELDS * per_dest, rows)
    hbm = pl.BlockSpec(memory_space=pltpu.HBM)
    scratch = [pltpu.VMEM(a.shape, f32) for a in (coords, smooth, masses)] + [pltpu.SemaphoreType.DMA((3,))]
    whole = (regions,) + block
    shapes = [block] * regions if pairwise else [whole]
    return pl.pallas_call(
        functools.partial(group_kernel, pairwise),
        out_shape=[jax.ShapeDtypeStruct(shape, f32) for shape in shapes],
        in_specs=[SMEM, hbm, hbm, hbm],
        out_specs=[VMEM] * len(shapes),
        scratch_shapes=([pltpu.VMEM(whole, f32)] if pairwise else []) + scratch,
        compiler_params=pltpu.CompilerParams(vmem_limit_bytes=63000000),
        name="group_tiles",
    )(owners, coords, smooth, masses)


def parts_of(x, count):
    parts = []
    for _ in range(count):
        part = x.astype(bf16).astype(f32)
        parts.append(part)
        x = x - part
    return parts


def dot(a, b):
    return jnp.dot(a, b, preferred_element_type=f32)


def own_field(block_ref, own_ref, live_ref, f):
    tile_dev = live_ref.shape[0]
    regions, per_dest = own_ref.shape[0], tile_dev // own_ref.shape[0]
    rows = pl.ds(f * per_dest, per_dest)
    value = jnp.concatenate([own_ref[block_ref[0] ^ r, rows] for r in range(regions)], axis=0)
    return value * live_ref[...] if f == 4 else value


def field_terms(fields):
    pos, h, mass = fields[:3], fields[3], fields[4]
    inverse_sq = 1.0 / (h * h)
    return pos, mass > 0, mass, inverse_sq, kernel_scale * inverse_sq / h


def put_rows(ref, values):
    count = values[0].shape[0]
    for k, value in enumerate(values):
        ref[k * count:(k + 1) * count] = value


def put_features(pos, live, mass, inverse_sq, partner_ref, mine_ref):
    c = inverse_sq * LOG2E
    square = pos[0] * pos[0] + pos[1] * pos[1] + pos[2] * pos[2]
    log_mass = jnp.where(live, jnp.log2(jnp.where(live, mass, 1.0)), EMPTY_LOG)
    one, zero = jnp.ones_like(c), jnp.zeros_like(c)
    put_rows(partner_ref, pos + [square, log_mass, one, zero, zero])
    put_rows(mine_ref, [2 * c * x for x in pos] + [-c, one, -c * square, zero, zero])


def tile_of(ref, e):
    return ref[pl.ds(e, 8, stride=ref.shape[0] // 8)]


def turned(ref, e):
    p1, p2, p3 = parts_of(tile_of(ref, e), 3)
    block = jnp.concatenate([p1, p1, p2, p1, p3, p2], axis=0).astype(bf16)
    fill = jnp.zeros((block.shape[1] - block.shape[0], block.shape[1]), bf16)
    return jnp.concatenate([block, fill], axis=0).T


def pair_weights(ref, e):
    def one_tile(e):
        o1, o2, o3 = parts_of(tile_of(ref, e), 3)
        block = jnp.concatenate([o1, o2, o1, o3, o1, o2], axis=0).astype(bf16)
        return jnp.concatenate([block, jnp.zeros((block.shape[1] - block.shape[0], block.shape[1]), bf16)], axis=0)

    first, second = one_tile(e), one_tile(e + 1)
    blank = jnp.zeros_like(first)
    return jnp.concatenate(
        [jnp.concatenate([first, blank], axis=1), jnp.concatenate([blank, second], axis=1)], axis=0
    )


def density_pair(turned_ref, own, partners, part_ref, at, store):
    rows = own.shape[1] // 2
    total = None
    for n, (e0, e1) in enumerate(partners):
        t = jnp.exp2(dot(jnp.concatenate([turned_ref[e0], turned_ref[e1]], axis=1), own))
        if store is not None:
            store[n * rows:(n + 1) * rows] = t
        part = jnp.sum(t.reshape(rows // 8, 8, 2 * rows), axis=0)
        total = part if total is None else total + part
    part_ref[pl.ds(at, 8)] = total[:, :rows]
    part_ref[pl.ds(at + 8, 8)] = total[:, rows:]


def inner_kernel(
    block_ref, lists_ref, own_ref, live_ref, pair_ref, part_ref, edge_ref, partner_ref, mine_ref, turned_ref, weights_ref,
):
    tile_dev = live_ref.shape[0]
    listed = lists_ref.shape[1]
    pos, live, mass, inverse_sq, _ = field_terms([own_field(block_ref, own_ref, live_ref, f) for f in range(FIELDS)])
    put_features(pos, live, mass, inverse_sq, partner_ref, mine_ref)

    @pl.loop(0, tile_dev, unroll=8)
    def _(t):
        turned_ref[t] = turned(partner_ref, t)

    edge_ref[:RIM] = turned_ref[:RIM]
    edge_ref[RIM:] = turned_ref[tile_dev - RIM:]
    count = pair_ref.shape[0]

    @pl.loop(0, count, unroll=UNROLL)
    def _(p):
        weights_ref[p] = pair_weights(mine_ref, HALO_TILES + 2 * p)

    @pl.loop(0, count, unroll=UNROLL)
    def _(p):
        t = HALO_TILES + 2 * p
        partners = [(lists_ref[t, n] - HALO_TILES, lists_ref[t + 1, n] - HALO_TILES) for n in range(listed)]
        density_pair(turned_ref, weights_ref[p], partners, part_ref, 16 * p, pair_ref.at[p])


def outer_kernel(
    block_ref, lists_ref, rim_lists_ref, own_ref, live_ref, below_ref, above_ref, pair_ref, part_ref, edge_ref,
    density_ref, accel_ref, partner_ref, mine_ref, turned_ref, rim_pair_ref, rim_part_ref, coef_ref, coefb_ref, out_ref,
):
    tile_dev, rows = live_ref.shape
    ext = tile_dev + 2 * RIM
    listed = lists_ref.shape[1]
    fields = [
        jnp.concatenate(
            [below_ref[f * RIM:(f + 1) * RIM], own_field(block_ref, own_ref, live_ref, f), above_ref[f * RIM:(f + 1) * RIM]], axis=0
        )
        for f in range(FIELDS)
    ]
    pos, live, mass, inverse_sq, norm = field_terms(fields)

    def rims(x):
        return jnp.concatenate([x[:2 * RIM], x[tile_dev:]], axis=0)

    put_features([rims(x) for x in pos], rims(live), rims(mass), rims(inverse_sq), partner_ref, mine_ref)
    for e in range(RIM):
        turned_ref[e] = turned(partner_ref, e)
        turned_ref[RIM + e] = edge_ref[e]
        turned_ref[2 * RIM + e] = edge_ref[RIM + e]
        turned_ref[3 * RIM + e] = turned(partner_ref, 3 * RIM + e)

    edge_pairs = HALO_TILES
    half = HALO_TILES // 2
    for side in range(2):
        for i in range(edge_pairs):
            e = 2 * RIM * side + HALO_TILES + 2 * i
            own_side = (i >= half) if side == 0 else (i < half)
            if own_side:
                t = e - RIM if side == 0 else e - 3 * RIM + tile_dev
                shift = HALO_TILES if side == 0 else HALO_TILES - tile_dev + 2 * RIM
                partners = [(lists_ref[t, n] + shift, lists_ref[t + 1, n] + shift) for n in range(listed)]
                store = rim_pair_ref.at[half * side + i % half]
            else:
                first = (2 * i if side == 0 else HALO_TILES + 2 * (i - half)) * listed
                shift = HALO_TILES - tile_dev if side == 0 else HALO_TILES + 2 * RIM
                partners = [
                    (rim_lists_ref[first + n] + shift, rim_lists_ref[first + listed + n] + shift) for n in range(listed)
                ]
                store = None
            at = 16 * (edge_pairs * side + i)
            density_pair(turned_ref, pair_weights(mine_ref, e), partners, rim_part_ref, at, store)

    inner_tiles = tile_dev - RIM
    raw = jnp.concatenate(
        [
            sum(rim_part_ref[pl.ds(k, RIM, stride=8)] for k in range(8)),
            sum(part_ref[pl.ds(k, inner_tiles, stride=8)] for k in range(8)),
            sum(rim_part_ref[pl.ds(8 * RIM + k, RIM, stride=8)] for k in range(8)),
        ],
        axis=0,
    )
    inner = slice(HALO_TILES, ext - HALO_TILES)
    raw = raw * norm[inner]
    q = jnp.where(live[inner], jnp.exp2(jnp.log2(jnp.where(live[inner], raw, 1.0)) * (-1.0 / 3.0)), 0.0)
    pad = jnp.zeros((HALO_TILES, rows), f32)
    q = jnp.concatenate([pad, q, pad], axis=0)
    put_rows(coef_ref, [jnp.ones_like(q)] + pos + [q] + [q * x for x in pos])

    @pl.loop(0, ext, unroll=8)
    def _(e):
        coefb_ref[e] = jnp.concatenate(parts_of(tile_of(coef_ref, e), 2), axis=0).astype(bf16)

    def force_pair(t, pair):
        total = None
        for n in range(listed):
            e0, e1 = lists_ref[t, n] + HALO_TILES, lists_ref[t + 1, n] + HALO_TILES
            left = jnp.concatenate([coefb_ref[e0], coefb_ref[e1]], axis=0)
            w = pair[n * rows:(n + 1) * rows]
            high = w.astype(bf16)
            part = dot(left, high) + dot(left, (w - high.astype(f32)).astype(bf16))
            total = part if total is None else total + part
        at = 8 * t
        out_ref[pl.ds(at, 8)] = total[:8, :rows] + total[8:16, :rows]
        out_ref[pl.ds(at + 8, 8)] = total[16:24, rows:] + total[24:, rows:]

    for i in range(half):
        force_pair(2 * i, rim_pair_ref.at[i])
        force_pair(tile_dev - HALO_TILES + 2 * i, rim_pair_ref.at[half + i])

    @pl.loop(0, pair_ref.shape[0], unroll=UNROLL)
    def _(p):
        force_pair(HALO_TILES + 2 * p, pair_ref.at[p])

    mine = slice(RIM, RIM + tile_dev)
    own_live = live_ref[...]
    density_ref[...] = raw[HALO_TILES:HALO_TILES + tile_dev] * own_live
    q_own = q[mine]
    scale = own_live * (2.0 * inverse_sq[mine] * norm[mine])
    sums = [out_ref[pl.ds(k, tile_dev, stride=8)] for k in range(8)]
    for c in range(3):
        x = pos[c][mine]
        accel_ref[c] = scale * (q_own * (x * sums[0] - sums[1 + c]) + (x * sums[4] - sums[5 + c]))


def inner_density(block, lists, own, live):
    tile_dev, rows = live.shape
    listed = lists.shape[1]
    count = (tile_dev - RIM) // 2
    return pl.pallas_call(
        inner_kernel,
        out_shape=(
            jax.ShapeDtypeStruct((count, listed * rows, 2 * rows), f32),
            jax.ShapeDtypeStruct((16 * count, rows), f32),
            jax.ShapeDtypeStruct((2 * RIM, rows, rows), bf16),
        ),
        in_specs=[SMEM, SMEM, VMEM, VMEM],
        out_specs=(VMEM, VMEM, VMEM),
        scratch_shapes=[
            pltpu.VMEM((8 * tile_dev, rows), f32),
            pltpu.VMEM((8 * tile_dev, rows), f32),
            pltpu.VMEM((tile_dev, rows, rows), bf16),
            pltpu.VMEM((count, 2 * rows, 2 * rows), bf16),
        ],
        compiler_params=pltpu.CompilerParams(vmem_limit_bytes=24 << 20),
        cost_estimate=pl.CostEstimate(flops=10 ** 9, bytes_accessed=10 ** 7, transcendentals=0),
        name="inner_density",
    )(block, lists, own, live)


def outer_step(block, lists, rim_lists, own, live, below, above, pair, part, edge):
    tile_dev, rows = live.shape
    ext = tile_dev + 2 * RIM
    listed = lists.shape[1]
    return pl.pallas_call(
        outer_kernel,
        out_shape=(jax.ShapeDtypeStruct((tile_dev, rows), f32), jax.ShapeDtypeStruct((3, tile_dev, rows), f32)),
        in_specs=[SMEM] * 3 + [VMEM] * 7,
        out_specs=(VMEM, VMEM),
        scratch_shapes=[
            pltpu.VMEM((8 * 4 * RIM, rows), f32),
            pltpu.VMEM((8 * 4 * RIM, rows), f32),
            pltpu.VMEM((4 * RIM, rows, rows), bf16),
            pltpu.VMEM((HALO_TILES, listed * rows, 2 * rows), f32),
            pltpu.VMEM((8 * 2 * RIM, rows), f32),
            pltpu.VMEM((8 * ext, rows), f32),
            pltpu.VMEM((ext, 16, rows), bf16),
            pltpu.VMEM((8 * tile_dev, rows), f32),
        ],
        compiler_params=pltpu.CompilerParams(vmem_limit_bytes=24 << 20),
        name="outer_step",
    )(block, lists, rim_lists, own, live, below, above, pair, part, edge)


def per_device(coords, smooth, masses, owners, counts, neighbours):
    tile_dev, rows = smooth.shape
    regions = lax.axis_size("region")
    subs = lax.axis_size("sub")
    per_dest = tile_dev // regions
    listed = neighbours.shape[1]
    pairwise = regions <= 4 and regions & (regions - 1) == 0
    grouped = group_tiles(coords, smooth, masses, owners, regions, pairwise)
    if pairwise:
        me = lax.axis_index("region")
        blocks = [grouped[0]]
        for k in range(1, regions):
            blocks.append(lax.ppermute(grouped[k], "region", [(i, i ^ k) for i in range(regions)]))
        own = jnp.stack(blocks)
    else:
        me = jnp.int32(0)
        own = lax.all_to_all(grouped[0], "region", 0, 0, tiled=True)
    first_block = me.astype(jnp.int32).reshape(1)
    live = (jnp.arange(rows, dtype=jnp.int32)[None, :] < counts[:, None]).astype(f32)
    by_field = own.reshape(regions, FIELDS, per_dest, rows)

    def rim(first):
        if pairwise:
            block = lax.dynamic_index_in_dim(by_field, me ^ (0 if first else regions - 1), 0, keepdims=False)
            block = block[:, :RIM] if first else block[:, per_dest - RIM:]
        else:
            blocks = RIM // per_dest
            block = by_field[:blocks] if first else by_field[regions - blocks:]
            block = jnp.swapaxes(block, 0, 1).reshape(FIELDS, RIM, rows)
        tiles = slice(0, RIM) if first else slice(tile_dev - RIM, tile_dev)
        block = jnp.concatenate([block[:4], (block[4] * live[tiles])[None]], axis=0).reshape(FIELDS * RIM, rows)
        near = slice(0, HALO_TILES) if first else slice(tile_dev - HALO_TILES, tile_dev)
        ids = neighbours[near].astype(f32).reshape(1, HALO_TILES * listed)
        return jnp.concatenate([block, jnp.pad(ids, ((0, 7), (0, rows - HALO_TILES * listed)))], axis=0)

    up = [(i, (i + 1) % subs) for i in range(subs)]
    down = [(j, i) for i, j in up]
    below = lax.ppermute(rim(False), "sub", up)
    above = lax.ppermute(rim(True), "sub", down)
    pair, part, edge = inner_density(first_block, neighbours, own, live)
    count = HALO_TILES * listed
    rim_lists = jnp.concatenate([below[FIELDS * RIM, :count], above[FIELDS * RIM, :count]]).astype(jnp.int32)
    return outer_step(first_block, neighbours, rim_lists, own, live, below, above, pair, part, edge)


def solution(mesh):
    in_specs = (
        P(None, ("region", "sub"), None),
        P(("region", "sub"), None),
        P(("region", "sub"), None),
        P(("region", "sub")),
        P(("region", "sub")),
        P(("region", "sub"), None),
    )
    out_specs = (P(("region", "sub"), None), P(None, ("region", "sub"), None))
    return jax.shard_map(
        per_device, mesh=mesh, in_specs=in_specs, out_specs=out_specs, check_vma=False
    )
```

```python
import functools
import math

import jax
import jax.numpy as jnp
from jax import lax
from jax.experimental import pallas as pl
from jax.experimental.pallas import tpu as pltpu
from jax.sharding import PartitionSpec as P


HALO_TILES = 4
RIM = 2 * HALO_TILES
FIELDS = 5
UNROLL = 7
EMPTY_LOG = -1024.0
LOG2E = 1.4426950408889634
kernel_scale = math.pi ** (-1.5)

f32, bf16 = jnp.float32, jnp.bfloat16
VMEM = pl.BlockSpec(memory_space=pltpu.VMEM)
SMEM = pl.BlockSpec(memory_space=pltpu.SMEM)


def group_kernel(pairwise, count, *refs):
    sources, outs = refs[:4], refs[4:4 + count]
    owners_ref, coords_ref, smooth_ref, masses_ref, block_ref, sems, out_sems = refs[4 + count:]
    targets = (owners_ref, coords_ref, smooth_ref, masses_ref)
    copies = [pltpu.make_async_copy(s, t, sems.at[i]) for i, (s, t) in enumerate(zip(sources, targets))]
    for copy in copies:
        copy.start()
    copies[0].wait()
    regions = block_ref.shape[0]
    per_dest = block_ref.shape[1] // FIELDS
    bits = per_dest.bit_length()
    per_word = 31 // bits
    seen = [jnp.int32(0)] * pl.cdiv(regions, per_word)
    me = lax.axis_index("region") if pairwise else 0
    places = []
    for n in range(owners_ref.shape[0]):
        d = owners_ref[n]
        word = d // per_word if len(seen) > 1 else 0
        shift = (d - word * per_word) * bits
        k = seen[0]
        for w in range(1, len(seen)):
            k = jnp.where(word == w, seen[w], k)
        k = (k >> shift) & ((1 << bits) - 1)
        step = jnp.int32(1) << shift
        seen = [s + (jnp.where(word == w, step, 0) if len(seen) > 1 else step) for w, s in enumerate(seen)]
        places.append((d ^ me if pairwise else d, k))
    for copy in copies[1:]:
        copy.wait()
    for n, (d, k) in enumerate(places):
        for c in range(3):
            block_ref[d, pl.ds(c * per_dest + k, 1)] = coords_ref[c, n:n + 1]
        block_ref[d, pl.ds(3 * per_dest + k, 1)] = smooth_ref[n:n + 1]
        block_ref[d, pl.ds(4 * per_dest + k, 1)] = masses_ref[n:n + 1]
    copies = [
        pltpu.make_async_copy(block_ref.at[k] if pairwise else block_ref, out, out_sems.at[k]) for k, out in enumerate(outs)
    ]
    for copy in copies:
        copy.start()
    for copy in copies:
        copy.wait()


def group_tiles(coords, smooth, masses, owners, regions, pairwise):
    tile_dev, rows = smooth.shape
    per_dest = tile_dev // regions
    block = (FIELDS * per_dest, rows)
    hbm = pl.BlockSpec(memory_space=pltpu.HBM)
    whole = (regions,) + block
    shapes = [block] * regions if pairwise else [whole]
    return pl.pallas_call(
        functools.partial(group_kernel, pairwise, len(shapes)),
        out_shape=[jax.ShapeDtypeStruct(shape, f32) for shape in shapes],
        in_specs=[hbm] * 4,
        out_specs=[hbm] * len(shapes),
        scratch_shapes=[pltpu.SMEM(owners.shape, jnp.int32)]
        + [pltpu.VMEM(a.shape, f32) for a in (coords, smooth, masses)]
        + [pltpu.VMEM(whole, f32), pltpu.SemaphoreType.DMA((4,)), pltpu.SemaphoreType.DMA((len(shapes),))],
        name="group_tiles",
    )(owners, coords, smooth, masses)


def stage_kernel(lists_ref, local_ref, live_ref, ids_ref, here_ref):
    tile_dev, rows = live_ref.shape
    listed = lists_ref.shape[0] - 1
    lane = lax.broadcasted_iota(jnp.int32, (8, rows), 1)
    row = lax.broadcasted_iota(jnp.int32, (8, rows), 0)
    for t in range(0, tile_dev, 8):
        limit = jnp.full((8, rows), lists_ref[listed, t])
        for i in range(1, 8):
            limit = jnp.where(row == i, lists_ref[listed, t + i], limit)
        live_ref[t:t + 8] = (lane < limit).astype(f32)
    for side, start in enumerate((0, tile_dev - HALO_TILES)):
        ids = jnp.zeros((8, rows), f32)
        for i in range(HALO_TILES):
            for n in range(listed):
                ids = jnp.where(lane == i * listed + n, lists_ref[n, start + i].astype(f32), ids)
        ids_ref[side] = ids
    here_ref[...] = local_ref[...]


def stage(lists, local):
    tile_dev, rows = lists.shape[1], local.shape[-1]
    return pl.pallas_call(
        stage_kernel,
        out_shape=(
            jax.ShapeDtypeStruct((tile_dev, rows), f32),
            jax.ShapeDtypeStruct((2, 8, rows), f32),
            jax.ShapeDtypeStruct(local.shape, f32),
        ),
        in_specs=[SMEM, VMEM],
        out_specs=(VMEM,) * 3,
        compiler_params=pltpu.CompilerParams(vmem_limit_bytes=4 << 20),
        name="stage",
    )(lists, local)


def parts_of(x, count):
    parts = []
    for _ in range(count):
        part = x.astype(bf16).astype(f32)
        parts.append(part)
        x = x - part
    return parts


def dot(a, b):
    return jnp.dot(a, b, preferred_element_type=f32)


def own_field(block_ref, own_ref, live_ref, f):
    tile_dev = live_ref.shape[0]
    regions, per_dest = own_ref.shape[0], tile_dev // own_ref.shape[0]
    rows = pl.ds(f * per_dest, per_dest)
    value = jnp.concatenate([own_ref[block_ref[0] ^ r, rows] for r in range(regions)], axis=0)
    return value * live_ref[...] if f == 4 else value


def field_terms(fields):
    pos, h, mass = fields[:3], fields[3], fields[4]
    inverse_sq = 1.0 / (h * h)
    return pos, mass > 0, mass, inverse_sq, kernel_scale * inverse_sq / h


def put_rows(ref, values):
    count = values[0].shape[0]
    for k, value in enumerate(values):
        ref[k * count:(k + 1) * count] = value


def put_features(pos, live, mass, inverse_sq, partner_ref, mine_ref):
    c = inverse_sq * LOG2E
    square = pos[0] * pos[0] + pos[1] * pos[1] + pos[2] * pos[2]
    log_mass = jnp.where(live, jnp.log2(jnp.where(live, mass, 1.0)), EMPTY_LOG)
    one, zero = jnp.ones_like(c), jnp.zeros_like(c)
    put_rows(partner_ref, pos + [square, log_mass, one, zero, zero])
    put_rows(mine_ref, [2 * c * x for x in pos] + [-c, one, -c * square, zero, zero])


def tile_of(ref, e):
    return ref[pl.ds(e, 8, stride=ref.shape[0] // 8)]


def turned(ref, e):
    p1, p2, p3 = parts_of(tile_of(ref, e), 3)
    block = jnp.concatenate([p1, p1, p2, p1, p3, p2], axis=0).astype(bf16)
    fill = jnp.zeros((block.shape[1] - block.shape[0], block.shape[1]), bf16)
    return jnp.concatenate([block, fill], axis=0).T


def pair_weights(ref, e):
    def one_tile(e):
        o1, o2, o3 = parts_of(tile_of(ref, e), 3)
        block = jnp.concatenate([o1, o2, o1, o3, o1, o2], axis=0).astype(bf16)
        return jnp.concatenate([block, jnp.zeros((block.shape[1] - block.shape[0], block.shape[1]), bf16)], axis=0)

    first, second = one_tile(e), one_tile(e + 1)
    blank = jnp.zeros_like(first)
    return jnp.concatenate(
        [jnp.concatenate([first, blank], axis=1), jnp.concatenate([blank, second], axis=1)], axis=0
    )


def density_pair(turned_ref, own, partners, part_ref, at, store):
    rows = own.shape[1] // 2
    total = None
    for n, (e0, e1) in enumerate(partners):
        t = jnp.exp2(dot(jnp.concatenate([turned_ref[e0], turned_ref[e1]], axis=1), own))
        if store is not None:
            store[n * rows:(n + 1) * rows] = t
        part = jnp.sum(t.reshape(rows // 8, 8, 2 * rows), axis=0)
        total = part if total is None else total + part
    part_ref[pl.ds(at, 8)] = total[:, :rows]
    part_ref[pl.ds(at + 8, 8)] = total[:, rows:]


def inner_kernel(
    block_ref, lists_ref, own_ref, live_ref, pair_ref, part_ref, edge_ref, partner_ref, mine_ref, turned_ref, weights_ref,
):
    tile_dev = live_ref.shape[0]
    listed = lists_ref.shape[0] - 1
    pos, live, mass, inverse_sq, _ = field_terms([own_field(block_ref, own_ref, live_ref, f) for f in range(FIELDS)])
    put_features(pos, live, mass, inverse_sq, partner_ref, mine_ref)

    @pl.loop(0, tile_dev, unroll=8)
    def _(t):
        turned_ref[t] = turned(partner_ref, t)

    edge_ref[:RIM] = turned_ref[:RIM]
    edge_ref[RIM:] = turned_ref[tile_dev - RIM:]
    count = pair_ref.shape[0]

    @pl.loop(0, count, unroll=UNROLL)
    def _(p):
        weights_ref[p] = pair_weights(mine_ref, HALO_TILES + 2 * p)

    @pl.loop(0, count, unroll=UNROLL)
    def _(p):
        t = HALO_TILES + 2 * p
        partners = [(lists_ref[n, t] - HALO_TILES, lists_ref[n, t + 1] - HALO_TILES) for n in range(listed)]
        density_pair(turned_ref, weights_ref[p], partners, part_ref, 16 * p, pair_ref.at[p])


def outer_kernel(
    block_ref, lists_ref, rim_lists_ref, own_ref, live_ref, below_ref, above_ref, pair_ref, part_ref, edge_ref,
    density_ref, accel_ref, partner_ref, mine_ref, turned_ref, rim_pair_ref, rim_part_ref, coef_ref, coefb_ref, out_ref,
):
    tile_dev, rows = live_ref.shape
    ext = tile_dev + 2 * RIM
    listed = lists_ref.shape[0] - 1
    fields = [
        jnp.concatenate(
            [below_ref[f * RIM:(f + 1) * RIM], own_field(block_ref, own_ref, live_ref, f), above_ref[f * RIM:(f + 1) * RIM]], axis=0
        )
        for f in range(FIELDS)
    ]
    pos, live, mass, inverse_sq, norm = field_terms(fields)

    def rims(x):
        return jnp.concatenate([x[:2 * RIM], x[tile_dev:]], axis=0)

    put_features([rims(x) for x in pos], rims(live), rims(mass), rims(inverse_sq), partner_ref, mine_ref)
    for e in range(RIM):
        turned_ref[e] = turned(partner_ref, e)
        turned_ref[RIM + e] = edge_ref[e]
        turned_ref[2 * RIM + e] = edge_ref[RIM + e]
        turned_ref[3 * RIM + e] = turned(partner_ref, 3 * RIM + e)

    edge_pairs = HALO_TILES
    half = HALO_TILES // 2
    for side in range(2):
        for i in range(edge_pairs):
            e = 2 * RIM * side + HALO_TILES + 2 * i
            own_side = (i >= half) if side == 0 else (i < half)
            if own_side:
                t = e - RIM if side == 0 else e - 3 * RIM + tile_dev
                shift = HALO_TILES if side == 0 else HALO_TILES - tile_dev + 2 * RIM
                partners = [(lists_ref[n, t] + shift, lists_ref[n, t + 1] + shift) for n in range(listed)]
                store = rim_pair_ref.at[half * side + i % half]
            else:
                first = (2 * i if side == 0 else HALO_TILES + 2 * (i - half)) * listed
                shift = HALO_TILES - tile_dev if side == 0 else HALO_TILES + 2 * RIM
                partners = [
                    (rim_lists_ref[first + n] + shift, rim_lists_ref[first + listed + n] + shift) for n in range(listed)
                ]
                store = None
            at = 16 * (edge_pairs * side + i)
            density_pair(turned_ref, pair_weights(mine_ref, e), partners, rim_part_ref, at, store)

    inner_tiles = tile_dev - RIM
    raw = jnp.concatenate(
        [
            sum(rim_part_ref[pl.ds(k, RIM, stride=8)] for k in range(8)),
            sum(part_ref[pl.ds(k, inner_tiles, stride=8)] for k in range(8)),
            sum(rim_part_ref[pl.ds(8 * RIM + k, RIM, stride=8)] for k in range(8)),
        ],
        axis=0,
    )
    inner = slice(HALO_TILES, ext - HALO_TILES)
    raw = raw * norm[inner]
    q = jnp.where(live[inner], jnp.exp2(jnp.log2(jnp.where(live[inner], raw, 1.0)) * (-1.0 / 3.0)), 0.0)
    pad = jnp.zeros((HALO_TILES, rows), f32)
    q = jnp.concatenate([pad, q, pad], axis=0)
    put_rows(coef_ref, [jnp.ones_like(q)] + pos + [q] + [q * x for x in pos])

    @pl.loop(0, ext, unroll=8)
    def _(e):
        coefb_ref[e] = jnp.concatenate(parts_of(tile_of(coef_ref, e), 2), axis=0).astype(bf16)

    def force_pair(t, pair):
        total = None
        for n in range(listed):
            e0, e1 = lists_ref[n, t] + HALO_TILES, lists_ref[n, t + 1] + HALO_TILES
            left = jnp.concatenate([coefb_ref[e0], coefb_ref[e1]], axis=0)
            w = pair[n * rows:(n + 1) * rows]
            high = w.astype(bf16)
            part = dot(left, high) + dot(left, (w - high.astype(f32)).astype(bf16))
            total = part if total is None else total + part
        at = 8 * t
        out_ref[pl.ds(at, 8)] = total[:8, :rows] + total[8:16, :rows]
        out_ref[pl.ds(at + 8, 8)] = total[16:24, rows:] + total[24:, rows:]

    for i in range(half):
        force_pair(2 * i, rim_pair_ref.at[i])
        force_pair(tile_dev - HALO_TILES + 2 * i, rim_pair_ref.at[half + i])

    @pl.loop(0, pair_ref.shape[0], unroll=UNROLL)
    def _(p):
        force_pair(HALO_TILES + 2 * p, pair_ref.at[p])

    mine = slice(RIM, RIM + tile_dev)
    own_live = live_ref[...]
    density_ref[...] = raw[HALO_TILES:HALO_TILES + tile_dev] * own_live
    q_own = q[mine]
    scale = own_live * (2.0 * inverse_sq[mine] * norm[mine])
    sums = [out_ref[pl.ds(k, tile_dev, stride=8)] for k in range(8)]
    for c in range(3):
        x = pos[c][mine]
        accel_ref[c] = scale * (q_own * (x * sums[0] - sums[1 + c]) + (x * sums[4] - sums[5 + c]))


def inner_density(block, lists, own, live):
    tile_dev, rows = live.shape
    listed = lists.shape[0] - 1
    count = (tile_dev - RIM) // 2
    return pl.pallas_call(
        inner_kernel,
        out_shape=(
            jax.ShapeDtypeStruct((count, listed * rows, 2 * rows), f32),
            jax.ShapeDtypeStruct((16 * count, rows), f32),
            jax.ShapeDtypeStruct((2 * RIM, rows, rows), bf16),
        ),
        in_specs=[SMEM, SMEM, VMEM, VMEM],
        out_specs=(VMEM, VMEM, VMEM),
        scratch_shapes=[
            pltpu.VMEM((8 * tile_dev, rows), f32),
            pltpu.VMEM((8 * tile_dev, rows), f32),
            pltpu.VMEM((tile_dev, rows, rows), bf16),
            pltpu.VMEM((count, 2 * rows, 2 * rows), bf16),
        ],
        compiler_params=pltpu.CompilerParams(vmem_limit_bytes=24 << 20),
        cost_estimate=pl.CostEstimate(flops=10 ** 9, bytes_accessed=10 ** 7, transcendentals=0),
        name="inner_density",
    )(block, lists, own, live)


def outer_step(block, lists, rim_lists, own, live, below, above, pair, part, edge):
    tile_dev, rows = live.shape
    ext = tile_dev + 2 * RIM
    listed = lists.shape[0] - 1
    return pl.pallas_call(
        outer_kernel,
        out_shape=(jax.ShapeDtypeStruct((tile_dev, rows), f32), jax.ShapeDtypeStruct((3, tile_dev, rows), f32)),
        in_specs=[SMEM] * 3 + [VMEM] * 7,
        out_specs=(VMEM, VMEM),
        scratch_shapes=[
            pltpu.VMEM((8 * 4 * RIM, rows), f32),
            pltpu.VMEM((8 * 4 * RIM, rows), f32),
            pltpu.VMEM((4 * RIM, rows, rows), bf16),
            pltpu.VMEM((HALO_TILES, listed * rows, 2 * rows), f32),
            pltpu.VMEM((8 * 2 * RIM, rows), f32),
            pltpu.VMEM((8 * ext, rows), f32),
            pltpu.VMEM((ext, 16, rows), bf16),
            pltpu.VMEM((8 * tile_dev, rows), f32),
        ],
        compiler_params=pltpu.CompilerParams(vmem_limit_bytes=24 << 20),
        name="outer_step",
    )(block, lists, rim_lists, own, live, below, above, pair, part, edge)


def per_device(coords, smooth, masses, owners, counts, neighbours):
    tile_dev, rows = smooth.shape
    regions = lax.axis_size("region")
    subs = lax.axis_size("sub")
    per_dest = tile_dev // regions
    listed = neighbours.shape[1]
    lists = jnp.concatenate([neighbours.T, counts[None]], axis=0)
    pairwise = regions <= 4 and regions & (regions - 1) == 0
    grouped = group_tiles(coords, smooth, masses, owners, regions, pairwise)
    if pairwise:
        me = lax.axis_index("region")
        live, ids, local = stage(lists, grouped[0])
        blocks = [local]
        for k in range(1, regions):
            blocks.append(lax.ppermute(grouped[k], "region", [(i, i ^ k) for i in range(regions)]))
        own = jnp.stack(blocks)
    else:
        me = jnp.int32(0)
        live, ids, _ = stage(lists, grouped[0][0])
        own = lax.all_to_all(grouped[0], "region", 0, 0, tiled=True)
    first_block = me.astype(jnp.int32).reshape(1)
    by_field = own.reshape(regions, FIELDS, per_dest, rows)

    def rim(first):
        if pairwise:
            block = lax.dynamic_index_in_dim(by_field, me ^ (0 if first else regions - 1), 0, keepdims=False)
            block = block[:, :RIM] if first else block[:, per_dest - RIM:]
        else:
            blocks = RIM // per_dest
            block = by_field[:blocks] if first else by_field[regions - blocks:]
            block = jnp.swapaxes(block, 0, 1).reshape(FIELDS, RIM, rows)
        tiles = slice(0, RIM) if first else slice(tile_dev - RIM, tile_dev)
        block = jnp.concatenate([block[:4], (block[4] * live[tiles])[None]], axis=0).reshape(FIELDS * RIM, rows)
        return jnp.concatenate([block, ids[0 if first else 1]], axis=0)

    up = [(i, (i + 1) % subs) for i in range(subs)]
    down = [(j, i) for i, j in up]
    below = lax.ppermute(rim(False), "sub", up)
    above = lax.ppermute(rim(True), "sub", down)
    pair, part, edge = inner_density(first_block, lists, own, live)
    count = HALO_TILES * listed
    rim_lists = jnp.concatenate([below[FIELDS * RIM, :count], above[FIELDS * RIM, :count]]).astype(jnp.int32)
    return outer_step(first_block, lists, rim_lists, own, live, below, above, pair, part, edge)


def solution(mesh):
    in_specs = (
        P(None, ("region", "sub"), None),
        P(("region", "sub"), None),
        P(("region", "sub"), None),
        P(("region", "sub")),
        P(("region", "sub")),
        P(("region", "sub"), None),
    )
    out_specs = (P(("region", "sub"), None), P(None, ("region", "sub"), None))
    return jax.shard_map(
        per_device, mesh=mesh, in_specs=in_specs, out_specs=out_specs, check_vma=False
    )
```

```python
import functools
import math

import jax
import jax.numpy as jnp
from jax import lax
from jax.experimental import pallas as pl
from jax.experimental.pallas import tpu as pltpu
from jax.sharding import PartitionSpec as P


HALO_TILES = 4
RIM = 2 * HALO_TILES
FIELDS = 5
UNROLL = 7
CHUNKS = 4
EMPTY_LOG = -1024.0
LOG2E = 1.4426950408889634
kernel_scale = math.pi ** (-1.5)

f32, bf16 = jnp.float32, jnp.bfloat16
VMEM = pl.BlockSpec(memory_space=pltpu.VMEM)
SMEM = pl.BlockSpec(memory_space=pltpu.SMEM)


def group_kernel(pairwise, count, *refs):
    sources, outs = refs[:4], refs[4:4 + count]
    owners_ref, coords_ref, smooth_ref, masses_ref, block_ref, sems, out_sems = refs[4 + count:]
    targets = (owners_ref, coords_ref, smooth_ref, masses_ref)
    copies = [pltpu.make_async_copy(s, t, sems.at[i]) for i, (s, t) in enumerate(zip(sources, targets))]
    for copy in copies:
        copy.start()
    copies[0].wait()
    regions = block_ref.shape[0]
    per_dest = block_ref.shape[1] // FIELDS
    bits = per_dest.bit_length()
    per_word = 31 // bits
    seen = [jnp.int32(0)] * pl.cdiv(regions, per_word)
    me = lax.axis_index("region") if pairwise else 0
    places = []
    for n in range(owners_ref.shape[0]):
        d = owners_ref[n]
        word = d // per_word if len(seen) > 1 else 0
        shift = (d - word * per_word) * bits
        k = seen[0]
        for w in range(1, len(seen)):
            k = jnp.where(word == w, seen[w], k)
        k = (k >> shift) & ((1 << bits) - 1)
        step = jnp.int32(1) << shift
        seen = [s + (jnp.where(word == w, step, 0) if len(seen) > 1 else step) for w, s in enumerate(seen)]
        places.append((d ^ me if pairwise else d, k))
    for copy in copies[1:]:
        copy.wait()
    for n, (d, k) in enumerate(places):
        for c in range(3):
            block_ref[d, pl.ds(c * per_dest + k, 1)] = coords_ref[c, n:n + 1]
        block_ref[d, pl.ds(3 * per_dest + k, 1)] = smooth_ref[n:n + 1]
        block_ref[d, pl.ds(4 * per_dest + k, 1)] = masses_ref[n:n + 1]
    copies = [
        pltpu.make_async_copy(block_ref.at[k] if pairwise else block_ref, out, out_sems.at[k]) for k, out in enumerate(outs)
    ]
    for copy in copies:
        copy.start()
    for copy in copies:
        copy.wait()


def group_tiles(coords, smooth, masses, owners, regions, pairwise):
    tile_dev, rows = smooth.shape
    per_dest = tile_dev // regions
    block = (FIELDS * per_dest, rows)
    hbm = pl.BlockSpec(memory_space=pltpu.HBM)
    whole = (regions,) + block
    shapes = [block] * regions if pairwise else [whole]
    return pl.pallas_call(
        functools.partial(group_kernel, pairwise, len(shapes)),
        out_shape=[jax.ShapeDtypeStruct(shape, f32) for shape in shapes],
        in_specs=[hbm] * 4,
        out_specs=[hbm] * len(shapes),
        scratch_shapes=[pltpu.SMEM(owners.shape, jnp.int32)]
        + [pltpu.VMEM(a.shape, f32) for a in (coords, smooth, masses)]
        + [pltpu.VMEM(whole, f32), pltpu.SemaphoreType.DMA((4,)), pltpu.SemaphoreType.DMA((len(shapes),))],
        name="group_tiles",
    )(owners, coords, smooth, masses)


def stage_kernel(lists_ref, local_ref, live_ref, ids_ref, here_ref):
    tile_dev, rows = live_ref.shape
    listed = lists_ref.shape[0] - 1
    lane = lax.broadcasted_iota(jnp.int32, (8, rows), 1)
    row = lax.broadcasted_iota(jnp.int32, (8, rows), 0)
    for t in range(0, tile_dev, 8):
        limit = jnp.full((8, rows), lists_ref[listed, t])
        for i in range(1, 8):
            limit = jnp.where(row == i, lists_ref[listed, t + i], limit)
        live_ref[t:t + 8] = (lane < limit).astype(f32)
    for side, start in enumerate((0, tile_dev - HALO_TILES)):
        ids = jnp.zeros((8, rows), f32)
        for i in range(HALO_TILES):
            for n in range(listed):
                ids = jnp.where(lane == i * listed + n, lists_ref[n, start + i].astype(f32), ids)
        ids_ref[side] = ids
    here_ref[...] = local_ref[...]


def stage(lists, local):
    tile_dev, rows = lists.shape[1], local.shape[-1]
    return pl.pallas_call(
        stage_kernel,
        out_shape=(
            jax.ShapeDtypeStruct((tile_dev, rows), f32),
            jax.ShapeDtypeStruct((2, 8, rows), f32),
            jax.ShapeDtypeStruct(local.shape, f32),
        ),
        in_specs=[SMEM, VMEM],
        out_specs=(VMEM,) * 3,
        compiler_params=pltpu.CompilerParams(vmem_limit_bytes=4 << 20),
        name="stage",
    )(lists, local)


def parts_of(x, count):
    parts = []
    for _ in range(count):
        part = x.astype(bf16).astype(f32)
        parts.append(part)
        x = x - part
    return parts


def dot(a, b):
    return jnp.dot(a, b, preferred_element_type=f32)


def own_field(block_ref, own_ref, live_ref, f):
    tile_dev = live_ref.shape[0]
    regions, per_dest = own_ref.shape[0], tile_dev // own_ref.shape[0]
    rows = pl.ds(f * per_dest, per_dest)
    value = jnp.concatenate([own_ref[block_ref[0] ^ r, rows] for r in range(regions)], axis=0)
    return value * live_ref[...] if f == 4 else value


def field_terms(fields):
    pos, h, mass = fields[:3], fields[3], fields[4]
    inverse_sq = 1.0 / (h * h)
    return pos, mass > 0, mass, inverse_sq, kernel_scale * inverse_sq / h


def put_rows(ref, values):
    count = values[0].shape[0]
    for k, value in enumerate(values):
        ref[k * count:(k + 1) * count] = value


def put_features(pos, live, mass, inverse_sq, partner_ref, mine_ref):
    c = inverse_sq * LOG2E
    square = pos[0] * pos[0] + pos[1] * pos[1] + pos[2] * pos[2]
    log_mass = jnp.where(live, jnp.log2(jnp.where(live, mass, 1.0)), EMPTY_LOG)
    one, zero = jnp.ones_like(c), jnp.zeros_like(c)
    put_rows(partner_ref, pos + [square, log_mass, one, zero, zero])
    put_rows(mine_ref, [2 * c * x for x in pos] + [-c, one, -c * square, zero, zero])


def tile_of(ref, e):
    return ref[pl.ds(e, 8, stride=ref.shape[0] // 8)]


def turned(ref, e):
    p1, p2, p3 = parts_of(tile_of(ref, e), 3)
    block = jnp.concatenate([p1, p1, p2, p1, p3, p2], axis=0).astype(bf16)
    fill = jnp.zeros((block.shape[1] - block.shape[0], block.shape[1]), bf16)
    return jnp.concatenate([block, fill], axis=0).T


def pair_weights(ref, e):
    def one_tile(e):
        o1, o2, o3 = parts_of(tile_of(ref, e), 3)
        block = jnp.concatenate([o1, o2, o1, o3, o1, o2], axis=0).astype(bf16)
        return jnp.concatenate([block, jnp.zeros((block.shape[1] - block.shape[0], block.shape[1]), bf16)], axis=0)

    first, second = one_tile(e), one_tile(e + 1)
    blank = jnp.zeros_like(first)
    return jnp.concatenate(
        [jnp.concatenate([first, blank], axis=1), jnp.concatenate([blank, second], axis=1)], axis=0
    )


def density_pair(turned_ref, own, partners, part_ref, at, store):
    rows = own.shape[1] // 2
    total = None
    for n, (e0, e1) in enumerate(partners):
        t = jnp.exp2(dot(jnp.concatenate([turned_ref[e0], turned_ref[e1]], axis=1), own))
        if store is not None:
            store[n * rows:(n + 1) * rows] = t
        part = jnp.sum(t.reshape(rows // 8, 8, 2 * rows), axis=0)
        total = part if total is None else total + part
    part_ref[pl.ds(at, 8)] = total[:, :rows]
    part_ref[pl.ds(at + 8, 8)] = total[:, rows:]


def inner_kernel(last, flag_ref, block_ref, lists_ref, own_ref, live_ref, *refs):
    pair_ref, part_ref, edge_ref, turned_ref, weights_ref, partner_ref, mine_ref = refs[5:] if last else refs
    tile_dev = live_ref.shape[0]
    listed = lists_ref.shape[0] - 1
    chunk = pair_ref.shape[0] // CHUNKS
    ahead = 2 * chunk + 2 * HALO_TILES

    def turn(t):
        turned_ref[t] = turned(partner_ref, t)

    def weigh(p):
        weights_ref[p] = pair_weights(mine_ref, HALO_TILES + 2 * p)

    def pair(p):
        t = HALO_TILES + 2 * p
        partners = [(lists_ref[n, t] - HALO_TILES, lists_ref[n, t + 1] - HALO_TILES) for n in range(listed)]
        density_pair(turned_ref, weights_ref[p], partners, part_ref, 16 * p, pair_ref.at[p])

    @pl.when(flag_ref[0] == 1)
    def _():
        pos, live, mass, inverse_sq, _ = field_terms(
            [own_field(block_ref, own_ref, live_ref, f) for f in range(FIELDS)]
        )
        put_features(pos, live, mass, inverse_sq, partner_ref, mine_ref)
        for t in range(ahead):
            turn(t)
        for p in range(chunk):
            weigh(p)

        @pl.loop(0, CHUNKS - 1)
        def _(c):
            for i in range(chunk):
                pair(c * chunk + i)
            for i in range(2 * chunk):
                turn(c * 2 * chunk + ahead + i)
            for i in range(chunk):
                weigh((c + 1) * chunk + i)

        edge_ref[:RIM] = turned_ref[:RIM]
        edge_ref[RIM:] = turned_ref[tile_dev - RIM:]

    if last:
        for i in range(chunk):
            pair((CHUNKS - 1) * chunk + i)


def outer_kernel(
    block_ref, lists_ref, rim_lists_ref, own_ref, live_ref, below_ref, above_ref, pair_ref, part_ref, edge_ref,
    density_ref, accel_ref, partner_ref, mine_ref, turned_ref, rim_pair_ref, rim_part_ref, coef_ref, coefb_ref, out_ref,
):
    tile_dev, rows = live_ref.shape
    ext = tile_dev + 2 * RIM
    listed = lists_ref.shape[0] - 1
    fields = [
        jnp.concatenate(
            [below_ref[f * RIM:(f + 1) * RIM], own_field(block_ref, own_ref, live_ref, f), above_ref[f * RIM:(f + 1) * RIM]], axis=0
        )
        for f in range(FIELDS)
    ]
    pos, live, mass, inverse_sq, norm = field_terms(fields)

    def rims(x):
        return jnp.concatenate([x[:2 * RIM], x[tile_dev:]], axis=0)

    put_features([rims(x) for x in pos], rims(live), rims(mass), rims(inverse_sq), partner_ref, mine_ref)
    for e in range(RIM):
        turned_ref[e] = turned(partner_ref, e)
        turned_ref[RIM + e] = edge_ref[e]
        turned_ref[2 * RIM + e] = edge_ref[RIM + e]
        turned_ref[3 * RIM + e] = turned(partner_ref, 3 * RIM + e)

    edge_pairs = HALO_TILES
    half = HALO_TILES // 2
    for side in range(2):
        for i in range(edge_pairs):
            e = 2 * RIM * side + HALO_TILES + 2 * i
            own_side = (i >= half) if side == 0 else (i < half)
            if own_side:
                t = e - RIM if side == 0 else e - 3 * RIM + tile_dev
                shift = HALO_TILES if side == 0 else HALO_TILES - tile_dev + 2 * RIM
                partners = [(lists_ref[n, t] + shift, lists_ref[n, t + 1] + shift) for n in range(listed)]
                store = rim_pair_ref.at[half * side + i % half]
            else:
                first = (2 * i if side == 0 else HALO_TILES + 2 * (i - half)) * listed
                shift = HALO_TILES - tile_dev if side == 0 else HALO_TILES + 2 * RIM
                partners = [
                    (rim_lists_ref[first + n] + shift, rim_lists_ref[first + listed + n] + shift) for n in range(listed)
                ]
                store = None
            at = 16 * (edge_pairs * side + i)
            density_pair(turned_ref, pair_weights(mine_ref, e), partners, rim_part_ref, at, store)

    inner_tiles = tile_dev - RIM
    raw = jnp.concatenate(
        [
            sum(rim_part_ref[pl.ds(k, RIM, stride=8)] for k in range(8)),
            sum(part_ref[pl.ds(k, inner_tiles, stride=8)] for k in range(8)),
            sum(rim_part_ref[pl.ds(8 * RIM + k, RIM, stride=8)] for k in range(8)),
        ],
        axis=0,
    )
    inner = slice(HALO_TILES, ext - HALO_TILES)
    raw = raw * norm[inner]
    q = jnp.where(live[inner], jnp.exp2(jnp.log2(jnp.where(live[inner], raw, 1.0)) * (-1.0 / 3.0)), 0.0)
    pad = jnp.zeros((HALO_TILES, rows), f32)
    q = jnp.concatenate([pad, q, pad], axis=0)
    put_rows(coef_ref, [jnp.ones_like(q)] + pos + [q] + [q * x for x in pos])

    @pl.loop(0, ext, unroll=8)
    def _(e):
        coefb_ref[e] = jnp.concatenate(parts_of(tile_of(coef_ref, e), 2), axis=0).astype(bf16)

    def force_pair(t, pair):
        total = None
        for n in range(listed):
            e0, e1 = lists_ref[n, t] + HALO_TILES, lists_ref[n, t + 1] + HALO_TILES
            left = jnp.concatenate([coefb_ref[e0], coefb_ref[e1]], axis=0)
            w = pair[n * rows:(n + 1) * rows]
            high = w.astype(bf16)
            part = dot(left, high) + dot(left, (w - high.astype(f32)).astype(bf16))
            total = part if total is None else total + part
        at = 8 * t
        out_ref[pl.ds(at, 8)] = total[:8, :rows] + total[8:16, :rows]
        out_ref[pl.ds(at + 8, 8)] = total[16:24, rows:] + total[24:, rows:]

    for i in range(half):
        force_pair(2 * i, rim_pair_ref.at[i])
        force_pair(tile_dev - HALO_TILES + 2 * i, rim_pair_ref.at[half + i])

    @pl.loop(0, pair_ref.shape[0], unroll=UNROLL)
    def _(p):
        force_pair(HALO_TILES + 2 * p, pair_ref.at[p])

    mine = slice(RIM, RIM + tile_dev)
    own_live = live_ref[...]
    density_ref[...] = raw[HALO_TILES:HALO_TILES + tile_dev] * own_live
    q_own = q[mine]
    scale = own_live * (2.0 * inverse_sq[mine] * norm[mine])
    sums = [out_ref[pl.ds(k, tile_dev, stride=8)] for k in range(8)]
    for c in range(3):
        x = pos[c][mine]
        accel_ref[c] = scale * (q_own * (x * sums[0] - sums[1 + c]) + (x * sums[4] - sums[5 + c]))


def inner_density(flag, block, lists, own, live, carried):
    tile_dev, rows = live.shape
    listed = lists.shape[0] - 1
    count = (tile_dev - RIM) // 2
    last = carried is not None
    shapes = (
        jax.ShapeDtypeStruct((count, listed * rows, 2 * rows), f32),
        jax.ShapeDtypeStruct((16 * count, rows), f32),
        jax.ShapeDtypeStruct((2 * RIM, rows, rows), bf16),
        jax.ShapeDtypeStruct((tile_dev, rows, rows), bf16),
        jax.ShapeDtypeStruct((count, 2 * rows, 2 * rows), bf16),
    )
    return pl.pallas_call(
        functools.partial(inner_kernel, last),
        out_shape=shapes,
        in_specs=[SMEM] * 3 + [VMEM] * (7 if last else 2),
        out_specs=(VMEM,) * 5,
        input_output_aliases={5 + i: i for i in range(5)} if last else {},
        scratch_shapes=[pltpu.VMEM((8 * tile_dev, rows), f32), pltpu.VMEM((8 * tile_dev, rows), f32)],
        compiler_params=pltpu.CompilerParams(vmem_limit_bytes=24 << 20),
        cost_estimate=pl.CostEstimate(flops=10 ** 9, bytes_accessed=10 ** 7, transcendentals=0),
        name="inner_density_last" if last else "inner_density",
    )(flag, block, lists, own, live, *(carried or ()))


def outer_step(block, lists, rim_lists, own, live, below, above, pair, part, edge):
    tile_dev, rows = live.shape
    ext = tile_dev + 2 * RIM
    listed = lists.shape[0] - 1
    return pl.pallas_call(
        outer_kernel,
        out_shape=(jax.ShapeDtypeStruct((tile_dev, rows), f32), jax.ShapeDtypeStruct((3, tile_dev, rows), f32)),
        in_specs=[SMEM] * 3 + [VMEM] * 7,
        out_specs=(VMEM, VMEM),
        scratch_shapes=[
            pltpu.VMEM((8 * 4 * RIM, rows), f32),
            pltpu.VMEM((8 * 4 * RIM, rows), f32),
            pltpu.VMEM((4 * RIM, rows, rows), bf16),
            pltpu.VMEM((HALO_TILES, listed * rows, 2 * rows), f32),
            pltpu.VMEM((8 * 2 * RIM, rows), f32),
            pltpu.VMEM((8 * ext, rows), f32),
            pltpu.VMEM((ext, 16, rows), bf16),
            pltpu.VMEM((8 * tile_dev, rows), f32),
        ],
        compiler_params=pltpu.CompilerParams(vmem_limit_bytes=24 << 20),
        name="outer_step",
    )(block, lists, rim_lists, own, live, below, above, pair, part, edge)


def per_device(coords, smooth, masses, owners, counts, neighbours):
    tile_dev, rows = smooth.shape
    regions = lax.axis_size("region")
    subs = lax.axis_size("sub")
    per_dest = tile_dev // regions
    listed = neighbours.shape[1]
    lists = jnp.concatenate([neighbours.T, counts[None]], axis=0)
    pairwise = regions <= 4 and regions & (regions - 1) == 0
    grouped = group_tiles(coords, smooth, masses, owners, regions, pairwise)
    if pairwise:
        me = lax.axis_index("region")
        live, ids, local = stage(lists, grouped[0])
        blocks = [local]
        for k in range(1, regions):
            blocks.append(lax.ppermute(grouped[k], "region", [(i, i ^ k) for i in range(regions)]))
        own = jnp.stack(blocks)
    else:
        me = jnp.int32(0)
        live, ids, unused = stage(lists, grouped[0][0])
        own = lax.all_to_all(grouped[0], "region", 0, 0, tiled=True)
    first_block = me.astype(jnp.int32).reshape(1)
    by_field = own.reshape(regions, FIELDS, per_dest, rows)

    def rim(first):
        if pairwise:
            block = lax.dynamic_index_in_dim(by_field, me ^ (0 if first else regions - 1), 0, keepdims=False)
            block = block[:, :RIM] if first else block[:, per_dest - RIM:]
        else:
            blocks = RIM // per_dest
            block = by_field[:blocks] if first else by_field[regions - blocks:]
            block = jnp.swapaxes(block, 0, 1).reshape(FIELDS, RIM, rows)
        tiles = slice(0, RIM) if first else slice(tile_dev - RIM, tile_dev)
        block = jnp.concatenate([block[:4], (block[4] * live[tiles])[None]], axis=0).reshape(FIELDS * RIM, rows)
        return jnp.concatenate([block, ids[0 if first else 1]], axis=0)

    up = [(i, (i + 1) % subs) for i in range(subs)]
    down = [(j, i) for i, j in up]
    first_sub = lax.axis_index("sub") == 0
    early = first_sub.astype(jnp.int32).reshape(1)
    below = lax.ppermute(rim(False), "sub", up)
    ends = rim(True)
    above = lax.ppermute(ends, "sub", [pair for pair in down if pair[0] != 0])
    carried = inner_density(early, first_block, lists, own, live, None)
    around = lax.ppermute(ends, "sub", [pair for pair in down if pair[0] == 0])
    pair, part, edge, *unused = inner_density(1 - early, first_block, lists, own, live, carried)
    above = jnp.where(lax.axis_index("sub") == subs - 1, around, above)
    count = HALO_TILES * listed
    rim_lists = jnp.concatenate([below[FIELDS * RIM, :count], above[FIELDS * RIM, :count]]).astype(jnp.int32)
    return outer_step(first_block, lists, rim_lists, own, live, below, above, pair, part, edge)


def solution(mesh):
    in_specs = (
        P(None, ("region", "sub"), None),
        P(("region", "sub"), None),
        P(("region", "sub"), None),
        P(("region", "sub")),
        P(("region", "sub")),
        P(("region", "sub"), None),
    )
    out_specs = (P(("region", "sub"), None), P(None, ("region", "sub"), None))
    return jax.shard_map(
        per_device, mesh=mesh, in_specs=in_specs, out_specs=out_specs, check_vma=False
    )
```

```python
import functools
import math

import jax
import jax.numpy as jnp
from jax import lax
from jax.experimental import pallas as pl
from jax.experimental.pallas import tpu as pltpu
from jax.sharding import PartitionSpec as P


HALO_TILES = 4
RIM = 2 * HALO_TILES
FIELDS = 5
UNROLL = 7
CHUNKS = 4
EARLY = 2
EMPTY_LOG = -1024.0
LOG2E = 1.4426950408889634
kernel_scale = math.pi ** (-1.5)

f32, bf16 = jnp.float32, jnp.bfloat16
VMEM = pl.BlockSpec(memory_space=pltpu.VMEM)
SMEM = pl.BlockSpec(memory_space=pltpu.SMEM)


def group_kernel(pairwise, count, *refs):
    sources, outs = refs[:4], refs[4:4 + count]
    owners_ref, coords_ref, smooth_ref, masses_ref, block_ref, sems, out_sems = refs[4 + count:]
    targets = (owners_ref, coords_ref, smooth_ref, masses_ref)
    copies = [pltpu.make_async_copy(s, t, sems.at[i]) for i, (s, t) in enumerate(zip(sources, targets))]
    for copy in copies:
        copy.start()
    copies[0].wait()
    regions = block_ref.shape[0]
    per_dest = block_ref.shape[1] // FIELDS
    bits = per_dest.bit_length()
    per_word = 31 // bits
    seen = [jnp.int32(0)] * pl.cdiv(regions, per_word)
    me = lax.axis_index("region") if pairwise else 0
    places = []
    for n in range(owners_ref.shape[0]):
        d = owners_ref[n]
        word = d // per_word if len(seen) > 1 else 0
        shift = (d - word * per_word) * bits
        k = seen[0]
        for w in range(1, len(seen)):
            k = jnp.where(word == w, seen[w], k)
        k = (k >> shift) & ((1 << bits) - 1)
        step = jnp.int32(1) << shift
        seen = [s + (jnp.where(word == w, step, 0) if len(seen) > 1 else step) for w, s in enumerate(seen)]
        places.append((d ^ me if pairwise else d, k))
    for copy in copies[1:]:
        copy.wait()
    for n, (d, k) in enumerate(places):
        for c in range(3):
            block_ref[d, pl.ds(c * per_dest + k, 1)] = coords_ref[c, n:n + 1]
        block_ref[d, pl.ds(3 * per_dest + k, 1)] = smooth_ref[n:n + 1]
        block_ref[d, pl.ds(4 * per_dest + k, 1)] = masses_ref[n:n + 1]
    copies = [
        pltpu.make_async_copy(block_ref.at[k] if pairwise else block_ref, out, out_sems.at[k]) for k, out in enumerate(outs)
    ]
    for copy in copies:
        copy.start()
    for copy in copies:
        copy.wait()


def group_tiles(coords, smooth, masses, owners, regions, pairwise):
    tile_dev, rows = smooth.shape
    per_dest = tile_dev // regions
    block = (FIELDS * per_dest, rows)
    hbm = pl.BlockSpec(memory_space=pltpu.HBM)
    whole = (regions,) + block
    shapes = [block] * regions if pairwise else [whole]
    return pl.pallas_call(
        functools.partial(group_kernel, pairwise, len(shapes)),
        out_shape=[jax.ShapeDtypeStruct(shape, f32) for shape in shapes],
        in_specs=[hbm] * 4,
        out_specs=[hbm] * len(shapes),
        scratch_shapes=[pltpu.SMEM(owners.shape, jnp.int32)]
        + [pltpu.VMEM(a.shape, f32) for a in (coords, smooth, masses)]
        + [pltpu.VMEM(whole, f32), pltpu.SemaphoreType.DMA((4,)), pltpu.SemaphoreType.DMA((len(shapes),))],
        name="group_tiles",
    )(owners, coords, smooth, masses)


def stage_kernel(table_ref, local_ref, live_ref, ids_ref, here_ref):
    tile_dev, rows = live_ref.shape
    listed = table_ref.shape[0] - 2
    lane = lax.broadcasted_iota(jnp.int32, (8, rows), 1)
    row = lax.broadcasted_iota(jnp.int32, (8, rows), 0)
    for t in range(0, tile_dev, 8):
        limit = jnp.full((8, rows), table_ref[listed, t])
        for i in range(1, 8):
            limit = jnp.where(row == i, table_ref[listed, t + i], limit)
        live_ref[t:t + 8] = (lane < limit).astype(f32)
    for side, start in enumerate((0, tile_dev - HALO_TILES)):
        ids = jnp.zeros((8, rows), f32)
        for i in range(HALO_TILES):
            for n in range(listed):
                ids = jnp.where(lane == i * listed + n, table_ref[n, start + i].astype(f32), ids)
        ids_ref[side] = ids
    here_ref[...] = local_ref[...]


def stage(table, local):
    tile_dev, rows = table.shape[1], local.shape[-1]
    return pl.pallas_call(
        stage_kernel,
        out_shape=(
            jax.ShapeDtypeStruct((tile_dev, rows), f32),
            jax.ShapeDtypeStruct((2, 8, rows), f32),
            jax.ShapeDtypeStruct(local.shape, f32),
        ),
        in_specs=[SMEM, VMEM],
        out_specs=(VMEM,) * 3,
        compiler_params=pltpu.CompilerParams(vmem_limit_bytes=4 << 20),
        name="stage",
    )(table, local)


def parts_of(x, count):
    parts = []
    for _ in range(count):
        part = x.astype(bf16).astype(f32)
        parts.append(part)
        x = x - part
    return parts


def dot(a, b):
    return jnp.dot(a, b, preferred_element_type=f32)


def own_field(table_ref, own_ref, live_ref, f):
    tile_dev = live_ref.shape[0]
    regions, per_dest = own_ref.shape[0], tile_dev // own_ref.shape[0]
    rows = pl.ds(f * per_dest, per_dest)
    value = jnp.concatenate([own_ref[table_ref[table_ref.shape[0] - 1, 0] ^ r, rows] for r in range(regions)], axis=0)
    return value * live_ref[...] if f == 4 else value


def field_terms(fields):
    pos, h, mass = fields[:3], fields[3], fields[4]
    inverse_sq = 1.0 / (h * h)
    return pos, mass > 0, mass, inverse_sq, kernel_scale * inverse_sq / h


def put_rows(ref, values):
    count = values[0].shape[0]
    for k, value in enumerate(values):
        ref[k * count:(k + 1) * count] = value


def put_features(pos, live, mass, inverse_sq, partner_ref, mine_ref):
    c = inverse_sq * LOG2E
    square = pos[0] * pos[0] + pos[1] * pos[1] + pos[2] * pos[2]
    log_mass = jnp.where(live, jnp.log2(jnp.where(live, mass, 1.0)), EMPTY_LOG)
    one, zero = jnp.ones_like(c), jnp.zeros_like(c)
    put_rows(partner_ref, pos + [square, log_mass, one, zero, zero])
    put_rows(mine_ref, [2 * c * x for x in pos] + [-c, one, -c * square, zero, zero])


def tile_of(ref, e):
    return ref[pl.ds(e, 8, stride=ref.shape[0] // 8)]


def turned(ref, e):
    p1, p2, p3 = parts_of(tile_of(ref, e), 3)
    block = jnp.concatenate([p1, p1, p2, p1, p3, p2], axis=0).astype(bf16)
    fill = jnp.zeros((block.shape[1] - block.shape[0], block.shape[1]), bf16)
    return jnp.concatenate([block, fill], axis=0).T


def pair_weights(ref, e):
    def one_tile(e):
        o1, o2, o3 = parts_of(tile_of(ref, e), 3)
        block = jnp.concatenate([o1, o2, o1, o3, o1, o2], axis=0).astype(bf16)
        return jnp.concatenate([block, jnp.zeros((block.shape[1] - block.shape[0], block.shape[1]), bf16)], axis=0)

    first, second = one_tile(e), one_tile(e + 1)
    blank = jnp.zeros_like(first)
    return jnp.concatenate(
        [jnp.concatenate([first, blank], axis=1), jnp.concatenate([blank, second], axis=1)], axis=0
    )


def density_pair(turned_ref, own, partners, part_ref, at, store):
    rows = own.shape[1] // 2
    total = None
    for n, (e0, e1) in enumerate(partners):
        t = jnp.exp2(dot(jnp.concatenate([turned_ref[e0], turned_ref[e1]], axis=1), own))
        if store is not None:
            store[n * rows:(n + 1) * rows] = t
        part = jnp.sum(t.reshape(rows // 8, 8, 2 * rows), axis=0)
        total = part if total is None else total + part
    part_ref[pl.ds(at, 8)] = total[:, :rows]
    part_ref[pl.ds(at + 8, 8)] = total[:, rows:]


def inner_kernel(late, table_ref, own_ref, live_ref, *refs):
    pair_ref, part_ref, turned_ref, weights_ref = refs[-6 - late:-2 - late]
    partner_ref, mine_ref = refs[-2:]
    tile_dev = live_ref.shape[0]
    listed = table_ref.shape[0] - 2
    chunk = pair_ref.shape[0] // CHUNKS
    ahead = 2 * chunk + 2 * HALO_TILES

    def turn(t):
        turned_ref[t] = turned(partner_ref, t)

    def weigh(p):
        weights_ref[p] = pair_weights(mine_ref, HALO_TILES + 2 * p)

    def features():
        pos, live, mass, inverse_sq, _ = field_terms(
            [own_field(table_ref, own_ref, live_ref, f) for f in range(FIELDS)]
        )
        put_features(pos, live, mass, inverse_sq, partner_ref, mine_ref)

    def do_chunk(c, more=True):
        for i in range(chunk):
            t = HALO_TILES + 2 * (c * chunk + i)
            partners = [(table_ref[n, t] - HALO_TILES, table_ref[n, t + 1] - HALO_TILES) for n in range(listed)]
            p = c * chunk + i
            density_pair(turned_ref, weights_ref[p], partners, part_ref, 16 * p, pair_ref.at[p])
        if more:
            for i in range(2 * chunk):
                turn(c * 2 * chunk + ahead + i)
            for i in range(chunk):
                weigh((c + 1) * chunk + i)

    if late:
        features()

    @pl.when(table_ref[listed + 1, 1] == (0 if late else 1))
    def _():
        if not late:
            features()
        for t in range(ahead):
            turn(t)
        for p in range(chunk):
            weigh(p)
        pl.loop(0, EARLY)(do_chunk)

    if late:
        edge_ref = refs[-3]
        pl.loop(EARLY, CHUNKS - 1)(do_chunk)
        do_chunk(CHUNKS - 1, False)
        edge_ref[:RIM] = turned_ref[:RIM]
        edge_ref[RIM:] = turned_ref[tile_dev - RIM:]


def outer_kernel(
    table_ref, rim_lists_ref, own_ref, live_ref, below_ref, above_ref, pair_ref, part_ref, edge_ref,
    density_ref, accel_ref, partner_ref, mine_ref, turned_ref, rim_pair_ref, rim_part_ref, coef_ref, coefb_ref, out_ref,
):
    tile_dev, rows = live_ref.shape
    ext = tile_dev + 2 * RIM
    listed = table_ref.shape[0] - 2
    fields = [
        jnp.concatenate(
            [below_ref[f * RIM:(f + 1) * RIM], own_field(table_ref, own_ref, live_ref, f), above_ref[f * RIM:(f + 1) * RIM]], axis=0
        )
        for f in range(FIELDS)
    ]
    pos, live, mass, inverse_sq, norm = field_terms(fields)

    def rims(x):
        return jnp.concatenate([x[:2 * RIM], x[tile_dev:]], axis=0)

    put_features([rims(x) for x in pos], rims(live), rims(mass), rims(inverse_sq), partner_ref, mine_ref)
    for e in range(RIM):
        turned_ref[e] = turned(partner_ref, e)
        turned_ref[RIM + e] = edge_ref[e]
        turned_ref[2 * RIM + e] = edge_ref[RIM + e]
        turned_ref[3 * RIM + e] = turned(partner_ref, 3 * RIM + e)

    edge_pairs = HALO_TILES
    half = HALO_TILES // 2
    for side in range(2):
        for i in range(edge_pairs):
            e = 2 * RIM * side + HALO_TILES + 2 * i
            own_side = (i >= half) if side == 0 else (i < half)
            if own_side:
                t = e - RIM if side == 0 else e - 3 * RIM + tile_dev
                shift = HALO_TILES if side == 0 else HALO_TILES - tile_dev + 2 * RIM
                partners = [(table_ref[n, t] + shift, table_ref[n, t + 1] + shift) for n in range(listed)]
                store = rim_pair_ref.at[half * side + i % half]
            else:
                first = (2 * i if side == 0 else HALO_TILES + 2 * (i - half)) * listed
                shift = HALO_TILES - tile_dev if side == 0 else HALO_TILES + 2 * RIM
                partners = [
                    (rim_lists_ref[first + n] + shift, rim_lists_ref[first + listed + n] + shift) for n in range(listed)
                ]
                store = None
            at = 16 * (edge_pairs * side + i)
            density_pair(turned_ref, pair_weights(mine_ref, e), partners, rim_part_ref, at, store)

    inner_tiles = tile_dev - RIM
    raw = jnp.concatenate(
        [
            sum(rim_part_ref[pl.ds(k, RIM, stride=8)] for k in range(8)),
            sum(part_ref[pl.ds(k, inner_tiles, stride=8)] for k in range(8)),
            sum(rim_part_ref[pl.ds(8 * RIM + k, RIM, stride=8)] for k in range(8)),
        ],
        axis=0,
    )
    inner = slice(HALO_TILES, ext - HALO_TILES)
    raw = raw * norm[inner]
    q = jnp.where(live[inner], jnp.exp2(jnp.log2(jnp.where(live[inner], raw, 1.0)) * (-1.0 / 3.0)), 0.0)
    pad = jnp.zeros((HALO_TILES, rows), f32)
    q = jnp.concatenate([pad, q, pad], axis=0)
    put_rows(coef_ref, [jnp.ones_like(q)] + pos + [q] + [q * x for x in pos])

    @pl.loop(0, ext, unroll=8)
    def _(e):
        coefb_ref[e] = jnp.concatenate(parts_of(tile_of(coef_ref, e), 2), axis=0).astype(bf16)

    def force_pair(t, pair):
        total = None
        for n in range(listed):
            e0, e1 = table_ref[n, t] + HALO_TILES, table_ref[n, t + 1] + HALO_TILES
            left = jnp.concatenate([coefb_ref[e0], coefb_ref[e1]], axis=0)
            w = pair[n * rows:(n + 1) * rows]
            high = w.astype(bf16)
            part = dot(left, high) + dot(left, (w - high.astype(f32)).astype(bf16))
            total = part if total is None else total + part
        at = 8 * t
        out_ref[pl.ds(at, 8)] = total[:8, :rows] + total[8:16, :rows]
        out_ref[pl.ds(at + 8, 8)] = total[16:24, rows:] + total[24:, rows:]

    for i in range(half):
        force_pair(2 * i, rim_pair_ref.at[i])
        force_pair(tile_dev - HALO_TILES + 2 * i, rim_pair_ref.at[half + i])

    @pl.loop(0, pair_ref.shape[0], unroll=UNROLL)
    def _(p):
        force_pair(HALO_TILES + 2 * p, pair_ref.at[p])

    mine = slice(RIM, RIM + tile_dev)
    own_live = live_ref[...]
    density_ref[...] = raw[HALO_TILES:HALO_TILES + tile_dev] * own_live
    q_own = q[mine]
    scale = own_live * (2.0 * inverse_sq[mine] * norm[mine])
    sums = [out_ref[pl.ds(k, tile_dev, stride=8)] for k in range(8)]
    for c in range(3):
        x = pos[c][mine]
        accel_ref[c] = scale * (q_own * (x * sums[0] - sums[1 + c]) + (x * sums[4] - sums[5 + c]))


def inner_density(table, own, live, carried=()):
    tile_dev, rows = live.shape
    listed = table.shape[0] - 2
    count = (tile_dev - RIM) // 2
    late = len(carried) > 0
    shapes = [
        jax.ShapeDtypeStruct((count, listed * rows, 2 * rows), f32),
        jax.ShapeDtypeStruct((16 * count, rows), f32),
        jax.ShapeDtypeStruct((tile_dev, rows, rows), bf16),
        jax.ShapeDtypeStruct((count, 2 * rows, 2 * rows), bf16),
    ]
    edges = [jax.ShapeDtypeStruct((2 * RIM, rows, rows), bf16)] if late else []
    return pl.pallas_call(
        functools.partial(inner_kernel, late),
        out_shape=shapes + edges,
        in_specs=[SMEM] + [VMEM] * (2 + len(carried)),
        out_specs=[VMEM] * len(shapes + edges),
        input_output_aliases={3 + i: i for i in range(len(carried))},
        scratch_shapes=[pltpu.VMEM((8 * tile_dev, rows), f32), pltpu.VMEM((8 * tile_dev, rows), f32)],
        compiler_params=pltpu.CompilerParams(vmem_limit_bytes=24 << 20),
        cost_estimate=pl.CostEstimate(flops=10 ** 9, bytes_accessed=10 ** 7, transcendentals=0),
        name="inner_late" if late else "inner_early",
    )(table, own, live, *carried)


def outer_step(table, rim_lists, own, live, below, above, pair, part, edge):
    tile_dev, rows = live.shape
    ext = tile_dev + 2 * RIM
    listed = table.shape[0] - 2
    return pl.pallas_call(
        outer_kernel,
        out_shape=(jax.ShapeDtypeStruct((tile_dev, rows), f32), jax.ShapeDtypeStruct((3, tile_dev, rows), f32)),
        in_specs=[SMEM] * 2 + [VMEM] * 7,
        out_specs=(VMEM, VMEM),
        scratch_shapes=[
            pltpu.VMEM((8 * 4 * RIM, rows), f32),
            pltpu.VMEM((8 * 4 * RIM, rows), f32),
            pltpu.VMEM((4 * RIM, rows, rows), bf16),
            pltpu.VMEM((HALO_TILES, listed * rows, 2 * rows), f32),
            pltpu.VMEM((8 * 2 * RIM, rows), f32),
            pltpu.VMEM((8 * ext, rows), f32),
            pltpu.VMEM((ext, 16, rows), bf16),
            pltpu.VMEM((8 * tile_dev, rows), f32),
        ],
        compiler_params=pltpu.CompilerParams(vmem_limit_bytes=24 << 20),
        name="outer_step",
    )(table, rim_lists, own, live, below, above, pair, part, edge)


def per_device(coords, smooth, masses, owners, counts, neighbours):
    tile_dev, rows = smooth.shape
    regions = lax.axis_size("region")
    subs = lax.axis_size("sub")
    per_dest = tile_dev // regions
    listed = neighbours.shape[1]
    early = (lax.axis_index("sub") == 0).astype(jnp.int32)
    pairwise = regions <= 4 and regions & (regions - 1) == 0
    grouped = group_tiles(coords, smooth, masses, owners, regions, pairwise)
    me = lax.axis_index("region") if pairwise else jnp.int32(0)
    slot = jnp.arange(tile_dev, dtype=jnp.int32)
    scalars = jnp.where(slot == 0, me, jnp.where(slot == 1, early, 0))
    table = jnp.concatenate([neighbours.T, counts[None], scalars[None]], axis=0)
    if pairwise:
        live, ids, local = stage(table, grouped[0])
        blocks = [local]
        for k in range(1, regions):
            blocks.append(lax.ppermute(grouped[k], "region", [(i, i ^ k) for i in range(regions)]))
        own = jnp.stack(blocks)
    else:
        live, ids, _ = stage(table, grouped[0][0])
        own = lax.all_to_all(grouped[0], "region", 0, 0, tiled=True)
    by_field = own.reshape(regions, FIELDS, per_dest, rows)

    def rim(first):
        if pairwise:
            block = lax.dynamic_index_in_dim(by_field, me ^ (0 if first else regions - 1), 0, keepdims=False)
            block = block[:, :RIM] if first else block[:, per_dest - RIM:]
        else:
            blocks = RIM // per_dest
            block = by_field[:blocks] if first else by_field[regions - blocks:]
            block = jnp.swapaxes(block, 0, 1).reshape(FIELDS, RIM, rows)
        tiles = slice(0, RIM) if first else slice(tile_dev - RIM, tile_dev)
        block = jnp.concatenate([block[:4], (block[4] * live[tiles])[None]], axis=0).reshape(FIELDS * RIM, rows)
        return jnp.concatenate([block, ids[0 if first else 1]], axis=0)

    up = [(i, (i + 1) % subs) for i in range(subs)]
    down = [(j, i) for i, j in up]
    below = lax.ppermute(rim(False), "sub", up)
    carried = inner_density(table, own, live)
    above = lax.ppermute(rim(True), "sub", down)
    pair, part, _, _, edge = inner_density(table, own, live, carried)
    count = HALO_TILES * listed
    rim_lists = jnp.concatenate([below[FIELDS * RIM, :count], above[FIELDS * RIM, :count]]).astype(jnp.int32)
    return outer_step(table, rim_lists, own, live, below, above, pair, part, edge)


def solution(mesh):
    in_specs = (
        P(None, ("region", "sub"), None),
        P(("region", "sub"), None),
        P(("region", "sub"), None),
        P(("region", "sub")),
        P(("region", "sub")),
        P(("region", "sub"), None),
    )
    out_specs = (P(("region", "sub"), None), P(None, ("region", "sub"), None))
    return jax.shard_map(
        per_device, mesh=mesh, in_specs=in_specs, out_specs=out_specs, check_vma=False
    )
```

```python
import functools
import math

import jax
import jax.numpy as jnp
from jax import lax
from jax.experimental import pallas as pl
from jax.experimental.pallas import tpu as pltpu
from jax.sharding import PartitionSpec as P


HALO_TILES = 4
RIM = 2 * HALO_TILES
FIELDS = 5
UNROLL = 7
CHUNKS = 4
EMPTY_LOG = -1024.0
LOG2E = 1.4426950408889634
kernel_scale = math.pi ** (-1.5)

f32, bf16 = jnp.float32, jnp.bfloat16
VMEM = pl.BlockSpec(memory_space=pltpu.VMEM)
SMEM = pl.BlockSpec(memory_space=pltpu.SMEM)


def group_kernel(pairwise, count, *refs):
    sources, outs = refs[:4], refs[4:4 + count]
    owners_ref, coords_ref, smooth_ref, masses_ref, block_ref, sems, out_sems = refs[4 + count:]
    targets = (owners_ref, coords_ref, smooth_ref, masses_ref)
    copies = [pltpu.make_async_copy(s, t, sems.at[i]) for i, (s, t) in enumerate(zip(sources, targets))]
    for copy in copies:
        copy.start()
    copies[0].wait()
    regions = block_ref.shape[0]
    per_dest = block_ref.shape[1] // FIELDS
    bits = per_dest.bit_length()
    per_word = 31 // bits
    seen = [jnp.int32(0)] * pl.cdiv(regions, per_word)
    me = lax.axis_index("region") if pairwise else 0
    places = []
    for n in range(owners_ref.shape[0]):
        d = owners_ref[n]
        word = d // per_word if len(seen) > 1 else 0
        shift = (d - word * per_word) * bits
        k = seen[0]
        for w in range(1, len(seen)):
            k = jnp.where(word == w, seen[w], k)
        k = (k >> shift) & ((1 << bits) - 1)
        step = jnp.int32(1) << shift
        seen = [s + (jnp.where(word == w, step, 0) if len(seen) > 1 else step) for w, s in enumerate(seen)]
        places.append((d ^ me if pairwise else d, k))
    for copy in copies[1:]:
        copy.wait()
    for n, (d, k) in enumerate(places):
        for c in range(3):
            block_ref[d, pl.ds(c * per_dest + k, 1)] = coords_ref[c, n:n + 1]
        block_ref[d, pl.ds(3 * per_dest + k, 1)] = smooth_ref[n:n + 1]
        block_ref[d, pl.ds(4 * per_dest + k, 1)] = masses_ref[n:n + 1]
    copies = [
        pltpu.make_async_copy(block_ref.at[k] if pairwise else block_ref, out, out_sems.at[k]) for k, out in enumerate(outs)
    ]
    for copy in copies:
        copy.start()
    for copy in copies:
        copy.wait()


def group_tiles(coords, smooth, masses, owners, regions, pairwise):
    tile_dev, rows = smooth.shape
    per_dest = tile_dev // regions
    block = (FIELDS * per_dest, rows)
    hbm = pl.BlockSpec(memory_space=pltpu.HBM)
    whole = (regions,) + block
    shapes = [block] * regions if pairwise else [whole]
    return pl.pallas_call(
        functools.partial(group_kernel, pairwise, len(shapes)),
        out_shape=[jax.ShapeDtypeStruct(shape, f32) for shape in shapes],
        in_specs=[hbm] * 4,
        out_specs=[hbm] * len(shapes),
        scratch_shapes=[pltpu.SMEM(owners.shape, jnp.int32)]
        + [pltpu.VMEM(a.shape, f32) for a in (coords, smooth, masses)]
        + [pltpu.VMEM(whole, f32), pltpu.SemaphoreType.DMA((4,)), pltpu.SemaphoreType.DMA((len(shapes),))],
        name="group_tiles",
    )(owners, coords, smooth, masses)


def stage_kernel(table_ref, local_ref, live_ref, ids_ref, here_ref):
    tile_dev, rows = live_ref.shape
    listed = table_ref.shape[0] - 2
    lane = lax.broadcasted_iota(jnp.int32, (8, rows), 1)
    row = lax.broadcasted_iota(jnp.int32, (8, rows), 0)
    for t in range(0, tile_dev, 8):
        limit = jnp.full((8, rows), table_ref[listed, t])
        for i in range(1, 8):
            limit = jnp.where(row == i, table_ref[listed, t + i], limit)
        live_ref[t:t + 8] = (lane < limit).astype(f32)
    for side, start in enumerate((0, tile_dev - HALO_TILES)):
        ids = jnp.zeros((8, rows), f32)
        for i in range(HALO_TILES):
            for n in range(listed):
                ids = jnp.where(lane == i * listed + n, table_ref[n, start + i].astype(f32), ids)
        ids_ref[side] = ids
    here_ref[...] = local_ref[...]


def stage(table, local):
    tile_dev, rows = table.shape[1], local.shape[-1]
    return pl.pallas_call(
        stage_kernel,
        out_shape=(
            jax.ShapeDtypeStruct((tile_dev, rows), f32),
            jax.ShapeDtypeStruct((2, 8, rows), f32),
            jax.ShapeDtypeStruct(local.shape, f32),
        ),
        in_specs=[SMEM, VMEM],
        out_specs=(VMEM,) * 3,
        compiler_params=pltpu.CompilerParams(vmem_limit_bytes=4 << 20),
        name="stage",
    )(table, local)


def parts_of(x, count):
    parts = []
    for _ in range(count):
        part = x.astype(bf16).astype(f32)
        parts.append(part)
        x = x - part
    return parts


def dot(a, b):
    return jnp.dot(a, b, preferred_element_type=f32)


def own_field(table_ref, own_ref, live_ref, f):
    tile_dev = live_ref.shape[0]
    regions, per_dest = own_ref.shape[0], tile_dev // own_ref.shape[0]
    rows = pl.ds(f * per_dest, per_dest)
    value = jnp.concatenate([own_ref[table_ref[table_ref.shape[0] - 1, 0] ^ r, rows] for r in range(regions)], axis=0)
    return value * live_ref[...] if f == 4 else value


def field_terms(fields):
    pos, h, mass = fields[:3], fields[3], fields[4]
    inverse_sq = 1.0 / (h * h)
    return pos, mass > 0, mass, inverse_sq, kernel_scale * inverse_sq / h


def put_rows(ref, values):
    count = values[0].shape[0]
    for k, value in enumerate(values):
        ref[k * count:(k + 1) * count] = value


def put_features(pos, live, mass, inverse_sq, partner_ref, mine_ref):
    c = inverse_sq * LOG2E
    square = pos[0] * pos[0] + pos[1] * pos[1] + pos[2] * pos[2]
    log_mass = jnp.where(live, jnp.log2(jnp.where(live, mass, 1.0)), EMPTY_LOG)
    one, zero = jnp.ones_like(c), jnp.zeros_like(c)
    put_rows(partner_ref, pos + [square, log_mass, one, zero, zero])
    put_rows(mine_ref, [2 * c * x for x in pos] + [-c, one, -c * square, zero, zero])


def tile_of(ref, e):
    return ref[pl.ds(e, 8, stride=ref.shape[0] // 8)]


def turned(ref, e):
    p1, p2, p3 = parts_of(tile_of(ref, e), 3)
    block = jnp.concatenate([p1, p1, p2, p1, p3, p2], axis=0).astype(bf16)
    fill = jnp.zeros((block.shape[1] - block.shape[0], block.shape[1]), bf16)
    return jnp.concatenate([block, fill], axis=0).T


def pair_weights(ref, e):
    def one_tile(e):
        o1, o2, o3 = parts_of(tile_of(ref, e), 3)
        block = jnp.concatenate([o1, o2, o1, o3, o1, o2], axis=0).astype(bf16)
        return jnp.concatenate([block, jnp.zeros((block.shape[1] - block.shape[0], block.shape[1]), bf16)], axis=0)

    first, second = one_tile(e), one_tile(e + 1)
    blank = jnp.zeros_like(first)
    return jnp.concatenate(
        [jnp.concatenate([first, blank], axis=1), jnp.concatenate([blank, second], axis=1)], axis=0
    )


def density_pair(turned_ref, own, partners, part_ref, at, store):
    rows = own.shape[1] // 2
    total = None
    for n, (e0, e1) in enumerate(partners):
        t = jnp.exp2(dot(jnp.concatenate([turned_ref[e0], turned_ref[e1]], axis=1), own))
        if store is not None:
            store[n * rows:(n + 1) * rows] = t
        part = jnp.sum(t.reshape(rows // 8, 8, 2 * rows), axis=0)
        total = part if total is None else total + part
    part_ref[pl.ds(at, 8)] = total[:, :rows]
    part_ref[pl.ds(at + 8, 8)] = total[:, rows:]


def inner_kernel(late, table_ref, own_ref, live_ref, *refs):
    pair_ref, part_ref, turned_ref, weights_ref = refs[-6 - late:-2 - late]
    partner_ref, mine_ref = refs[-2:]
    tile_dev = live_ref.shape[0]
    listed = table_ref.shape[0] - 2
    chunk = pair_ref.shape[0] // CHUNKS
    ahead = 2 * chunk + 2 * HALO_TILES

    def turn(t):
        turned_ref[t] = turned(partner_ref, t)

    def weigh(p):
        weights_ref[p] = pair_weights(mine_ref, HALO_TILES + 2 * p)

    def features():
        pos, live, mass, inverse_sq, _ = field_terms(
            [own_field(table_ref, own_ref, live_ref, f) for f in range(FIELDS)]
        )
        put_features(pos, live, mass, inverse_sq, partner_ref, mine_ref)

    def do_chunk(c, more=True):
        for i in range(chunk):
            t = HALO_TILES + 2 * (c * chunk + i)
            partners = [(table_ref[n, t] - HALO_TILES, table_ref[n, t + 1] - HALO_TILES) for n in range(listed)]
            p = c * chunk + i
            density_pair(turned_ref, weights_ref[p], partners, part_ref, 16 * p, pair_ref.at[p])
        if more:
            for i in range(2 * chunk):
                turn(c * 2 * chunk + ahead + i)
            for i in range(chunk):
                weigh((c + 1) * chunk + i)

    early = table_ref[listed + 1, 1]

    def begin():
        features()
        for t in range(ahead):
            turn(t)
        for p in range(chunk):
            weigh(p)

    if late:
        pl.when(early > 0)(features)
        pl.when(early == 0)(begin)
        edge_ref = refs[-3]
        pl.loop(early, CHUNKS - 1)(do_chunk)
        do_chunk(CHUNKS - 1, False)
        edge_ref[:RIM] = turned_ref[:RIM]
        edge_ref[RIM:] = turned_ref[tile_dev - RIM:]
    else:

        @pl.when(early > 0)
        def _():
            begin()
            pl.loop(0, early)(do_chunk)


def outer_kernel(
    table_ref, rim_lists_ref, own_ref, live_ref, below_ref, above_ref, pair_ref, part_ref, edge_ref,
    density_ref, accel_ref, partner_ref, mine_ref, turned_ref, rim_pair_ref, rim_part_ref, coef_ref, coefb_ref, out_ref,
):
    tile_dev, rows = live_ref.shape
    ext = tile_dev + 2 * RIM
    listed = table_ref.shape[0] - 2
    fields = [
        jnp.concatenate(
            [below_ref[f * RIM:(f + 1) * RIM], own_field(table_ref, own_ref, live_ref, f), above_ref[f * RIM:(f + 1) * RIM]], axis=0
        )
        for f in range(FIELDS)
    ]
    pos, live, mass, inverse_sq, norm = field_terms(fields)

    def rims(x):
        return jnp.concatenate([x[:2 * RIM], x[tile_dev:]], axis=0)

    put_features([rims(x) for x in pos], rims(live), rims(mass), rims(inverse_sq), partner_ref, mine_ref)
    for e in range(RIM):
        turned_ref[e] = turned(partner_ref, e)
        turned_ref[RIM + e] = edge_ref[e]
        turned_ref[2 * RIM + e] = edge_ref[RIM + e]
        turned_ref[3 * RIM + e] = turned(partner_ref, 3 * RIM + e)

    edge_pairs = HALO_TILES
    half = HALO_TILES // 2
    for side in range(2):
        for i in range(edge_pairs):
            e = 2 * RIM * side + HALO_TILES + 2 * i
            own_side = (i >= half) if side == 0 else (i < half)
            if own_side:
                t = e - RIM if side == 0 else e - 3 * RIM + tile_dev
                shift = HALO_TILES if side == 0 else HALO_TILES - tile_dev + 2 * RIM
                partners = [(table_ref[n, t] + shift, table_ref[n, t + 1] + shift) for n in range(listed)]
                store = rim_pair_ref.at[half * side + i % half]
            else:
                first = (2 * i if side == 0 else HALO_TILES + 2 * (i - half)) * listed
                shift = HALO_TILES - tile_dev if side == 0 else HALO_TILES + 2 * RIM
                partners = [
                    (rim_lists_ref[first + n] + shift, rim_lists_ref[first + listed + n] + shift) for n in range(listed)
                ]
                store = None
            at = 16 * (edge_pairs * side + i)
            density_pair(turned_ref, pair_weights(mine_ref, e), partners, rim_part_ref, at, store)

    inner_tiles = tile_dev - RIM
    raw = jnp.concatenate(
        [
            sum(rim_part_ref[pl.ds(k, RIM, stride=8)] for k in range(8)),
            sum(part_ref[pl.ds(k, inner_tiles, stride=8)] for k in range(8)),
            sum(rim_part_ref[pl.ds(8 * RIM + k, RIM, stride=8)] for k in range(8)),
        ],
        axis=0,
    )
    inner = slice(HALO_TILES, ext - HALO_TILES)
    raw = raw * norm[inner]
    q = jnp.where(live[inner], jnp.exp2(jnp.log2(jnp.where(live[inner], raw, 1.0)) * (-1.0 / 3.0)), 0.0)
    pad = jnp.zeros((HALO_TILES, rows), f32)
    q = jnp.concatenate([pad, q, pad], axis=0)
    put_rows(coef_ref, [jnp.ones_like(q)] + pos + [q] + [q * x for x in pos])

    @pl.loop(0, ext, unroll=8)
    def _(e):
        coefb_ref[e] = jnp.concatenate(parts_of(tile_of(coef_ref, e), 2), axis=0).astype(bf16)

    def force_pair(t, pair):
        total = None
        for n in range(listed):
            e0, e1 = table_ref[n, t] + HALO_TILES, table_ref[n, t + 1] + HALO_TILES
            left = jnp.concatenate([coefb_ref[e0], coefb_ref[e1]], axis=0)
            w = pair[n * rows:(n + 1) * rows]
            high = w.astype(bf16)
            part = dot(left, high) + dot(left, (w - high.astype(f32)).astype(bf16))
            total = part if total is None else total + part
        at = 8 * t
        out_ref[pl.ds(at, 8)] = total[:8, :rows] + total[8:16, :rows]
        out_ref[pl.ds(at + 8, 8)] = total[16:24, rows:] + total[24:, rows:]

    for i in range(half):
        force_pair(2 * i, rim_pair_ref.at[i])
        force_pair(tile_dev - HALO_TILES + 2 * i, rim_pair_ref.at[half + i])

    @pl.loop(0, pair_ref.shape[0], unroll=UNROLL)
    def _(p):
        force_pair(HALO_TILES + 2 * p, pair_ref.at[p])

    mine = slice(RIM, RIM + tile_dev)
    own_live = live_ref[...]
    density_ref[...] = raw[HALO_TILES:HALO_TILES + tile_dev] * own_live
    q_own = q[mine]
    scale = own_live * (2.0 * inverse_sq[mine] * norm[mine])
    sums = [out_ref[pl.ds(k, tile_dev, stride=8)] for k in range(8)]
    for c in range(3):
        x = pos[c][mine]
        accel_ref[c] = scale * (q_own * (x * sums[0] - sums[1 + c]) + (x * sums[4] - sums[5 + c]))


def inner_density(table, own, live, carried=()):
    tile_dev, rows = live.shape
    listed = table.shape[0] - 2
    count = (tile_dev - RIM) // 2
    late = len(carried) > 0
    shapes = [
        jax.ShapeDtypeStruct((count, listed * rows, 2 * rows), f32),
        jax.ShapeDtypeStruct((16 * count, rows), f32),
        jax.ShapeDtypeStruct((tile_dev, rows, rows), bf16),
        jax.ShapeDtypeStruct((count, 2 * rows, 2 * rows), bf16),
    ]
    edges = [jax.ShapeDtypeStruct((2 * RIM, rows, rows), bf16)] if late else []
    return pl.pallas_call(
        functools.partial(inner_kernel, late),
        out_shape=shapes + edges,
        in_specs=[SMEM] + [VMEM] * (2 + len(carried)),
        out_specs=[VMEM] * len(shapes + edges),
        input_output_aliases={3 + i: i for i in range(len(carried))},
        scratch_shapes=[pltpu.VMEM((8 * tile_dev, rows), f32), pltpu.VMEM((8 * tile_dev, rows), f32)],
        compiler_params=pltpu.CompilerParams(vmem_limit_bytes=24 << 20),
        cost_estimate=pl.CostEstimate(flops=10 ** 9, bytes_accessed=10 ** 7, transcendentals=0),
        name="inner_late" if late else "inner_early",
    )(table, own, live, *carried)


def outer_step(table, rim_lists, own, live, below, above, pair, part, edge):
    tile_dev, rows = live.shape
    ext = tile_dev + 2 * RIM
    listed = table.shape[0] - 2
    return pl.pallas_call(
        outer_kernel,
        out_shape=(jax.ShapeDtypeStruct((tile_dev, rows), f32), jax.ShapeDtypeStruct((3, tile_dev, rows), f32)),
        in_specs=[SMEM] * 2 + [VMEM] * 7,
        out_specs=(VMEM, VMEM),
        scratch_shapes=[
            pltpu.VMEM((8 * 4 * RIM, rows), f32),
            pltpu.VMEM((8 * 4 * RIM, rows), f32),
            pltpu.VMEM((4 * RIM, rows, rows), bf16),
            pltpu.VMEM((HALO_TILES, listed * rows, 2 * rows), f32),
            pltpu.VMEM((8 * 2 * RIM, rows), f32),
            pltpu.VMEM((8 * ext, rows), f32),
            pltpu.VMEM((ext, 16, rows), bf16),
            pltpu.VMEM((8 * tile_dev, rows), f32),
        ],
        compiler_params=pltpu.CompilerParams(vmem_limit_bytes=24 << 20),
        name="outer_step",
    )(table, rim_lists, own, live, below, above, pair, part, edge)


def per_device(coords, smooth, masses, owners, counts, neighbours):
    tile_dev, rows = smooth.shape
    regions = lax.axis_size("region")
    subs = lax.axis_size("sub")
    per_dest = tile_dev // regions
    listed = neighbours.shape[1]
    early = jnp.maximum(CHUNKS - 1 - lax.axis_index("sub"), 0).astype(jnp.int32)
    pairwise = regions <= 4 and regions & (regions - 1) == 0
    grouped = group_tiles(coords, smooth, masses, owners, regions, pairwise)
    me = lax.axis_index("region") if pairwise else jnp.int32(0)
    slot = jnp.arange(tile_dev, dtype=jnp.int32)
    scalars = jnp.where(slot == 0, me, jnp.where(slot == 1, early, 0))
    table = jnp.concatenate([neighbours.T, counts[None], scalars[None]], axis=0)
    if pairwise:
        live, ids, local = stage(table, grouped[0])
        blocks = [local]
        for k in range(1, regions):
            blocks.append(lax.ppermute(grouped[k], "region", [(i, i ^ k) for i in range(regions)]))
        own = jnp.stack(blocks)
    else:
        live, ids, _ = stage(table, grouped[0][0])
        own = lax.all_to_all(grouped[0], "region", 0, 0, tiled=True)
    by_field = own.reshape(regions, FIELDS, per_dest, rows)

    def rim(first):
        if pairwise:
            block = lax.dynamic_index_in_dim(by_field, me ^ (0 if first else regions - 1), 0, keepdims=False)
            block = block[:, :RIM] if first else block[:, per_dest - RIM:]
        else:
            blocks = RIM // per_dest
            block = by_field[:blocks] if first else by_field[regions - blocks:]
            block = jnp.swapaxes(block, 0, 1).reshape(FIELDS, RIM, rows)
        tiles = slice(0, RIM) if first else slice(tile_dev - RIM, tile_dev)
        block = jnp.concatenate([block[:4], (block[4] * live[tiles])[None]], axis=0).reshape(FIELDS * RIM, rows)
        return jnp.concatenate([block, ids[0 if first else 1]], axis=0)

    up = [(i, (i + 1) % subs) for i in range(subs)]
    down = [(j, i) for i, j in up]
    below = lax.ppermute(rim(False), "sub", up)
    carried = inner_density(table, own, live)
    above = lax.ppermute(rim(True), "sub", down)
    pair, part, _, _, edge = inner_density(table, own, live, carried)
    count = HALO_TILES * listed
    rim_lists = jnp.concatenate([below[FIELDS * RIM, :count], above[FIELDS * RIM, :count]]).astype(jnp.int32)
    return outer_step(table, rim_lists, own, live, below, above, pair, part, edge)


def solution(mesh):
    in_specs = (
        P(None, ("region", "sub"), None),
        P(("region", "sub"), None),
        P(("region", "sub"), None),
        P(("region", "sub")),
        P(("region", "sub")),
        P(("region", "sub"), None),
    )
    out_specs = (P(("region", "sub"), None), P(None, ("region", "sub"), None))
    return jax.shard_map(
        per_device, mesh=mesh, in_specs=in_specs, out_specs=out_specs, check_vma=False
    )
```

```python
import functools
import math

import jax
import jax.numpy as jnp
from jax import lax
from jax.experimental import pallas as pl
from jax.experimental.pallas import tpu as pltpu
from jax.sharding import PartitionSpec as P


HALO_TILES = 4
RIM = 2 * HALO_TILES
FIELDS = 5
CHUNKS = 4
EMPTY_LOG = -1024.0
LOG2E = 1.4426950408889634
kernel_scale = math.pi ** (-1.5)

f32, bf16 = jnp.float32, jnp.bfloat16
VMEM = pl.BlockSpec(memory_space=pltpu.VMEM)
SMEM = pl.BlockSpec(memory_space=pltpu.SMEM)


def group_kernel(pairwise, count, *refs):
    sources, outs = refs[:4], refs[4:4 + count]
    owners_ref, coords_ref, smooth_ref, masses_ref, block_ref, sems, out_sems = refs[4 + count:]
    targets = (owners_ref, coords_ref, smooth_ref, masses_ref)
    copies = [pltpu.make_async_copy(s, t, sems.at[i]) for i, (s, t) in enumerate(zip(sources, targets))]
    for copy in copies:
        copy.start()
    copies[0].wait()
    regions = block_ref.shape[0]
    per_dest = block_ref.shape[1] // FIELDS
    bits = per_dest.bit_length()
    per_word = 31 // bits
    seen = [jnp.int32(0)] * pl.cdiv(regions, per_word)
    me = lax.axis_index("region") if pairwise else 0
    places = []
    for n in range(owners_ref.shape[0]):
        d = owners_ref[n]
        word = d // per_word if len(seen) > 1 else 0
        shift = (d - word * per_word) * bits
        k = seen[0]
        for w in range(1, len(seen)):
            k = jnp.where(word == w, seen[w], k)
        k = (k >> shift) & ((1 << bits) - 1)
        step = jnp.int32(1) << shift
        seen = [s + (jnp.where(word == w, step, 0) if len(seen) > 1 else step) for w, s in enumerate(seen)]
        places.append((d ^ me if pairwise else d, k))
    for copy in copies[1:]:
        copy.wait()
    for n, (d, k) in enumerate(places):
        for c in range(3):
            block_ref[d, pl.ds(c * per_dest + k, 1)] = coords_ref[c, n:n + 1]
        block_ref[d, pl.ds(3 * per_dest + k, 1)] = smooth_ref[n:n + 1]
        block_ref[d, pl.ds(4 * per_dest + k, 1)] = masses_ref[n:n + 1]
    copies = [
        pltpu.make_async_copy(block_ref.at[k] if pairwise else block_ref, out, out_sems.at[k]) for k, out in enumerate(outs)
    ]
    for copy in copies:
        copy.start()
    for copy in copies:
        copy.wait()


def group_tiles(coords, smooth, masses, owners, regions, pairwise):
    tile_dev, rows = smooth.shape
    per_dest = tile_dev // regions
    block = (FIELDS * per_dest, rows)
    hbm = pl.BlockSpec(memory_space=pltpu.HBM)
    whole = (regions,) + block
    shapes = [block] * regions if pairwise else [whole]
    return pl.pallas_call(
        functools.partial(group_kernel, pairwise, len(shapes)),
        out_shape=[jax.ShapeDtypeStruct(shape, f32) for shape in shapes],
        in_specs=[hbm] * 4,
        out_specs=[hbm] * len(shapes),
        scratch_shapes=[pltpu.SMEM(owners.shape, jnp.int32)]
        + [pltpu.VMEM(a.shape, f32) for a in (coords, smooth, masses)]
        + [pltpu.VMEM(whole, f32), pltpu.SemaphoreType.DMA((4,)), pltpu.SemaphoreType.DMA((len(shapes),))],
        name="group_tiles",
    )(owners, coords, smooth, masses)


def stage_kernel(table_ref, local_ref, live_ref, ids_ref, here_ref):
    tile_dev, rows = live_ref.shape
    listed = table_ref.shape[0] - 2
    lane = lax.broadcasted_iota(jnp.int32, (8, rows), 1)
    row = lax.broadcasted_iota(jnp.int32, (8, rows), 0)
    for t in range(0, tile_dev, 8):
        limit = jnp.full((8, rows), table_ref[listed, t])
        for i in range(1, 8):
            limit = jnp.where(row == i, table_ref[listed, t + i], limit)
        live_ref[t:t + 8] = (lane < limit).astype(f32)
    for side, start in enumerate((0, tile_dev - HALO_TILES)):
        ids = jnp.zeros((8, rows), f32)
        for i in range(HALO_TILES):
            for n in range(listed):
                ids = jnp.where(lane == i * listed + n, table_ref[n, start + i].astype(f32), ids)
        ids_ref[side] = ids
    here_ref[...] = local_ref[...]


def stage(table, local):
    tile_dev, rows = table.shape[1], local.shape[-1]
    return pl.pallas_call(
        stage_kernel,
        out_shape=(
            jax.ShapeDtypeStruct((tile_dev, rows), f32),
            jax.ShapeDtypeStruct((2, 8, rows), f32),
            jax.ShapeDtypeStruct(local.shape, f32),
        ),
        in_specs=[SMEM, VMEM],
        out_specs=(VMEM,) * 3,
        compiler_params=pltpu.CompilerParams(vmem_limit_bytes=4 << 20),
        name="stage",
    )(table, local)


def parts_of(x, count):
    parts = []
    for _ in range(count):
        part = x.astype(bf16).astype(f32)
        parts.append(part)
        x = x - part
    return parts


def dot(a, b):
    return jnp.dot(a, b, preferred_element_type=f32)


def own_field(table_ref, own_ref, live_ref, f):
    tile_dev = live_ref.shape[0]
    regions, per_dest = own_ref.shape[0], tile_dev // own_ref.shape[0]
    rows = pl.ds(f * per_dest, per_dest)
    value = jnp.concatenate([own_ref[table_ref[table_ref.shape[0] - 1, 0] ^ r, rows] for r in range(regions)], axis=0)
    return value * live_ref[...] if f == 4 else value


def field_terms(fields):
    pos, h, mass = fields[:3], fields[3], fields[4]
    inverse_sq = 1.0 / (h * h)
    return pos, mass > 0, mass, inverse_sq, kernel_scale * inverse_sq / h


def put_rows(ref, values):
    count = values[0].shape[0]
    for k, value in enumerate(values):
        ref[k * count:(k + 1) * count] = value


def put_features(pos, live, mass, inverse_sq, partner_ref, mine_ref):
    c = inverse_sq * LOG2E
    square = pos[0] * pos[0] + pos[1] * pos[1] + pos[2] * pos[2]
    log_mass = jnp.where(live, jnp.log2(jnp.where(live, mass, 1.0)), EMPTY_LOG)
    one, zero = jnp.ones_like(c), jnp.zeros_like(c)
    put_rows(partner_ref, pos + [square, log_mass, one, zero, zero])
    put_rows(mine_ref, [2 * c * x for x in pos] + [-c, one, -c * square, zero, zero])


def tile_of(ref, e):
    return ref[pl.ds(e, 8, stride=ref.shape[0] // 8)]


def turned(ref, e):
    p1, p2, p3 = parts_of(tile_of(ref, e), 3)
    block = jnp.concatenate([p1, p1, p2, p1, p3, p2], axis=0).astype(bf16)
    fill = jnp.zeros((block.shape[1] - block.shape[0], block.shape[1]), bf16)
    return jnp.concatenate([block, fill], axis=0).T


def pair_weights(ref, e):
    def one_tile(e):
        o1, o2, o3 = parts_of(tile_of(ref, e), 3)
        block = jnp.concatenate([o1, o2, o1, o3, o1, o2], axis=0).astype(bf16)
        return jnp.concatenate([block, jnp.zeros((block.shape[1] - block.shape[0], block.shape[1]), bf16)], axis=0)

    first, second = one_tile(e), one_tile(e + 1)
    blank = jnp.zeros_like(first)
    return jnp.concatenate(
        [jnp.concatenate([first, blank], axis=1), jnp.concatenate([blank, second], axis=1)], axis=0
    )


def density_pair(turned_ref, own, partners, part_ref, at, store):
    rows = own.shape[1] // 2
    total = None
    for n, (e0, e1) in enumerate(partners):
        t = jnp.exp2(dot(jnp.concatenate([turned_ref[e0], turned_ref[e1]], axis=1), own))
        if store is not None:
            store[n * rows:(n + 1) * rows] = t
        part = jnp.sum(t.reshape(rows // 8, 8, 2 * rows), axis=0)
        total = part if total is None else total + part
    part_ref[pl.ds(at, 8)] = total[:, :rows]
    part_ref[pl.ds(at + 8, 8)] = total[:, rows:]


def pressure(raw, live):
    return jnp.where(live, jnp.exp2(jnp.log2(jnp.where(live, raw, 1.0)) * (-1.0 / 3.0)), 0.0)


def put_coefficients(ref, pos, q):
    put_rows(ref, [jnp.ones_like(q)] + pos + [q] + [q * x for x in pos])


def narrow(narrow_ref, ref, e):
    narrow_ref[e] = jnp.concatenate(parts_of(tile_of(ref, e), 2), axis=0).astype(bf16)


def force_pair(narrow_ref, partners, pair, out_ref, at):
    rows = pair.shape[1] // 2
    total = None
    for n, (e0, e1) in enumerate(partners):
        left = jnp.concatenate([narrow_ref[e0], narrow_ref[e1]], axis=0)
        w = pair[n * rows:(n + 1) * rows]
        high = w.astype(bf16)
        part = dot(left, high) + dot(left, (w - high.astype(f32)).astype(bf16))
        total = part if total is None else total + part
    out_ref[pl.ds(at, 8)] = total[:8, :rows] + total[8:16, :rows]
    out_ref[pl.ds(at + 8, 8)] = total[16:24, rows:] + total[24:, rows:]


def inner_kernel(late, table_ref, own_ref, live_ref, *refs):
    if late:
        refs, (edge_ref, out_ref, partner_ref, mine_ref, coef_ref, narrow_ref) = refs[:-6], refs[-6:]
    else:
        refs, (partner_ref, mine_ref) = refs[:-2], refs[-2:]
    pair_ref, part_ref, turned_ref, weights_ref = refs[-4:]
    tile_dev = live_ref.shape[0]
    listed = table_ref.shape[0] - 2
    chunk = pair_ref.shape[0] // CHUNKS
    ahead = 2 * chunk + 2 * HALO_TILES

    def turn(t):
        turned_ref[t] = turned(partner_ref, t)

    def weigh(p):
        weights_ref[p] = pair_weights(mine_ref, HALO_TILES + 2 * p)

    def features():
        pos, live, mass, inverse_sq, _ = field_terms(
            [own_field(table_ref, own_ref, live_ref, f) for f in range(FIELDS)]
        )
        put_features(pos, live, mass, inverse_sq, partner_ref, mine_ref)

    def do_chunk(c, more=True):
        for i in range(chunk):
            t = HALO_TILES + 2 * (c * chunk + i)
            partners = [(table_ref[n, t] - HALO_TILES, table_ref[n, t + 1] - HALO_TILES) for n in range(listed)]
            p = c * chunk + i
            density_pair(turned_ref, weights_ref[p], partners, part_ref, 16 * p, pair_ref.at[p])
        if more:
            for i in range(2 * chunk):
                turn(c * 2 * chunk + ahead + i)
            for i in range(chunk):
                weigh((c + 1) * chunk + i)

    early = table_ref[listed + 1, 1]

    def begin():
        features()
        for t in range(ahead):
            turn(t)
        for p in range(chunk):
            weigh(p)

    if late:
        pl.when(early > 0)(features)
        pl.when(early == 0)(begin)
        pl.loop(early, CHUNKS - 1)(do_chunk)
        do_chunk(CHUNKS - 1, False)
        edge_ref[:RIM] = turned_ref[:RIM]
        edge_ref[RIM:] = turned_ref[tile_dev - RIM:]
        pos, live, _, _, norm = field_terms([own_field(table_ref, own_ref, live_ref, f) for f in range(FIELDS)])
        inside = slice(HALO_TILES, tile_dev - HALO_TILES)
        raw = sum(part_ref[pl.ds(k, tile_dev - RIM, stride=8)] for k in range(8)) * norm[inside]
        blank = jnp.zeros((HALO_TILES, live_ref.shape[1]), f32)
        put_coefficients(coef_ref, pos, jnp.concatenate([blank, pressure(raw, live[inside]), blank], axis=0))

        @pl.loop(HALO_TILES, tile_dev - HALO_TILES, unroll=8)
        def _(t):
            narrow(narrow_ref, coef_ref, t)

        half = HALO_TILES // 2

        @pl.loop(half, pair_ref.shape[0] - half, unroll=8)
        def _(p):
            t = HALO_TILES + 2 * p
            partners = [(table_ref[n, t] - HALO_TILES, table_ref[n, t + 1] - HALO_TILES) for n in range(listed)]
            force_pair(narrow_ref, partners, pair_ref.at[p], out_ref, 8 * t)
    else:

        @pl.when(early > 0)
        def _():
            begin()
            pl.loop(0, early)(do_chunk)


def outer_kernel(
    table_ref, rim_lists_ref, own_ref, live_ref, below_ref, above_ref, pair_ref, part_ref, edge_ref, inner_out_ref,
    density_ref, accel_ref, partner_ref, mine_ref, turned_ref, weights_ref, rim_pair_ref, rim_part_ref, coef_ref,
    coefb_ref, out_ref,
):
    tile_dev, rows = live_ref.shape
    ext = tile_dev + 2 * RIM
    listed = table_ref.shape[0] - 2
    fields = [
        jnp.concatenate(
            [
                below_ref[f * RIM:(f + 1) * RIM],
                own_field(table_ref, own_ref, live_ref, f),
                above_ref[f * RIM:(f + 1) * RIM],
            ],
            axis=0,
        )
        for f in range(FIELDS)
    ]
    pos, live, mass, inverse_sq, norm = field_terms(fields)
    rim_pairs = RIM

    def rims(x):
        return jnp.concatenate([x[:2 * RIM], x[tile_dev:]], axis=0)

    put_features([rims(x) for x in pos], rims(live), rims(mass), rims(inverse_sq), partner_ref, mine_ref)
    for e in range(RIM):
        turned_ref[e] = turned(partner_ref, e)
        turned_ref[RIM + e] = edge_ref[e]
        turned_ref[2 * RIM + e] = edge_ref[RIM + e]
        turned_ref[3 * RIM + e] = turned(partner_ref, 3 * RIM + e)
    for r in range(rim_pairs):
        weights_ref[r] = pair_weights(mine_ref, HALO_TILES + 2 * r + (RIM if 2 * r >= rim_pairs else 0))

    outer = RIM + HALO_TILES
    inner_raw = sum(part_ref[pl.ds(k, tile_dev - RIM, stride=8)] for k in range(8)) * norm[outer:ext - outer]
    for r in range(rim_pairs):
        first = 2 * r * listed
        partners = [(rim_lists_ref[first + n], rim_lists_ref[first + listed + n]) for n in range(listed)]
        density_pair(turned_ref, weights_ref[r], partners, rim_part_ref, 16 * r, rim_pair_ref.at[r])

    rim_raw = sum(rim_part_ref[pl.ds(k, 2 * RIM, stride=8)] for k in range(8))
    raw = jnp.concatenate(
        [rim_raw[:RIM] * norm[HALO_TILES:outer], inner_raw, rim_raw[RIM:] * norm[ext - outer:ext - HALO_TILES]], axis=0
    )
    q = pressure(raw, live[HALO_TILES:ext - HALO_TILES])
    pad = jnp.zeros((HALO_TILES, rows), f32)
    q = jnp.concatenate([pad, q, pad], axis=0)
    put_coefficients(coef_ref, pos, q)
    for e in range(2 * RIM):
        narrow(coefb_ref, coef_ref, HALO_TILES + e)
        narrow(coefb_ref, coef_ref, ext - HALO_TILES - 2 * RIM + e)
    half = HALO_TILES // 2
    count = pair_ref.shape[0]

    def edge_force(t, pair):
        partners = [(table_ref[n, t] + HALO_TILES, table_ref[n, t + 1] + HALO_TILES) for n in range(listed)]
        force_pair(coefb_ref, partners, pair, out_ref, 8 * t)

    for i in range(half):
        edge_force(2 * i, rim_pair_ref.at[half + i])
        edge_force(HALO_TILES + 2 * i, pair_ref.at[i])
        edge_force(tile_dev - RIM + 2 * i, pair_ref.at[count - half + i])
        edge_force(tile_dev - HALO_TILES + 2 * i, rim_pair_ref.at[2 * half + i])

    mine = slice(RIM, RIM + tile_dev)
    own_live = live_ref[...]
    density_ref[...] = raw[HALO_TILES:HALO_TILES + tile_dev] * own_live
    q_own = q[mine]
    scale = own_live * (2.0 * inverse_sq[mine] * norm[mine])
    sums = [
        jnp.concatenate(
            [
                out_ref[pl.ds(k, RIM, stride=8)],
                inner_out_ref[pl.ds(8 * RIM + k, tile_dev - 2 * RIM, stride=8)],
                out_ref[pl.ds(8 * (tile_dev - RIM) + k, RIM, stride=8)],
            ],
            axis=0,
        )
        for k in range(8)
    ]
    for c in range(3):
        x = pos[c][mine]
        accel_ref[c] = scale * (q_own * (x * sums[0] - sums[1 + c]) + (x * sums[4] - sums[5 + c]))


def inner_density(table, own, live, carried=()):
    tile_dev, rows = live.shape
    listed = table.shape[0] - 2
    count = (tile_dev - RIM) // 2
    late = len(carried) > 0
    shapes = [
        jax.ShapeDtypeStruct((count, listed * rows, 2 * rows), f32),
        jax.ShapeDtypeStruct((16 * count, rows), f32),
        jax.ShapeDtypeStruct((tile_dev, rows, rows), bf16),
        jax.ShapeDtypeStruct((count, 2 * rows, 2 * rows), bf16),
    ]
    features = [pltpu.VMEM((8 * tile_dev, rows), f32), pltpu.VMEM((8 * tile_dev, rows), f32)]
    edges, forces = [], []
    if late:
        edges = [jax.ShapeDtypeStruct((2 * RIM, rows, rows), bf16), jax.ShapeDtypeStruct((8 * tile_dev, rows), f32)]
        forces = [pltpu.VMEM((8 * tile_dev, rows), f32), pltpu.VMEM((tile_dev, 16, rows), bf16)]
    return pl.pallas_call(
        functools.partial(inner_kernel, late),
        out_shape=shapes + edges,
        in_specs=[SMEM] + [VMEM] * (2 + len(carried)),
        out_specs=[VMEM] * len(shapes + edges),
        input_output_aliases={3 + i: i for i in range(len(carried))},
        scratch_shapes=features + forces,
        compiler_params=pltpu.CompilerParams(vmem_limit_bytes=24 << 20),
        cost_estimate=pl.CostEstimate(flops=10 ** 9, bytes_accessed=10 ** 7, transcendentals=0),
        name="inner_late" if late else "inner_early",
    )(table, own, live, *carried)


def outer_step(table, rim_lists, own, live, below, above, pair, part, edge, inner_out):
    tile_dev, rows = live.shape
    ext = tile_dev + 2 * RIM
    listed = table.shape[0] - 2
    return pl.pallas_call(
        outer_kernel,
        out_shape=(jax.ShapeDtypeStruct((tile_dev, rows), f32), jax.ShapeDtypeStruct((3, tile_dev, rows), f32)),
        in_specs=[SMEM] * 2 + [VMEM] * 8,
        out_specs=(VMEM, VMEM),
        scratch_shapes=[
            pltpu.VMEM((8 * 4 * RIM, rows), f32),
            pltpu.VMEM((8 * 4 * RIM, rows), f32),
            pltpu.VMEM((4 * RIM, rows, rows), bf16),
            pltpu.VMEM((RIM, 2 * rows, 2 * rows), bf16),
            pltpu.VMEM((RIM, listed * rows, 2 * rows), f32),
            pltpu.VMEM((8 * 2 * RIM, rows), f32),
            pltpu.VMEM((8 * ext, rows), f32),
            pltpu.VMEM((ext, 16, rows), bf16),
            pltpu.VMEM((8 * tile_dev, rows), f32),
        ],
        compiler_params=pltpu.CompilerParams(vmem_limit_bytes=24 << 20),
        name="outer_step",
    )(table, rim_lists, own, live, below, above, pair, part, edge, inner_out)


def per_device(coords, smooth, masses, owners, counts, neighbours):
    tile_dev, rows = smooth.shape
    regions = lax.axis_size("region")
    subs = lax.axis_size("sub")
    per_dest = tile_dev // regions
    listed = neighbours.shape[1]
    early = jnp.maximum(CHUNKS - 1 - 2 * lax.axis_index("sub"), 0).astype(jnp.int32)
    pairwise = regions <= 4 and regions & (regions - 1) == 0
    grouped = group_tiles(coords, smooth, masses, owners, regions, pairwise)
    me = lax.axis_index("region") if pairwise else jnp.int32(0)
    slot = jnp.arange(tile_dev, dtype=jnp.int32)
    scalars = jnp.where(slot == 0, me, jnp.where(slot == 1, early, 0))
    table = jnp.concatenate([neighbours.T, counts[None], scalars[None]], axis=0)
    if pairwise:
        live, ids, local = stage(table, grouped[0])
        blocks = [local]
        for k in range(1, regions):
            blocks.append(lax.ppermute(grouped[k], "region", [(i, i ^ k) for i in range(regions)]))
        own = jnp.stack(blocks)
    else:
        live, ids, _ = stage(table, grouped[0][0])
        own = lax.all_to_all(grouped[0], "region", 0, 0, tiled=True)
    by_field = own.reshape(regions, FIELDS, per_dest, rows)

    def rim(first):
        if pairwise:
            block = lax.dynamic_index_in_dim(by_field, me ^ (0 if first else regions - 1), 0, keepdims=False)
            block = block[:, :RIM] if first else block[:, per_dest - RIM:]
        else:
            blocks = RIM // per_dest
            block = by_field[:blocks] if first else by_field[regions - blocks:]
            block = jnp.swapaxes(block, 0, 1).reshape(FIELDS, RIM, rows)
        tiles = slice(0, RIM) if first else slice(tile_dev - RIM, tile_dev)
        block = jnp.concatenate([block[:4], (block[4] * live[tiles])[None]], axis=0).reshape(FIELDS * RIM, rows)
        return jnp.concatenate([block, ids[0 if first else 1]], axis=0)

    up = [(i, (i + 1) % subs) for i in range(subs)]
    down = [(j, i) for i, j in up]
    below = lax.ppermute(rim(False), "sub", up)
    carried = inner_density(table, own, live)
    above = lax.ppermute(rim(True), "sub", down)
    pair, part, _, _, edge, inner_out = inner_density(table, own, live, carried)
    count = HALO_TILES * listed
    places = [
        below[FIELDS * RIM, :count] + (HALO_TILES - tile_dev),
        ids[0, 0, :count] + HALO_TILES,
        ids[1, 0, :count] + (HALO_TILES - tile_dev + 2 * RIM),
        above[FIELDS * RIM, :count] + (HALO_TILES + 2 * RIM),
    ]
    rim_lists = jnp.concatenate(places).astype(jnp.int32)
    return outer_step(table, rim_lists, own, live, below, above, pair, part, edge, inner_out)


def solution(mesh):
    in_specs = (
        P(None, ("region", "sub"), None),
        P(("region", "sub"), None),
        P(("region", "sub"), None),
        P(("region", "sub")),
        P(("region", "sub")),
        P(("region", "sub"), None),
    )
    out_specs = (P(("region", "sub"), None), P(None, ("region", "sub"), None))
    return jax.shard_map(
        per_device, mesh=mesh, in_specs=in_specs, out_specs=out_specs, check_vma=False
    )
```

```python
import functools
import math

import jax
import jax.numpy as jnp
from jax import lax
from jax.experimental import pallas as pl
from jax.experimental.pallas import tpu as pltpu
from jax.sharding import PartitionSpec as P


HALO_TILES = 4
RIM = 2 * HALO_TILES
FIELDS = 5
CHUNKS = 4
EMPTY_LOG = -1024.0
LOG2E = 1.4426950408889634
kernel_scale = math.pi ** (-1.5)

f32, bf16 = jnp.float32, jnp.bfloat16
VMEM = pl.BlockSpec(memory_space=pltpu.VMEM)
SMEM = pl.BlockSpec(memory_space=pltpu.SMEM)
ANY = pl.BlockSpec(memory_space=pl.ANY)


def group_kernel(pairwise, count, *refs):
    sources, outs = refs[:4], refs[4:4 + count]
    owners_ref, coords_ref, smooth_ref, masses_ref, block_ref, sems, out_sems = refs[4 + count:]
    targets = (owners_ref, coords_ref, smooth_ref, masses_ref)
    copies = [pltpu.make_async_copy(s, t, sems.at[i]) for i, (s, t) in enumerate(zip(sources, targets))]
    for copy in copies:
        copy.start()
    copies[0].wait()
    regions = block_ref.shape[0]
    per_dest = block_ref.shape[1] // FIELDS
    bits = per_dest.bit_length()
    per_word = 31 // bits
    seen = [jnp.int32(0)] * pl.cdiv(regions, per_word)
    me = lax.axis_index("region") if pairwise else 0
    places = []
    for n in range(owners_ref.shape[0]):
        d = owners_ref[n]
        word = d // per_word if len(seen) > 1 else 0
        shift = (d - word * per_word) * bits
        k = seen[0]
        for w in range(1, len(seen)):
            k = jnp.where(word == w, seen[w], k)
        k = (k >> shift) & ((1 << bits) - 1)
        step = jnp.int32(1) << shift
        seen = [s + (jnp.where(word == w, step, 0) if len(seen) > 1 else step) for w, s in enumerate(seen)]
        places.append((d ^ me if pairwise else d, k))
    for copy in copies[1:]:
        copy.wait()
    for n, (d, k) in enumerate(places):
        for c in range(3):
            block_ref[d, pl.ds(c * per_dest + k, 1)] = coords_ref[c, n:n + 1]
        block_ref[d, pl.ds(3 * per_dest + k, 1)] = smooth_ref[n:n + 1]
        block_ref[d, pl.ds(4 * per_dest + k, 1)] = masses_ref[n:n + 1]
    copies = [
        pltpu.make_async_copy(block_ref.at[k] if pairwise else block_ref, out, out_sems.at[k]) for k, out in enumerate(outs)
    ]
    for copy in copies:
        copy.start()
    for copy in copies:
        copy.wait()


def group_tiles(coords, smooth, masses, owners, regions, pairwise):
    tile_dev, rows = smooth.shape
    per_dest = tile_dev // regions
    block = (FIELDS * per_dest, rows)
    hbm = pl.BlockSpec(memory_space=pltpu.HBM)
    whole = (regions,) + block
    shapes = [block] * regions if pairwise else [whole]
    return pl.pallas_call(
        functools.partial(group_kernel, pairwise, len(shapes)),
        out_shape=[jax.ShapeDtypeStruct(shape, f32) for shape in shapes],
        in_specs=[hbm] * 4,
        out_specs=[hbm] * len(shapes),
        scratch_shapes=[pltpu.SMEM(owners.shape, jnp.int32)]
        + [pltpu.VMEM(a.shape, f32) for a in (coords, smooth, masses)]
        + [pltpu.VMEM(whole, f32), pltpu.SemaphoreType.DMA((4,)), pltpu.SemaphoreType.DMA((len(shapes),))],
        name="group_tiles",
    )(owners, coords, smooth, masses)


def stage_kernel(table_ref, local_ref, live_ref, ids_ref, here_ref):
    tile_dev, rows = live_ref.shape
    listed = table_ref.shape[0] - 1
    lane = lax.broadcasted_iota(jnp.int32, (8, rows), 1)
    row = lax.broadcasted_iota(jnp.int32, (8, rows), 0)
    for t in range(0, tile_dev, 8):
        limit = jnp.full((8, rows), table_ref[listed, t])
        for i in range(1, 8):
            limit = jnp.where(row == i, table_ref[listed, t + i], limit)
        live_ref[t:t + 8] = (lane < limit).astype(f32)
    for side, start in enumerate((0, tile_dev - HALO_TILES)):
        ids = jnp.zeros((8, rows), f32)
        for i in range(HALO_TILES):
            for n in range(listed):
                ids = jnp.where(lane == i * listed + n, table_ref[n, start + i].astype(f32), ids)
        ids_ref[side] = ids
    here_ref[...] = local_ref[...]


def stage(table, local):
    tile_dev, rows = table.shape[1], local.shape[-1]
    return pl.pallas_call(
        stage_kernel,
        out_shape=(
            jax.ShapeDtypeStruct((tile_dev, rows), f32),
            jax.ShapeDtypeStruct((2, 8, rows), f32),
            jax.ShapeDtypeStruct(local.shape, f32),
        ),
        in_specs=[SMEM, VMEM],
        out_specs=(VMEM,) * 3,
        compiler_params=pltpu.CompilerParams(vmem_limit_bytes=4 << 20),
        name="stage",
    )(table, local)


def parts_of(x, count):
    parts = []
    for _ in range(count):
        part = x.astype(bf16).astype(f32)
        parts.append(part)
        x = x - part
    return parts


def dot(a, b):
    return jnp.dot(a, b, preferred_element_type=f32)


def own_field(pairwise, own_ref, live_ref, f):
    tile_dev = live_ref.shape[0]
    regions, per_dest = own_ref.shape[0], tile_dev // own_ref.shape[0]
    rows = pl.ds(f * per_dest, per_dest)
    me = lax.axis_index("region") if pairwise else 0
    value = jnp.concatenate([own_ref[me ^ r, rows] for r in range(regions)], axis=0)
    return value * live_ref[...] if f == 4 else value


def field_terms(fields):
    pos, h, mass = fields[:3], fields[3], fields[4]
    inverse_sq = 1.0 / (h * h)
    return pos, mass > 0, mass, inverse_sq, kernel_scale * inverse_sq / h


def put_rows(ref, values):
    count = values[0].shape[0]
    for k, value in enumerate(values):
        ref[k * count:(k + 1) * count] = value


def put_features(pos, live, mass, inverse_sq, partner_ref, mine_ref):
    c = inverse_sq * LOG2E
    square = pos[0] * pos[0] + pos[1] * pos[1] + pos[2] * pos[2]
    log_mass = jnp.where(live, jnp.log2(jnp.where(live, mass, 1.0)), EMPTY_LOG)
    one, zero = jnp.ones_like(c), jnp.zeros_like(c)
    put_rows(partner_ref, pos + [square, log_mass, one, zero, zero])
    put_rows(mine_ref, [2 * c * x for x in pos] + [-c, one, -c * square, zero, zero])


def tile_of(ref, e):
    return ref[pl.ds(e, 8, stride=ref.shape[0] // 8)]


def turned(ref, e):
    p1, p2, p3 = parts_of(tile_of(ref, e), 3)
    block = jnp.concatenate([p1, p1, p2, p1, p3, p2], axis=0).astype(bf16)
    fill = jnp.zeros((block.shape[1] - block.shape[0], block.shape[1]), bf16)
    return jnp.concatenate([block, fill], axis=0).T


def pair_weights(ref, e):
    def one_tile(e):
        o1, o2, o3 = parts_of(tile_of(ref, e), 3)
        block = jnp.concatenate([o1, o2, o1, o3, o1, o2], axis=0).astype(bf16)
        return jnp.concatenate([block, jnp.zeros((block.shape[1] - block.shape[0], block.shape[1]), bf16)], axis=0)

    first, second = one_tile(e), one_tile(e + 1)
    blank = jnp.zeros_like(first)
    return jnp.concatenate(
        [jnp.concatenate([first, blank], axis=1), jnp.concatenate([blank, second], axis=1)], axis=0
    )


def density_pair(turned_ref, own, partners, part_ref, at, store):
    rows = own.shape[1] // 2
    total = None
    for n, (e0, e1) in enumerate(partners):
        t = jnp.exp2(dot(jnp.concatenate([turned_ref[e0], turned_ref[e1]], axis=1), own))
        if store is not None:
            store[n * rows:(n + 1) * rows] = t
        part = jnp.sum(t.reshape(rows // 8, 8, 2 * rows), axis=0)
        total = part if total is None else total + part
    part_ref[pl.ds(at, 8)] = total[:, :rows]
    part_ref[pl.ds(at + 8, 8)] = total[:, rows:]


def pressure(raw, live):
    return jnp.where(live, jnp.exp2(jnp.log2(jnp.where(live, raw, 1.0)) * (-1.0 / 3.0)), 0.0)


def put_coefficients(ref, pos, q):
    put_rows(ref, [jnp.ones_like(q)] + pos + [q] + [q * x for x in pos])


def narrow(narrow_ref, ref, e):
    narrow_ref[e] = jnp.concatenate(parts_of(tile_of(ref, e), 2), axis=0).astype(bf16)


def force_pair(narrow_ref, partners, pair, out_ref, at):
    rows = pair.shape[1] // 2
    total = None
    for n, (e0, e1) in enumerate(partners):
        left = jnp.concatenate([narrow_ref[e0], narrow_ref[e1]], axis=0)
        w = pair[n * rows:(n + 1) * rows]
        high = w.astype(bf16)
        part = dot(left, high) + dot(left, (w - high.astype(f32)).astype(bf16))
        total = part if total is None else total + part
    out_ref[pl.ds(at, 8)] = total[:8, :rows] + total[8:16, :rows]
    out_ref[pl.ds(at + 8, 8)] = total[16:24, rows:] + total[24:, rows:]


def inner_kernel(late, pairwise, table_in_ref, own_ref, live_ref, *refs):
    refs, (table_ref, table_sem) = refs[:-2], refs[-2:]
    table_copy = pltpu.make_async_copy(table_in_ref, table_ref, table_sem.at[0])
    if late:
        refs, (edge_ref, out_ref, partner_ref, mine_ref, coef_ref, narrow_ref) = refs[:-6], refs[-6:]
    else:
        refs, (partner_ref, mine_ref) = refs[:-2], refs[-2:]
    pair_ref, part_ref, turned_ref, weights_ref = refs[-4:]
    tile_dev = live_ref.shape[0]
    listed = table_ref.shape[0] - 1
    chunk = pair_ref.shape[0] // CHUNKS
    ahead = 2 * chunk + 2 * HALO_TILES

    def turn(t):
        turned_ref[t] = turned(partner_ref, t)

    def weigh(p):
        weights_ref[p] = pair_weights(mine_ref, HALO_TILES + 2 * p)

    def features():
        pos, live, mass, inverse_sq, _ = field_terms([own_field(pairwise, own_ref, live_ref, f) for f in range(FIELDS)])
        put_features(pos, live, mass, inverse_sq, partner_ref, mine_ref)

    def do_chunk(c, more=True):
        for i in range(chunk):
            t = HALO_TILES + 2 * (c * chunk + i)
            partners = [(table_ref[n, t] - HALO_TILES, table_ref[n, t + 1] - HALO_TILES) for n in range(listed)]
            p = c * chunk + i
            density_pair(turned_ref, weights_ref[p], partners, part_ref, 16 * p, pair_ref.at[p])
        if more:
            for i in range(2 * chunk):
                turn(c * 2 * chunk + ahead + i)
            for i in range(chunk):
                weigh((c + 1) * chunk + i)

    early = jnp.maximum(CHUNKS - 1 - 2 * lax.axis_index("sub"), 0)

    def begin():
        for t in range(ahead):
            turn(t)
        for p in range(chunk):
            weigh(p)

    if late:
        table_copy.start()
        features()
        pl.when(early == 0)(begin)
        table_copy.wait()
        pl.loop(early, CHUNKS - 1)(do_chunk)
        do_chunk(CHUNKS - 1, False)
        edge_ref[:RIM] = turned_ref[:RIM]
        edge_ref[RIM:] = turned_ref[tile_dev - RIM:]
        pos, live, _, _, norm = field_terms([own_field(pairwise, own_ref, live_ref, f) for f in range(FIELDS)])
        inside = slice(HALO_TILES, tile_dev - HALO_TILES)
        raw = sum(part_ref[pl.ds(k, tile_dev - RIM, stride=8)] for k in range(8)) * norm[inside]
        blank = jnp.zeros((HALO_TILES, live_ref.shape[1]), f32)
        put_coefficients(coef_ref, pos, jnp.concatenate([blank, pressure(raw, live[inside]), blank], axis=0))

        @pl.loop(HALO_TILES, tile_dev - HALO_TILES, unroll=8)
        def _(t):
            narrow(narrow_ref, coef_ref, t)

        half = HALO_TILES // 2

        @pl.loop(half, pair_ref.shape[0] - half, unroll=8)
        def _(p):
            t = HALO_TILES + 2 * p
            partners = [(table_ref[n, t] - HALO_TILES, table_ref[n, t + 1] - HALO_TILES) for n in range(listed)]
            force_pair(narrow_ref, partners, pair_ref.at[p], out_ref, 8 * t)
    else:

        @pl.when(early > 0)
        def _():
            table_copy.start()
            features()
            begin()
            table_copy.wait()
            pl.loop(0, early)(do_chunk)


def outer_kernel(
    pairwise, table_in_ref, rim_lists_in_ref, own_ref, live_ref, below_ref, above_ref, pair_ref, part_ref, edge_ref, inner_out_ref,
    density_ref, accel_ref, partner_ref, mine_ref, turned_ref, weights_ref, rim_pair_ref, rim_part_ref, coef_ref,
    coefb_ref, out_ref, table_ref, rim_lists_ref, sems,
):
    copies = [
        pltpu.make_async_copy(table_in_ref, table_ref, sems.at[0]),
        pltpu.make_async_copy(rim_lists_in_ref, rim_lists_ref, sems.at[1]),
    ]
    for copy in copies:
        copy.start()
    tile_dev, rows = live_ref.shape
    ext = tile_dev + 2 * RIM
    listed = table_ref.shape[0] - 1
    fields = [
        jnp.concatenate(
            [
                below_ref[f * RIM:(f + 1) * RIM],
                own_field(pairwise, own_ref, live_ref, f),
                above_ref[f * RIM:(f + 1) * RIM],
            ],
            axis=0,
        )
        for f in range(FIELDS)
    ]
    pos, live, mass, inverse_sq, norm = field_terms(fields)
    rim_pairs = RIM

    def rims(x):
        return jnp.concatenate([x[:2 * RIM], x[tile_dev:]], axis=0)

    put_features([rims(x) for x in pos], rims(live), rims(mass), rims(inverse_sq), partner_ref, mine_ref)
    for e in range(RIM):
        turned_ref[e] = turned(partner_ref, e)
        turned_ref[RIM + e] = edge_ref[e]
        turned_ref[2 * RIM + e] = edge_ref[RIM + e]
        turned_ref[3 * RIM + e] = turned(partner_ref, 3 * RIM + e)
    for r in range(rim_pairs):
        weights_ref[r] = pair_weights(mine_ref, HALO_TILES + 2 * r + (RIM if 2 * r >= rim_pairs else 0))

    outer = RIM + HALO_TILES
    inner_raw = sum(part_ref[pl.ds(k, tile_dev - RIM, stride=8)] for k in range(8)) * norm[outer:ext - outer]
    for copy in copies:
        copy.wait()
    for r in range(rim_pairs):
        first = 2 * r * listed
        partners = [(rim_lists_ref[first + n], rim_lists_ref[first + listed + n]) for n in range(listed)]
        density_pair(turned_ref, weights_ref[r], partners, rim_part_ref, 16 * r, rim_pair_ref.at[r])

    rim_raw = sum(rim_part_ref[pl.ds(k, 2 * RIM, stride=8)] for k in range(8))
    raw = jnp.concatenate(
        [rim_raw[:RIM] * norm[HALO_TILES:outer], inner_raw, rim_raw[RIM:] * norm[ext - outer:ext - HALO_TILES]], axis=0
    )
    q = pressure(raw, live[HALO_TILES:ext - HALO_TILES])
    pad = jnp.zeros((HALO_TILES, rows), f32)
    q = jnp.concatenate([pad, q, pad], axis=0)
    put_coefficients(coef_ref, pos, q)
    for e in range(2 * RIM):
        narrow(coefb_ref, coef_ref, HALO_TILES + e)
        narrow(coefb_ref, coef_ref, ext - HALO_TILES - 2 * RIM + e)
    half = HALO_TILES // 2
    count = pair_ref.shape[0]

    def edge_force(t, pair):
        partners = [(table_ref[n, t] + HALO_TILES, table_ref[n, t + 1] + HALO_TILES) for n in range(listed)]
        force_pair(coefb_ref, partners, pair, out_ref, 8 * t)

    for i in range(half):
        edge_force(2 * i, rim_pair_ref.at[half + i])
        edge_force(HALO_TILES + 2 * i, pair_ref.at[i])
        edge_force(tile_dev - RIM + 2 * i, pair_ref.at[count - half + i])
        edge_force(tile_dev - HALO_TILES + 2 * i, rim_pair_ref.at[2 * half + i])

    mine = slice(RIM, RIM + tile_dev)
    own_live = live_ref[...]
    density_ref[...] = raw[HALO_TILES:HALO_TILES + tile_dev] * own_live
    q_own = q[mine]
    scale = own_live * (2.0 * inverse_sq[mine] * norm[mine])
    sums = [
        jnp.concatenate(
            [
                out_ref[pl.ds(k, RIM, stride=8)],
                inner_out_ref[pl.ds(8 * RIM + k, tile_dev - 2 * RIM, stride=8)],
                out_ref[pl.ds(8 * (tile_dev - RIM) + k, RIM, stride=8)],
            ],
            axis=0,
        )
        for k in range(8)
    ]
    for c in range(3):
        x = pos[c][mine]
        accel_ref[c] = scale * (q_own * (x * sums[0] - sums[1 + c]) + (x * sums[4] - sums[5 + c]))


def inner_density(pairwise, table, own, live, carried=()):
    tile_dev, rows = live.shape
    listed = table.shape[0] - 1
    count = (tile_dev - RIM) // 2
    late = len(carried) > 0
    shapes = [
        jax.ShapeDtypeStruct((count, listed * rows, 2 * rows), f32),
        jax.ShapeDtypeStruct((16 * count, rows), f32),
        jax.ShapeDtypeStruct((tile_dev, rows, rows), bf16),
        jax.ShapeDtypeStruct((count, 2 * rows, 2 * rows), bf16),
    ]
    features = [pltpu.VMEM((8 * tile_dev, rows), f32), pltpu.VMEM((8 * tile_dev, rows), f32)]
    edges, forces = [], []
    if late:
        edges = [jax.ShapeDtypeStruct((2 * RIM, rows, rows), bf16), jax.ShapeDtypeStruct((8 * tile_dev, rows), f32)]
        forces = [pltpu.VMEM((8 * tile_dev, rows), f32), pltpu.VMEM((tile_dev, 16, rows), bf16)]
    return pl.pallas_call(
        functools.partial(inner_kernel, late, pairwise),
        out_shape=shapes + edges,
        in_specs=[ANY] + [VMEM] * (2 + len(carried)),
        out_specs=[VMEM] * len(shapes + edges),
        input_output_aliases={3 + i: i for i in range(len(carried))},
        scratch_shapes=features + forces + [pltpu.SMEM(table.shape, jnp.int32), pltpu.SemaphoreType.DMA((1,))],
        compiler_params=pltpu.CompilerParams(vmem_limit_bytes=24 << 20),
        cost_estimate=pl.CostEstimate(flops=10 ** 9, bytes_accessed=10 ** 7, transcendentals=0),
        name="inner_late" if late else "inner_early",
    )(table, own, live, *carried)


def outer_step(pairwise, table, rim_lists, own, live, below, above, pair, part, edge, inner_out):
    tile_dev, rows = live.shape
    ext = tile_dev + 2 * RIM
    listed = table.shape[0] - 1
    return pl.pallas_call(
        functools.partial(outer_kernel, pairwise),
        out_shape=(jax.ShapeDtypeStruct((tile_dev, rows), f32), jax.ShapeDtypeStruct((3, tile_dev, rows), f32)),
        in_specs=[ANY] * 2 + [VMEM] * 8,
        out_specs=(VMEM, VMEM),
        scratch_shapes=[
            pltpu.VMEM((8 * 4 * RIM, rows), f32),
            pltpu.VMEM((8 * 4 * RIM, rows), f32),
            pltpu.VMEM((4 * RIM, rows, rows), bf16),
            pltpu.VMEM((RIM, 2 * rows, 2 * rows), bf16),
            pltpu.VMEM((RIM, listed * rows, 2 * rows), f32),
            pltpu.VMEM((8 * 2 * RIM, rows), f32),
            pltpu.VMEM((8 * ext, rows), f32),
            pltpu.VMEM((ext, 16, rows), bf16),
            pltpu.VMEM((8 * tile_dev, rows), f32),
            pltpu.SMEM(table.shape, jnp.int32),
            pltpu.SMEM(rim_lists.shape, jnp.int32),
            pltpu.SemaphoreType.DMA((2,)),
        ],
        compiler_params=pltpu.CompilerParams(vmem_limit_bytes=24 << 20),
        name="outer_step",
    )(table, rim_lists, own, live, below, above, pair, part, edge, inner_out)


def per_device(coords, smooth, masses, owners, counts, neighbours):
    tile_dev, rows = smooth.shape
    regions = lax.axis_size("region")
    subs = lax.axis_size("sub")
    per_dest = tile_dev // regions
    listed = neighbours.shape[1]
    pairwise = regions <= 4 and regions & (regions - 1) == 0
    grouped = group_tiles(coords, smooth, masses, owners, regions, pairwise)
    me = lax.axis_index("region") if pairwise else jnp.int32(0)
    table = jnp.concatenate([neighbours.T, counts[None]], axis=0)
    if pairwise:
        live, ids, local = stage(table, grouped[0])
        blocks = [local]
        for k in range(1, regions):
            blocks.append(lax.ppermute(grouped[k], "region", [(i, i ^ k) for i in range(regions)]))
        own = jnp.stack(blocks)
    else:
        live, ids, _ = stage(table, grouped[0][0])
        own = lax.all_to_all(grouped[0], "region", 0, 0, tiled=True)
    by_field = own.reshape(regions, FIELDS, per_dest, rows)

    def rim(first):
        if pairwise:
            block = lax.dynamic_index_in_dim(by_field, me ^ (0 if first else regions - 1), 0, keepdims=False)
            block = block[:, :RIM] if first else block[:, per_dest - RIM:]
        else:
            blocks = RIM // per_dest
            block = by_field[:blocks] if first else by_field[regions - blocks:]
            block = jnp.swapaxes(block, 0, 1).reshape(FIELDS, RIM, rows)
        tiles = slice(0, RIM) if first else slice(tile_dev - RIM, tile_dev)
        block = jnp.concatenate([block[:4], (block[4] * live[tiles])[None]], axis=0).reshape(FIELDS * RIM, rows)
        return jnp.concatenate([block, ids[0 if first else 1]], axis=0)

    up = [(i, (i + 1) % subs) for i in range(subs)]
    down = [(j, i) for i, j in up]
    below = lax.ppermute(rim(False), "sub", up)
    carried = inner_density(pairwise, table, own, live)
    above = lax.ppermute(rim(True), "sub", down)
    pair, part, _, _, edge, inner_out = inner_density(pairwise, table, own, live, carried)
    count = HALO_TILES * listed
    places = [
        below[FIELDS * RIM, :count] + (HALO_TILES - tile_dev),
        ids[0, 0, :count] + HALO_TILES,
        ids[1, 0, :count] + (HALO_TILES - tile_dev + 2 * RIM),
        above[FIELDS * RIM, :count] + (HALO_TILES + 2 * RIM),
    ]
    rim_lists = jnp.concatenate(places).astype(jnp.int32)
    return outer_step(pairwise, table, rim_lists, own, live, below, above, pair, part, edge, inner_out)


def solution(mesh):
    in_specs = (
        P(None, ("region", "sub"), None),
        P(("region", "sub"), None),
        P(("region", "sub"), None),
        P(("region", "sub")),
        P(("region", "sub")),
        P(("region", "sub"), None),
    )
    out_specs = (P(("region", "sub"), None), P(None, ("region", "sub"), None))
    return jax.shard_map(
        per_device, mesh=mesh, in_specs=in_specs, out_specs=out_specs, check_vma=False
    )
```

```python
import functools
import math

import jax
import jax.numpy as jnp
from jax import lax
from jax.experimental import pallas as pl
from jax.experimental.pallas import tpu as pltpu
from jax.sharding import PartitionSpec as P


HALO_TILES = 4
RIM = 2 * HALO_TILES
FIELDS = 5
CHUNKS = 4
EMPTY_LOG = -1024.0
LOG2E = 1.4426950408889634
kernel_scale = math.pi ** (-1.5)

f32, bf16 = jnp.float32, jnp.bfloat16
VMEM = pl.BlockSpec(memory_space=pltpu.VMEM)
SMEM = pl.BlockSpec(memory_space=pltpu.SMEM)
ANY = pl.BlockSpec(memory_space=pl.ANY)


def group_kernel(pairwise, count, *refs):
    sources, outs = refs[:4], refs[4:4 + count]
    owners_ref, coords_ref, smooth_ref, masses_ref, block_ref, sems = refs[4 + count:]
    targets = (owners_ref, coords_ref, smooth_ref, masses_ref)
    copies = [pltpu.make_async_copy(s, t, sems.at[i]) for i, (s, t) in enumerate(zip(sources, targets))]
    for copy in copies:
        copy.start()
    copies[0].wait()
    regions = block_ref.shape[0]
    per_dest = block_ref.shape[1] // FIELDS
    bits = per_dest.bit_length()
    per_word = 31 // bits
    seen = [jnp.int32(0)] * pl.cdiv(regions, per_word)
    me = lax.axis_index("region") if pairwise else 0
    places = []
    for n in range(owners_ref.shape[0]):
        d = owners_ref[n]
        word = d // per_word if len(seen) > 1 else 0
        shift = (d - word * per_word) * bits
        k = seen[0]
        for w in range(1, len(seen)):
            k = jnp.where(word == w, seen[w], k)
        k = (k >> shift) & ((1 << bits) - 1)
        step = jnp.int32(1) << shift
        seen = [s + (jnp.where(word == w, step, 0) if len(seen) > 1 else step) for w, s in enumerate(seen)]
        places.append((d ^ me if pairwise else d, k))
    for copy in copies[1:]:
        copy.wait()
    for n, (d, k) in enumerate(places):
        for c in range(3):
            block_ref[d, pl.ds(c * per_dest + k, 1)] = coords_ref[c, n:n + 1]
        block_ref[d, pl.ds(3 * per_dest + k, 1)] = smooth_ref[n:n + 1]
        block_ref[d, pl.ds(4 * per_dest + k, 1)] = masses_ref[n:n + 1]
    for k, out in enumerate(outs):
        out[...] = block_ref[k] if pairwise else block_ref[...]


def group_tiles(coords, smooth, masses, owners, regions, pairwise):
    tile_dev, rows = smooth.shape
    per_dest = tile_dev // regions
    block = (FIELDS * per_dest, rows)
    hbm = pl.BlockSpec(memory_space=pltpu.HBM)
    whole = (regions,) + block
    shapes = [block] * regions if pairwise else [whole]
    return pl.pallas_call(
        functools.partial(group_kernel, pairwise, len(shapes)),
        out_shape=[jax.ShapeDtypeStruct(shape, f32) for shape in shapes],
        in_specs=[hbm] * 4,
        out_specs=[VMEM] * len(shapes),
        scratch_shapes=[pltpu.SMEM(owners.shape, jnp.int32)]
        + [pltpu.VMEM(a.shape, f32) for a in (coords, smooth, masses)]
        + [pltpu.VMEM(whole, f32), pltpu.SemaphoreType.DMA((4,))],
        compiler_params=pltpu.CompilerParams(vmem_limit_bytes=8 << 20),
        name="group_tiles",
    )(*[pltpu.with_memory_space_constraint(a, pltpu.HBM) for a in (owners, coords, smooth, masses)])


def stage_kernel(table_ref, live_ref, ids_ref):
    tile_dev, rows = live_ref.shape
    listed = table_ref.shape[0] - 1
    lane = lax.broadcasted_iota(jnp.int32, (8, rows), 1)
    row = lax.broadcasted_iota(jnp.int32, (8, rows), 0)
    for t in range(0, tile_dev, 8):
        limit = jnp.full((8, rows), table_ref[listed, t])
        for i in range(1, 8):
            limit = jnp.where(row == i, table_ref[listed, t + i], limit)
        live_ref[t:t + 8] = (lane < limit).astype(f32)
    for side, start in enumerate((0, tile_dev - HALO_TILES)):
        ids = jnp.zeros((8, rows), f32)
        for i in range(HALO_TILES):
            for n in range(listed):
                ids = jnp.where(lane == i * listed + n, table_ref[n, start + i].astype(f32), ids)
        ids_ref[side] = ids


def stage(table, rows):
    tile_dev = table.shape[1]
    return pl.pallas_call(
        stage_kernel,
        out_shape=(
            jax.ShapeDtypeStruct((tile_dev, rows), f32),
            jax.ShapeDtypeStruct((2, 8, rows), f32),
        ),
        in_specs=[SMEM],
        out_specs=(VMEM,) * 2,
        compiler_params=pltpu.CompilerParams(vmem_limit_bytes=4 << 20),
        name="stage",
    )(table)


def parts_of(x, count):
    parts = []
    for _ in range(count):
        part = x.astype(bf16).astype(f32)
        parts.append(part)
        x = x - part
    return parts


def dot(a, b):
    return jnp.dot(a, b, preferred_element_type=f32)


def own_field(pairwise, own_ref, live_ref, f):
    tile_dev = live_ref.shape[0]
    regions, per_dest = own_ref.shape[0], tile_dev // own_ref.shape[0]
    rows = pl.ds(f * per_dest, per_dest)
    me = lax.axis_index("region") if pairwise else 0
    value = jnp.concatenate([own_ref[me ^ r, rows] for r in range(regions)], axis=0)
    return value * live_ref[...] if f == 4 else value


def field_terms(fields):
    pos, h, mass = fields[:3], fields[3], fields[4]
    inverse_sq = 1.0 / (h * h)
    return pos, mass > 0, mass, inverse_sq, kernel_scale * inverse_sq / h


def put_rows(ref, values):
    count = values[0].shape[0]
    for k, value in enumerate(values):
        ref[k * count:(k + 1) * count] = value


def put_features(pos, live, mass, inverse_sq, partner_ref, mine_ref):
    c = inverse_sq * LOG2E
    square = pos[0] * pos[0] + pos[1] * pos[1] + pos[2] * pos[2]
    log_mass = jnp.where(live, jnp.log2(jnp.where(live, mass, 1.0)), EMPTY_LOG)
    one, zero = jnp.ones_like(c), jnp.zeros_like(c)
    put_rows(partner_ref, pos + [square, log_mass, one, zero, zero])
    put_rows(mine_ref, [2 * c * x for x in pos] + [-c, one, -c * square, zero, zero])


def tile_of(ref, e):
    return ref[pl.ds(e, 8, stride=ref.shape[0] // 8)]


def turned(ref, e):
    p1, p2, p3 = parts_of(tile_of(ref, e), 3)
    block = jnp.concatenate([p1, p1, p2, p1, p3, p2], axis=0).astype(bf16)
    fill = jnp.zeros((block.shape[1] - block.shape[0], block.shape[1]), bf16)
    return jnp.concatenate([block, fill], axis=0).T


def pair_weights(ref, e):
    def one_tile(e):
        o1, o2, o3 = parts_of(tile_of(ref, e), 3)
        block = jnp.concatenate([o1, o2, o1, o3, o1, o2], axis=0).astype(bf16)
        return jnp.concatenate([block, jnp.zeros((block.shape[1] - block.shape[0], block.shape[1]), bf16)], axis=0)

    first, second = one_tile(e), one_tile(e + 1)
    blank = jnp.zeros_like(first)
    return jnp.concatenate(
        [jnp.concatenate([first, blank], axis=1), jnp.concatenate([blank, second], axis=1)], axis=0
    )


def density_pair(turned_ref, own, partners, part_ref, at, store):
    rows = own.shape[1] // 2
    left = [jnp.concatenate([turned_ref[a], turned_ref[b]], axis=1) for a, b in partners]
    t = jnp.exp2(dot(jnp.concatenate(left, axis=0), own))
    if store is not None:
        store[...] = t
    total = jnp.sum(t.reshape(t.shape[0] // 8, 8, 2 * rows), axis=0)
    part_ref[pl.ds(at, 8)] = total[:, :rows]
    part_ref[pl.ds(at + 8, 8)] = total[:, rows:]


def pressure(raw, live):
    return jnp.where(live, jnp.exp2(jnp.log2(jnp.where(live, raw, 1.0)) * (-1.0 / 3.0)), 0.0)


def put_coefficients(ref, pos, q):
    put_rows(ref, [jnp.ones_like(q)] + pos + [q] + [q * x for x in pos])


def narrow(narrow_ref, ref, e):
    narrow_ref[e] = jnp.concatenate(parts_of(tile_of(ref, e), 2), axis=0).astype(bf16)


def force_pair(narrow_ref, partners, pair, out_ref, at):
    rows = pair.shape[1] // 2
    total = None
    for n, (e0, e1) in enumerate(partners):
        left = jnp.concatenate([narrow_ref[e0], narrow_ref[e1]], axis=0)
        w = pair[n * rows:(n + 1) * rows]
        high = w.astype(bf16)
        part = dot(left, high) + dot(left, (w - high.astype(f32)).astype(bf16))
        total = part if total is None else total + part
    out_ref[pl.ds(at, 8)] = total[:8, :rows] + total[8:16, :rows]
    out_ref[pl.ds(at + 8, 8)] = total[16:24, rows:] + total[24:, rows:]


def inner_kernel(late, pairwise, table_in_ref, own_ref, live_ref, *refs):
    refs, (table_ref, table_sem) = refs[:-2], refs[-2:]
    table_copy = pltpu.make_async_copy(table_in_ref, table_ref, table_sem.at[0])
    if late:
        refs, (edge_ref, out_ref, partner_ref, mine_ref, coef_ref, narrow_ref) = refs[:-6], refs[-6:]
    else:
        refs, (partner_ref, mine_ref) = refs[:-2], refs[-2:]
    pair_ref, part_ref, turned_ref, weights_ref = refs[-4:]
    tile_dev = live_ref.shape[0]
    listed = table_ref.shape[0] - 1
    chunk = pair_ref.shape[0] // CHUNKS
    ahead = 2 * chunk + 2 * HALO_TILES

    def turn(t):
        turned_ref[t] = turned(partner_ref, t)

    def weigh(p):
        weights_ref[p] = pair_weights(mine_ref, HALO_TILES + 2 * p)

    def features():
        pos, live, mass, inverse_sq, _ = field_terms([own_field(pairwise, own_ref, live_ref, f) for f in range(FIELDS)])
        put_features(pos, live, mass, inverse_sq, partner_ref, mine_ref)

    def do_chunk(c, more=True):
        for i in range(chunk):
            t = HALO_TILES + 2 * (c * chunk + i)
            partners = [(table_ref[n, t] - HALO_TILES, table_ref[n, t + 1] - HALO_TILES) for n in range(listed)]
            p = c * chunk + i
            density_pair(turned_ref, weights_ref[p], partners, part_ref, 16 * p, pair_ref.at[p])
        if more:
            for i in range(2 * chunk):
                turn(c * 2 * chunk + ahead + i)
            for i in range(chunk):
                weigh((c + 1) * chunk + i)

    early = jnp.maximum(CHUNKS - 1 - 2 * lax.axis_index("sub"), 0)

    def begin():
        for t in range(ahead):
            turn(t)
        for p in range(chunk):
            weigh(p)

    if late:
        table_copy.start()
        features()
        pl.when(early == 0)(begin)
        table_copy.wait()
        pl.loop(early, CHUNKS - 1)(do_chunk)
        do_chunk(CHUNKS - 1, False)
        edge_ref[:RIM] = turned_ref[:RIM]
        edge_ref[RIM:] = turned_ref[tile_dev - RIM:]
        pos, live, _, _, norm = field_terms([own_field(pairwise, own_ref, live_ref, f) for f in range(FIELDS)])
        inside = slice(HALO_TILES, tile_dev - HALO_TILES)
        raw = sum(part_ref[pl.ds(k, tile_dev - RIM, stride=8)] for k in range(8)) * norm[inside]
        blank = jnp.zeros((HALO_TILES, live_ref.shape[1]), f32)
        put_coefficients(coef_ref, pos, jnp.concatenate([blank, pressure(raw, live[inside]), blank], axis=0))

        @pl.loop(HALO_TILES, tile_dev - HALO_TILES, unroll=8)
        def _(t):
            narrow(narrow_ref, coef_ref, t)

        half = HALO_TILES // 2

        @pl.loop(half, pair_ref.shape[0] - half, unroll=8)
        def _(p):
            t = HALO_TILES + 2 * p
            partners = [(table_ref[n, t] - HALO_TILES, table_ref[n, t + 1] - HALO_TILES) for n in range(listed)]
            force_pair(narrow_ref, partners, pair_ref.at[p], out_ref, 8 * t)
    else:

        @pl.when(early > 0)
        def _():
            table_copy.start()
            features()
            begin()
            table_copy.wait()
            pl.loop(0, early)(do_chunk)


def outer_kernel(
    pairwise, table_in_ref, rim_lists_in_ref, own_ref, live_ref, below_ref, above_ref, pair_ref, part_ref, edge_ref, inner_out_ref,
    density_ref, accel_ref, partner_ref, mine_ref, turned_ref, weights_ref, rim_pair_ref, rim_part_ref, coef_ref,
    coefb_ref, out_ref, table_ref, rim_lists_ref, sems,
):
    copies = [
        pltpu.make_async_copy(table_in_ref, table_ref, sems.at[0]),
        pltpu.make_async_copy(rim_lists_in_ref, rim_lists_ref, sems.at[1]),
    ]
    for copy in copies:
        copy.start()
    tile_dev, rows = live_ref.shape
    ext = tile_dev + 2 * RIM
    listed = table_ref.shape[0] - 1
    fields = [
        jnp.concatenate(
            [
                below_ref[f * RIM:(f + 1) * RIM],
                own_field(pairwise, own_ref, live_ref, f),
                above_ref[f * RIM:(f + 1) * RIM],
            ],
            axis=0,
        )
        for f in range(FIELDS)
    ]
    pos, live, mass, inverse_sq, norm = field_terms(fields)
    rim_pairs = RIM

    def rims(x):
        return jnp.concatenate([x[:2 * RIM], x[tile_dev:]], axis=0)

    put_features([rims(x) for x in pos], rims(live), rims(mass), rims(inverse_sq), partner_ref, mine_ref)
    for e in range(RIM):
        turned_ref[e] = turned(partner_ref, e)
        turned_ref[RIM + e] = edge_ref[e]
        turned_ref[2 * RIM + e] = edge_ref[RIM + e]
        turned_ref[3 * RIM + e] = turned(partner_ref, 3 * RIM + e)
    for r in range(rim_pairs):
        weights_ref[r] = pair_weights(mine_ref, HALO_TILES + 2 * r + (RIM if 2 * r >= rim_pairs else 0))

    outer = RIM + HALO_TILES
    inner_raw = sum(part_ref[pl.ds(k, tile_dev - RIM, stride=8)] for k in range(8)) * norm[outer:ext - outer]
    for copy in copies:
        copy.wait()
    for r in range(rim_pairs):
        first = 2 * r * listed
        partners = [(rim_lists_ref[first + n], rim_lists_ref[first + listed + n]) for n in range(listed)]
        density_pair(turned_ref, weights_ref[r], partners, rim_part_ref, 16 * r, rim_pair_ref.at[r])

    rim_raw = sum(rim_part_ref[pl.ds(k, 2 * RIM, stride=8)] for k in range(8))
    raw = jnp.concatenate(
        [rim_raw[:RIM] * norm[HALO_TILES:outer], inner_raw, rim_raw[RIM:] * norm[ext - outer:ext - HALO_TILES]], axis=0
    )
    q = pressure(raw, live[HALO_TILES:ext - HALO_TILES])
    pad = jnp.zeros((HALO_TILES, rows), f32)
    q = jnp.concatenate([pad, q, pad], axis=0)
    put_coefficients(coef_ref, pos, q)
    for e in range(2 * RIM):
        narrow(coefb_ref, coef_ref, HALO_TILES + e)
        narrow(coefb_ref, coef_ref, ext - HALO_TILES - 2 * RIM + e)
    half = HALO_TILES // 2
    count = pair_ref.shape[0]

    def edge_force(t, pair):
        partners = [(table_ref[n, t] + HALO_TILES, table_ref[n, t + 1] + HALO_TILES) for n in range(listed)]
        force_pair(coefb_ref, partners, pair, out_ref, 8 * t)

    for i in range(half):
        edge_force(2 * i, rim_pair_ref.at[half + i])
        edge_force(HALO_TILES + 2 * i, pair_ref.at[i])
        edge_force(tile_dev - RIM + 2 * i, pair_ref.at[count - half + i])
        edge_force(tile_dev - HALO_TILES + 2 * i, rim_pair_ref.at[2 * half + i])

    mine = slice(RIM, RIM + tile_dev)
    own_live = live_ref[...]
    density_ref[...] = raw[HALO_TILES:HALO_TILES + tile_dev] * own_live
    q_own = q[mine]
    scale = own_live * (2.0 * inverse_sq[mine] * norm[mine])
    sums = [
        jnp.concatenate(
            [
                out_ref[pl.ds(k, RIM, stride=8)],
                inner_out_ref[pl.ds(8 * RIM + k, tile_dev - 2 * RIM, stride=8)],
                out_ref[pl.ds(8 * (tile_dev - RIM) + k, RIM, stride=8)],
            ],
            axis=0,
        )
        for k in range(8)
    ]
    for c in range(3):
        x = pos[c][mine]
        accel_ref[c] = scale * (q_own * (x * sums[0] - sums[1 + c]) + (x * sums[4] - sums[5 + c]))


def inner_density(pairwise, table, own, live, carried=()):
    tile_dev, rows = live.shape
    listed = table.shape[0] - 1
    count = (tile_dev - RIM) // 2
    late = len(carried) > 0
    shapes = [
        jax.ShapeDtypeStruct((count, listed * rows, 2 * rows), f32),
        jax.ShapeDtypeStruct((16 * count, rows), f32),
        jax.ShapeDtypeStruct((tile_dev, rows, rows), bf16),
        jax.ShapeDtypeStruct((count, 2 * rows, 2 * rows), bf16),
    ]
    features = [pltpu.VMEM((8 * tile_dev, rows), f32), pltpu.VMEM((8 * tile_dev, rows), f32)]
    edges, forces = [], []
    if late:
        edges = [jax.ShapeDtypeStruct((2 * RIM, rows, rows), bf16), jax.ShapeDtypeStruct((8 * tile_dev, rows), f32)]
        forces = [pltpu.VMEM((8 * tile_dev, rows), f32), pltpu.VMEM((tile_dev, 16, rows), bf16)]
    return pl.pallas_call(
        functools.partial(inner_kernel, late, pairwise),
        out_shape=shapes + edges,
        in_specs=[ANY] + [VMEM] * (2 + len(carried)),
        out_specs=[VMEM] * len(shapes + edges),
        input_output_aliases={3 + i: i for i in range(len(carried))},
        scratch_shapes=features + forces + [pltpu.SMEM(table.shape, jnp.int32), pltpu.SemaphoreType.DMA((1,))],
        compiler_params=pltpu.CompilerParams(vmem_limit_bytes=24 << 20),
        cost_estimate=pl.CostEstimate(flops=10 ** 9, bytes_accessed=10 ** 7, transcendentals=0),
        name="inner_late" if late else "inner_early",
    )(table, own, live, *carried)


def outer_step(pairwise, table, rim_lists, own, live, below, above, pair, part, edge, inner_out):
    tile_dev, rows = live.shape
    ext = tile_dev + 2 * RIM
    listed = table.shape[0] - 1
    return pl.pallas_call(
        functools.partial(outer_kernel, pairwise),
        out_shape=(jax.ShapeDtypeStruct((tile_dev, rows), f32), jax.ShapeDtypeStruct((3, tile_dev, rows), f32)),
        in_specs=[ANY] * 2 + [VMEM] * 8,
        out_specs=(VMEM, VMEM),
        scratch_shapes=[
            pltpu.VMEM((8 * 4 * RIM, rows), f32),
            pltpu.VMEM((8 * 4 * RIM, rows), f32),
            pltpu.VMEM((4 * RIM, rows, rows), bf16),
            pltpu.VMEM((RIM, 2 * rows, 2 * rows), bf16),
            pltpu.VMEM((RIM, listed * rows, 2 * rows), f32),
            pltpu.VMEM((8 * 2 * RIM, rows), f32),
            pltpu.VMEM((8 * ext, rows), f32),
            pltpu.VMEM((ext, 16, rows), bf16),
            pltpu.VMEM((8 * tile_dev, rows), f32),
            pltpu.SMEM(table.shape, jnp.int32),
            pltpu.SMEM(rim_lists.shape, jnp.int32),
            pltpu.SemaphoreType.DMA((2,)),
        ],
        compiler_params=pltpu.CompilerParams(vmem_limit_bytes=24 << 20),
        name="outer_step",
    )(table, rim_lists, own, live, below, above, pair, part, edge, inner_out)


def per_device(coords, smooth, masses, owners, counts, neighbours):
    tile_dev, rows = smooth.shape
    regions = lax.axis_size("region")
    subs = lax.axis_size("sub")
    per_dest = tile_dev // regions
    listed = neighbours.shape[1]
    pairwise = regions <= 4 and regions & (regions - 1) == 0
    grouped = group_tiles(coords, smooth, masses, owners, regions, pairwise)
    me = lax.axis_index("region") if pairwise else jnp.int32(0)
    table = jnp.concatenate([neighbours.T, counts[None]], axis=0)
    if pairwise:
        live, ids = stage(table, rows)
        blocks = [grouped[0]]
        for k in range(1, regions):
            blocks.append(lax.ppermute(grouped[k], "region", [(i, i ^ k) for i in range(regions)]))
        own = jnp.stack(blocks)
    else:
        live, ids = stage(table, rows)
        own = lax.all_to_all(grouped[0], "region", 0, 0, tiled=True)
    by_field = own.reshape(regions, FIELDS, per_dest, rows)

    def rim(first):
        if pairwise:
            block = lax.dynamic_index_in_dim(by_field, me ^ (0 if first else regions - 1), 0, keepdims=False)
            block = block[:, :RIM] if first else block[:, per_dest - RIM:]
        else:
            blocks = RIM // per_dest
            block = by_field[:blocks] if first else by_field[regions - blocks:]
            block = jnp.swapaxes(block, 0, 1).reshape(FIELDS, RIM, rows)
        tiles = slice(0, RIM) if first else slice(tile_dev - RIM, tile_dev)
        block = jnp.concatenate([block[:4], (block[4] * live[tiles])[None]], axis=0).reshape(FIELDS * RIM, rows)
        return jnp.concatenate([block, ids[0 if first else 1]], axis=0)

    up = [(i, (i + 1) % subs) for i in range(subs)]
    down = [(j, i) for i, j in up]
    below = lax.ppermute(rim(False), "sub", up)
    carried = inner_density(pairwise, table, own, live)
    above = lax.ppermute(rim(True), "sub", down)
    pair, part, _, _, edge, inner_out = inner_density(pairwise, table, own, live, carried)
    count = HALO_TILES * listed
    places = [
        below[FIELDS * RIM, :count] + (HALO_TILES - tile_dev),
        ids[0, 0, :count] + HALO_TILES,
        ids[1, 0, :count] + (HALO_TILES - tile_dev + 2 * RIM),
        above[FIELDS * RIM, :count] + (HALO_TILES + 2 * RIM),
    ]
    rim_lists = jnp.concatenate(places).astype(jnp.int32)
    return outer_step(pairwise, table, rim_lists, own, live, below, above, pair, part, edge, inner_out)


def solution(mesh):
    in_specs = (
        P(None, ("region", "sub"), None),
        P(("region", "sub"), None),
        P(("region", "sub"), None),
        P(("region", "sub")),
        P(("region", "sub")),
        P(("region", "sub"), None),
    )
    out_specs = (P(("region", "sub"), None), P(None, ("region", "sub"), None))
    return jax.shard_map(
        per_device, mesh=mesh, in_specs=in_specs, out_specs=out_specs, check_vma=False
    )
```

```python
import functools
import math

import jax
import jax.numpy as jnp
from jax import lax
from jax.experimental import pallas as pl
from jax.experimental.pallas import tpu as pltpu
from jax.sharding import PartitionSpec as P


HALO_TILES = 4
RIM = 2 * HALO_TILES
FIELDS = 5
CHUNKS = 4
EMPTY_LOG = -1024.0
LOG2E = 1.4426950408889634
kernel_scale = math.pi ** (-1.5)

f32, bf16 = jnp.float32, jnp.bfloat16
VMEM = pl.BlockSpec(memory_space=pltpu.VMEM)
SMEM = pl.BlockSpec(memory_space=pltpu.SMEM)
ANY = pl.BlockSpec(memory_space=pl.ANY)


def group_kernel(pairwise, count, *refs):
    sources, outs = refs[:4], refs[4:4 + count]
    owners_ref, coords_ref, smooth_ref, masses_ref, block_ref, sems = refs[4 + count:]
    targets = (owners_ref, coords_ref, smooth_ref, masses_ref)
    copies = [pltpu.make_async_copy(s, t, sems.at[i]) for i, (s, t) in enumerate(zip(sources, targets))]
    for copy in copies:
        copy.start()
    copies[0].wait()
    regions = block_ref.shape[0]
    per_dest = block_ref.shape[1] // FIELDS
    bits = per_dest.bit_length()
    per_word = 31 // bits
    seen = [jnp.int32(0)] * pl.cdiv(regions, per_word)
    me = lax.axis_index("region") if pairwise else 0
    places = []
    for n in range(owners_ref.shape[0]):
        d = owners_ref[n]
        word = d // per_word if len(seen) > 1 else 0
        shift = (d - word * per_word) * bits
        k = seen[0]
        for w in range(1, len(seen)):
            k = jnp.where(word == w, seen[w], k)
        k = (k >> shift) & ((1 << bits) - 1)
        step = jnp.int32(1) << shift
        seen = [s + (jnp.where(word == w, step, 0) if len(seen) > 1 else step) for w, s in enumerate(seen)]
        places.append((d ^ me if pairwise else d, k))
    for copy in copies[1:]:
        copy.wait()
    for n, (d, k) in enumerate(places):
        for c in range(3):
            block_ref[d, pl.ds(c * per_dest + k, 1)] = coords_ref[c, n:n + 1]
        block_ref[d, pl.ds(3 * per_dest + k, 1)] = smooth_ref[n:n + 1]
        block_ref[d, pl.ds(4 * per_dest + k, 1)] = masses_ref[n:n + 1]
    for k, out in enumerate(outs):
        out[...] = block_ref[k] if pairwise else block_ref[...]


def group_tiles(coords, smooth, masses, owners, regions, pairwise):
    tile_dev, rows = smooth.shape
    per_dest = tile_dev // regions
    block = (FIELDS * per_dest, rows)
    hbm = pl.BlockSpec(memory_space=pltpu.HBM)
    whole = (regions,) + block
    shapes = [block] * regions if pairwise else [whole]
    return pl.pallas_call(
        functools.partial(group_kernel, pairwise, len(shapes)),
        out_shape=[jax.ShapeDtypeStruct(shape, f32) for shape in shapes],
        in_specs=[hbm] * 4,
        out_specs=[VMEM] * len(shapes),
        scratch_shapes=[pltpu.SMEM(owners.shape, jnp.int32)]
        + [pltpu.VMEM(a.shape, f32) for a in (coords, smooth, masses)]
        + [pltpu.VMEM(whole, f32), pltpu.SemaphoreType.DMA((4,))],
        compiler_params=pltpu.CompilerParams(vmem_limit_bytes=8 << 20),
        name="group_tiles",
    )(*[pltpu.with_memory_space_constraint(a, pltpu.HBM) for a in (owners, coords, smooth, masses)])


def stage_kernel(table_ref, live_ref, ids_ref):
    tile_dev, rows = live_ref.shape
    listed = table_ref.shape[0] - 1
    lane = lax.broadcasted_iota(jnp.int32, (8, rows), 1)
    row = lax.broadcasted_iota(jnp.int32, (8, rows), 0)
    for t in range(0, tile_dev, 8):
        limit = jnp.full((8, rows), table_ref[listed, t])
        for i in range(1, 8):
            limit = jnp.where(row == i, table_ref[listed, t + i], limit)
        live_ref[t:t + 8] = (lane < limit).astype(f32)
    for side, start in enumerate((0, tile_dev - HALO_TILES)):
        ids = jnp.zeros((8, rows), f32)
        for i in range(HALO_TILES):
            for n in range(listed):
                ids = jnp.where(lane == i * listed + n, table_ref[n, start + i].astype(f32), ids)
        ids_ref[side] = ids


def stage(table, rows):
    tile_dev = table.shape[1]
    return pl.pallas_call(
        stage_kernel,
        out_shape=(
            jax.ShapeDtypeStruct((tile_dev, rows), f32),
            jax.ShapeDtypeStruct((2, 8, rows), f32),
        ),
        in_specs=[SMEM],
        out_specs=(VMEM,) * 2,
        compiler_params=pltpu.CompilerParams(vmem_limit_bytes=4 << 20),
        name="stage",
    )(table)


def parts_of(x, count):
    parts = []
    for _ in range(count):
        part = x.astype(bf16).astype(f32)
        parts.append(part)
        x = x - part
    return parts


def dot(a, b):
    return jnp.dot(a, b, preferred_element_type=f32)


def own_field(pairwise, own_ref, live_ref, f):
    tile_dev = live_ref.shape[0]
    regions, per_dest = own_ref.shape[0], tile_dev // own_ref.shape[0]
    rows = pl.ds(f * per_dest, per_dest)
    me = lax.axis_index("region") if pairwise else 0
    value = jnp.concatenate([own_ref[me ^ r, rows] for r in range(regions)], axis=0)
    return value * live_ref[...] if f == 4 else value


def field_terms(fields):
    pos, h, mass = fields[:3], fields[3], fields[4]
    inverse_sq = 1.0 / (h * h)
    return pos, mass > 0, mass, inverse_sq, kernel_scale * inverse_sq / h


def put_rows(ref, values):
    count = values[0].shape[0]
    for k, value in enumerate(values):
        ref[k * count:(k + 1) * count] = value


def put_features(pos, live, mass, inverse_sq, partner_ref, mine_ref):
    c = inverse_sq * LOG2E
    square = pos[0] * pos[0] + pos[1] * pos[1] + pos[2] * pos[2]
    log_mass = jnp.where(live, jnp.log2(jnp.where(live, mass, 1.0)), EMPTY_LOG)
    one, zero = jnp.ones_like(c), jnp.zeros_like(c)
    put_rows(partner_ref, pos + [square, log_mass, one, zero, zero])
    put_rows(mine_ref, [2 * c * x for x in pos] + [-c, one, -c * square, zero, zero])


def tile_of(ref, e):
    return ref[pl.ds(e, 8, stride=ref.shape[0] // 8)]


def turned(ref, e):
    p1, p2, p3 = parts_of(tile_of(ref, e), 3)
    block = jnp.concatenate([p1, p1, p2, p1, p3, p2], axis=0).astype(bf16)
    fill = jnp.zeros((block.shape[1] - block.shape[0], block.shape[1]), bf16)
    return jnp.concatenate([block, fill], axis=0).T


def pair_weights(ref, e):
    def one_tile(e):
        o1, o2, o3 = parts_of(tile_of(ref, e), 3)
        block = jnp.concatenate([o1, o2, o1, o3, o1, o2], axis=0).astype(bf16)
        return jnp.concatenate([block, jnp.zeros((block.shape[1] - block.shape[0], block.shape[1]), bf16)], axis=0)

    first, second = one_tile(e), one_tile(e + 1)
    blank = jnp.zeros_like(first)
    return jnp.concatenate(
        [jnp.concatenate([first, blank], axis=1), jnp.concatenate([blank, second], axis=1)], axis=0
    )


def density_pair(turned_ref, own, partners, part_ref, at, store):
    rows = own.shape[1] // 2
    left = [jnp.concatenate([turned_ref[a], turned_ref[b]], axis=1) for a, b in partners]
    t = jnp.exp2(dot(jnp.concatenate(left, axis=0), own))
    if store is not None:
        store[...] = t
    total = jnp.sum(t.reshape(t.shape[0] // 8, 8, 2 * rows), axis=0)
    part_ref[pl.ds(at, 8)] = total[:, :rows]
    part_ref[pl.ds(at + 8, 8)] = total[:, rows:]


def pressure(raw, live):
    return jnp.where(live, jnp.exp2(jnp.log2(jnp.where(live, raw, 1.0)) * (-1.0 / 3.0)), 0.0)


def put_coefficients(ref, pos, q):
    put_rows(ref, [jnp.ones_like(q)] + pos + [q] + [q * x for x in pos])


def narrow(narrow_ref, ref, e):
    narrow_ref[e] = jnp.concatenate(parts_of(tile_of(ref, e), 2), axis=0).astype(bf16)


def force_pair(narrow_ref, partners, pair, out_ref, at):
    rows = pair.shape[1] // 2
    total = None
    for n, (e0, e1) in enumerate(partners):
        left = jnp.concatenate([narrow_ref[e0], narrow_ref[e1]], axis=0)
        w = pair[n * rows:(n + 1) * rows]
        high = w.astype(bf16)
        part = dot(left, high) + dot(left, (w - high.astype(f32)).astype(bf16))
        total = part if total is None else total + part
    out_ref[pl.ds(at, 8)] = total[:8, :rows] + total[8:16, :rows]
    out_ref[pl.ds(at + 8, 8)] = total[16:24, rows:] + total[24:, rows:]


def inner_kernel(late, pairwise, table_in_ref, own_ref, live_ref, *refs):
    refs, (table_ref, table_sem) = refs[:-2], refs[-2:]
    table_copy = pltpu.make_async_copy(table_in_ref, table_ref, table_sem.at[0])
    if late:
        refs, (edge_ref, out_ref, partner_ref, mine_ref, coef_ref, narrow_ref) = refs[:-6], refs[-6:]
    else:
        refs, (partner_ref, mine_ref) = refs[:-2], refs[-2:]
    pair_ref, part_ref, turned_ref, weights_ref = refs[-4:]
    tile_dev = live_ref.shape[0]
    listed = table_ref.shape[0] - 1
    chunk = pair_ref.shape[0] // CHUNKS
    ahead = 2 * chunk + 2 * HALO_TILES

    def turn(t):
        turned_ref[t] = turned(partner_ref, t)

    def weigh(p):
        weights_ref[p] = pair_weights(mine_ref, HALO_TILES + 2 * p)

    def features():
        pos, live, mass, inverse_sq, _ = field_terms([own_field(pairwise, own_ref, live_ref, f) for f in range(FIELDS)])
        put_features(pos, live, mass, inverse_sq, partner_ref, mine_ref)

    def do_chunk(c, more=True):
        for i in range(chunk):
            t = HALO_TILES + 2 * (c * chunk + i)
            partners = [(table_ref[n, t] - HALO_TILES, table_ref[n, t + 1] - HALO_TILES) for n in range(listed)]
            p = c * chunk + i
            density_pair(turned_ref, weights_ref[p], partners, part_ref, 16 * p, pair_ref.at[p])
        if more:
            for i in range(2 * chunk):
                turn(c * 2 * chunk + ahead + i)
            for i in range(chunk):
                weigh((c + 1) * chunk + i)

    early = jnp.maximum(2 * CHUNKS - lax.axis_index("sub"), 0) // 2

    def begin():
        for t in range(ahead):
            turn(t)
        for p in range(chunk):
            weigh(p)

    if late:
        table_copy.start()
        features()
        pl.when(early == 0)(begin)
        table_copy.wait()
        pl.loop(jnp.minimum(early, CHUNKS - 1), CHUNKS - 1)(do_chunk)
        pl.when(early < CHUNKS)(lambda: do_chunk(CHUNKS - 1, False))
        edge_ref[:RIM] = turned_ref[:RIM]
        edge_ref[RIM:] = turned_ref[tile_dev - RIM:]
        pos, live, _, _, norm = field_terms([own_field(pairwise, own_ref, live_ref, f) for f in range(FIELDS)])
        inside = slice(HALO_TILES, tile_dev - HALO_TILES)
        raw = sum(part_ref[pl.ds(k, tile_dev - RIM, stride=8)] for k in range(8)) * norm[inside]
        blank = jnp.zeros((HALO_TILES, live_ref.shape[1]), f32)
        put_coefficients(coef_ref, pos, jnp.concatenate([blank, pressure(raw, live[inside]), blank], axis=0))

        @pl.loop(HALO_TILES, tile_dev - HALO_TILES, unroll=8)
        def _(t):
            narrow(narrow_ref, coef_ref, t)

        half = HALO_TILES // 2

        @pl.loop(half, pair_ref.shape[0] - half, unroll=8)
        def _(p):
            t = HALO_TILES + 2 * p
            partners = [(table_ref[n, t] - HALO_TILES, table_ref[n, t + 1] - HALO_TILES) for n in range(listed)]
            force_pair(narrow_ref, partners, pair_ref.at[p], out_ref, 8 * t)
    else:

        @pl.when(early > 0)
        def _():
            table_copy.start()
            features()
            begin()
            table_copy.wait()
            pl.loop(0, jnp.minimum(early, CHUNKS - 1))(do_chunk)
            pl.when(early == CHUNKS)(lambda: do_chunk(CHUNKS - 1, False))


def outer_kernel(
    pairwise, table_in_ref, rim_lists_in_ref, own_ref, live_ref, below_ref, above_ref, pair_ref, part_ref, edge_ref, inner_out_ref,
    density_ref, accel_ref, partner_ref, mine_ref, turned_ref, weights_ref, rim_pair_ref, rim_part_ref, coef_ref,
    coefb_ref, out_ref, table_ref, rim_lists_ref, sems,
):
    copies = [
        pltpu.make_async_copy(table_in_ref, table_ref, sems.at[0]),
        pltpu.make_async_copy(rim_lists_in_ref, rim_lists_ref, sems.at[1]),
    ]
    for copy in copies:
        copy.start()
    tile_dev, rows = live_ref.shape
    ext = tile_dev + 2 * RIM
    listed = table_ref.shape[0] - 1
    fields = [
        jnp.concatenate(
            [
                below_ref[f * RIM:(f + 1) * RIM],
                own_field(pairwise, own_ref, live_ref, f),
                above_ref[f * RIM:(f + 1) * RIM],
            ],
            axis=0,
        )
        for f in range(FIELDS)
    ]
    pos, live, mass, inverse_sq, norm = field_terms(fields)
    rim_pairs = RIM

    def rims(x):
        return jnp.concatenate([x[:2 * RIM], x[tile_dev:]], axis=0)

    put_features([rims(x) for x in pos], rims(live), rims(mass), rims(inverse_sq), partner_ref, mine_ref)
    for e in range(RIM):
        turned_ref[e] = turned(partner_ref, e)
        turned_ref[RIM + e] = edge_ref[e]
        turned_ref[2 * RIM + e] = edge_ref[RIM + e]
        turned_ref[3 * RIM + e] = turned(partner_ref, 3 * RIM + e)
    for r in range(rim_pairs):
        weights_ref[r] = pair_weights(mine_ref, HALO_TILES + 2 * r + (RIM if 2 * r >= rim_pairs else 0))

    outer = RIM + HALO_TILES
    inner_raw = sum(part_ref[pl.ds(k, tile_dev - RIM, stride=8)] for k in range(8)) * norm[outer:ext - outer]
    for copy in copies:
        copy.wait()
    for r in range(rim_pairs):
        first = 2 * r * listed
        partners = [(rim_lists_ref[first + n], rim_lists_ref[first + listed + n]) for n in range(listed)]
        density_pair(turned_ref, weights_ref[r], partners, rim_part_ref, 16 * r, rim_pair_ref.at[r])

    rim_raw = sum(rim_part_ref[pl.ds(k, 2 * RIM, stride=8)] for k in range(8))
    raw = jnp.concatenate(
        [rim_raw[:RIM] * norm[HALO_TILES:outer], inner_raw, rim_raw[RIM:] * norm[ext - outer:ext - HALO_TILES]], axis=0
    )
    q = pressure(raw, live[HALO_TILES:ext - HALO_TILES])
    pad = jnp.zeros((HALO_TILES, rows), f32)
    q = jnp.concatenate([pad, q, pad], axis=0)
    put_coefficients(coef_ref, pos, q)
    for e in range(2 * RIM):
        narrow(coefb_ref, coef_ref, HALO_TILES + e)
        narrow(coefb_ref, coef_ref, ext - HALO_TILES - 2 * RIM + e)
    half = HALO_TILES // 2
    count = pair_ref.shape[0]

    def edge_force(t, pair):
        partners = [(table_ref[n, t] + HALO_TILES, table_ref[n, t + 1] + HALO_TILES) for n in range(listed)]
        force_pair(coefb_ref, partners, pair, out_ref, 8 * t)

    for i in range(half):
        edge_force(2 * i, rim_pair_ref.at[half + i])
        edge_force(HALO_TILES + 2 * i, pair_ref.at[i])
        edge_force(tile_dev - RIM + 2 * i, pair_ref.at[count - half + i])
        edge_force(tile_dev - HALO_TILES + 2 * i, rim_pair_ref.at[2 * half + i])

    mine = slice(RIM, RIM + tile_dev)
    own_live = live_ref[...]
    density_ref[...] = raw[HALO_TILES:HALO_TILES + tile_dev] * own_live
    q_own = q[mine]
    scale = own_live * (2.0 * inverse_sq[mine] * norm[mine])
    sums = [
        jnp.concatenate(
            [
                out_ref[pl.ds(k, RIM, stride=8)],
                inner_out_ref[pl.ds(8 * RIM + k, tile_dev - 2 * RIM, stride=8)],
                out_ref[pl.ds(8 * (tile_dev - RIM) + k, RIM, stride=8)],
            ],
            axis=0,
        )
        for k in range(8)
    ]
    for c in range(3):
        x = pos[c][mine]
        accel_ref[c] = scale * (q_own * (x * sums[0] - sums[1 + c]) + (x * sums[4] - sums[5 + c]))


def inner_density(pairwise, table, own, live, carried=()):
    tile_dev, rows = live.shape
    listed = table.shape[0] - 1
    count = (tile_dev - RIM) // 2
    late = len(carried) > 0
    shapes = [
        jax.ShapeDtypeStruct((count, listed * rows, 2 * rows), f32),
        jax.ShapeDtypeStruct((16 * count, rows), f32),
        jax.ShapeDtypeStruct((tile_dev, rows, rows), bf16),
        jax.ShapeDtypeStruct((count, 2 * rows, 2 * rows), bf16),
    ]
    features = [pltpu.VMEM((8 * tile_dev, rows), f32), pltpu.VMEM((8 * tile_dev, rows), f32)]
    edges, forces = [], []
    if late:
        edges = [jax.ShapeDtypeStruct((2 * RIM, rows, rows), bf16), jax.ShapeDtypeStruct((8 * tile_dev, rows), f32)]
        forces = [pltpu.VMEM((8 * tile_dev, rows), f32), pltpu.VMEM((tile_dev, 16, rows), bf16)]
    return pl.pallas_call(
        functools.partial(inner_kernel, late, pairwise),
        out_shape=shapes + edges,
        in_specs=[ANY] + [VMEM] * (2 + len(carried)),
        out_specs=[VMEM] * len(shapes + edges),
        input_output_aliases={3 + i: i for i in range(len(carried))},
        scratch_shapes=features + forces + [pltpu.SMEM(table.shape, jnp.int32), pltpu.SemaphoreType.DMA((1,))],
        compiler_params=pltpu.CompilerParams(vmem_limit_bytes=24 << 20),
        cost_estimate=pl.CostEstimate(flops=10 ** 9, bytes_accessed=10 ** 7, transcendentals=0),
        name="inner_late" if late else "inner_early",
    )(table, own, live, *carried)


def outer_step(pairwise, table, rim_lists, own, live, below, above, pair, part, edge, inner_out):
    tile_dev, rows = live.shape
    ext = tile_dev + 2 * RIM
    listed = table.shape[0] - 1
    return pl.pallas_call(
        functools.partial(outer_kernel, pairwise),
        out_shape=(jax.ShapeDtypeStruct((tile_dev, rows), f32), jax.ShapeDtypeStruct((3, tile_dev, rows), f32)),
        in_specs=[ANY] * 2 + [VMEM] * 8,
        out_specs=(VMEM, VMEM),
        scratch_shapes=[
            pltpu.VMEM((8 * 4 * RIM, rows), f32),
            pltpu.VMEM((8 * 4 * RIM, rows), f32),
            pltpu.VMEM((4 * RIM, rows, rows), bf16),
            pltpu.VMEM((RIM, 2 * rows, 2 * rows), bf16),
            pltpu.VMEM((RIM, listed * rows, 2 * rows), f32),
            pltpu.VMEM((8 * 2 * RIM, rows), f32),
            pltpu.VMEM((8 * ext, rows), f32),
            pltpu.VMEM((ext, 16, rows), bf16),
            pltpu.VMEM((8 * tile_dev, rows), f32),
            pltpu.SMEM(table.shape, jnp.int32),
            pltpu.SMEM(rim_lists.shape, jnp.int32),
            pltpu.SemaphoreType.DMA((2,)),
        ],
        compiler_params=pltpu.CompilerParams(vmem_limit_bytes=24 << 20),
        name="outer_step",
    )(table, rim_lists, own, live, below, above, pair, part, edge, inner_out)


def per_device(coords, smooth, masses, owners, counts, neighbours):
    tile_dev, rows = smooth.shape
    regions = lax.axis_size("region")
    subs = lax.axis_size("sub")
    per_dest = tile_dev // regions
    listed = neighbours.shape[1]
    pairwise = regions <= 4 and regions & (regions - 1) == 0
    grouped = group_tiles(coords, smooth, masses, owners, regions, pairwise)
    me = lax.axis_index("region") if pairwise else jnp.int32(0)
    table = jnp.concatenate([neighbours.T, counts[None]], axis=0)
    if pairwise:
        live, ids = stage(table, rows)
        blocks = [grouped[0]]
        for k in range(1, regions):
            blocks.append(lax.ppermute(grouped[k], "region", [(i, i ^ k) for i in range(regions)]))
        own = jnp.stack(blocks)
    else:
        live, ids = stage(table, rows)
        own = lax.all_to_all(grouped[0], "region", 0, 0, tiled=True)
    by_field = own.reshape(regions, FIELDS, per_dest, rows)

    def rim(first):
        if pairwise:
            block = lax.dynamic_index_in_dim(by_field, me ^ (0 if first else regions - 1), 0, keepdims=False)
            block = block[:, :RIM] if first else block[:, per_dest - RIM:]
        else:
            blocks = RIM // per_dest
            block = by_field[:blocks] if first else by_field[regions - blocks:]
            block = jnp.swapaxes(block, 0, 1).reshape(FIELDS, RIM, rows)
        tiles = slice(0, RIM) if first else slice(tile_dev - RIM, tile_dev)
        block = jnp.concatenate([block[:4], (block[4] * live[tiles])[None]], axis=0).reshape(FIELDS * RIM, rows)
        return jnp.concatenate([block, ids[0 if first else 1]], axis=0)

    up = [(i, (i + 1) % subs) for i in range(subs)]
    down = [(j, i) for i, j in up]
    below = lax.ppermute(rim(False), "sub", up)
    carried = inner_density(pairwise, table, own, live)
    above = lax.ppermute(rim(True), "sub", down)
    pair, part, _, _, edge, inner_out = inner_density(pairwise, table, own, live, carried)
    count = HALO_TILES * listed
    places = [
        below[FIELDS * RIM, :count] + (HALO_TILES - tile_dev),
        ids[0, 0, :count] + HALO_TILES,
        ids[1, 0, :count] + (HALO_TILES - tile_dev + 2 * RIM),
        above[FIELDS * RIM, :count] + (HALO_TILES + 2 * RIM),
    ]
    rim_lists = jnp.concatenate(places).astype(jnp.int32)
    return outer_step(pairwise, table, rim_lists, own, live, below, above, pair, part, edge, inner_out)


def solution(mesh):
    in_specs = (
        P(None, ("region", "sub"), None),
        P(("region", "sub"), None),
        P(("region", "sub"), None),
        P(("region", "sub")),
        P(("region", "sub")),
        P(("region", "sub"), None),
    )
    out_specs = (P(("region", "sub"), None), P(None, ("region", "sub"), None))
    return jax.shard_map(
        per_device, mesh=mesh, in_specs=in_specs, out_specs=out_specs, check_vma=False
    )
```
